32 devices in a mesh: groups: 2 (over x), dp: 2 (over core), tensor: 8 (over z, y).
Axes of the slice: x: 2, y: 2, z: 4, core: 2. Of those that a mesh axis runs over, the one named last changes fastest.
Arguments:
- reward_hidden: bfloat16 [32, 256, 8192], P(('groups', 'dp'), None, 'tensor'), parts along dimension 0, may hold values from -6 to 6
- reward_gain: float32 [8192], P('tensor'), may hold values from 0.5 to 1.5
- reward_head: float32 [8192], P('tensor'), may hold values from -1 to 1
- decode_inputs: bfloat16 [2, 32, 8192], P(None, ('groups', 'dp'), 'tensor'), parts along dimension 1, may hold values from -6 to 6
- attn_gain: float32 [8192], replicated, may hold values from 0.5 to 1.5
- w_query: bfloat16 [8192, 8192], P(None, 'tensor'), may hold values from -0.0625 to 0.0625
- w_keyval: bfloat16 [8192, 2048], P(None, 'tensor'), may hold values from -0.0625 to 0.0625
- w_out: bfloat16 [8192, 8192], P('tensor'), may hold values from -3 to 3
- cache_keys: bfloat16 [32, 2048, 1024], P(('groups', 'dp'), 'tensor'), parts along dimension 0, may hold values from -720 to 720
- cache_values: bfloat16 [32, 2048, 1024], P(('groups', 'dp'), 'tensor'), parts along dimension 0, may hold values from -6 to 6
- lengths: int32 [32], P('groups'), parts along dimension 0, may hold values from 512 to 2048
- slot_map: int32 [32], P('groups'), parts along dimension 0, may hold values from 0 to 15, as said below
Outputs:
- reward: float32 [32], P(('groups', 'dp')), parts along dimension 0
- decoded: bfloat16 [2, 32, 8192], P(None, ('groups', 'dp'), 'tensor'), parts along dimension 1
The draws below stay inside these ranges and needn't reach their ends.
There are 2 independent parts, one for each index of `groups`. The reference program is written for one: setup_inputs(seed, part) draws one part's arguments, and reference() takes and returns one part's arrays. A program takes and returns all parts, laid end to end along the dimension named above; an argument that names none is the same for every part. Nothing has to cross between parts.
Inputs may be any that keep to these rules, and one draw needn't show every extreme that they name: `slot_map`: each aligned block of 8 slots holds exactly 4 survivors, which map to themselves; every other slot maps to a survivor, and every survivor is named by exactly one other slot.
All inputs are finite; a program needn't handle non-finite values.
Results may differ from the reference program's by a relative error of at most 0.0055.
The reference program's roundings to bfloat16 on the way (of `normed`, `query`, `keyval`, `weights` and `attended`) count: a program that leaves them out, or rounds other values in their place, can miss the bound.
Values may be sent and summed in bfloat16 or wider, within the bound.
No kernel may reach another device: no remote copies, remote signals or barrier semaphores. Data moves between devices by JAX's collectives and lax.ppermute only.
A program may use at most 128 MiB of HBM per device.

```python
import jax
import jax.numpy as jnp
from jax import lax

D = 8192
QH = 64
KVH = 8
HD = 128
SPAN = 256
CACHE_LEN = 2048
RESP_DEV = 8
STEPS = 2
RESP = 16
BLOCK_POS = 256
N_TENSOR = 8


def draw_lengths(key, part):
    drawn = jax.random.randint(jax.random.fold_in(key, 11), (RESP,), CACHE_LEN // 4, CACHE_LEN + 1)
    return drawn.at[0].set(CACHE_LEN).astype(jnp.int32)


def draw_slot_map(key, part):
    blocks = RESP // RESP_DEV
    half = RESP_DEV // 2
    block_keys = jax.random.split(jax.random.fold_in(key, 23), blocks)
    orders = jax.vmap(lambda k: jax.random.permutation(k, RESP_DEV))(block_keys)
    offsets = (jnp.arange(blocks) * RESP_DEV)[:, None]
    kept = (orders[:, :half] + offsets).reshape(-1)
    freed = (orders[:, half:] + offsets).reshape(-1)
    match = jax.random.permutation(jax.random.fold_in(key, 37), RESP // 2)
    result = jnp.arange(RESP).at[freed].set(kept[match])
    return result.astype(jnp.int32)


def draw_cache_keys(key, part):
    base = jax.random.normal(jax.random.fold_in(key, 41), (RESP, CACHE_LEN, KVH, HD), jnp.float32)
    base = jnp.clip(base, -6.0, 6.0)
    return base.reshape(RESP, CACHE_LEN, KVH * HD).astype(jnp.bfloat16)


def block_levels(rng, shape, cuts, low, high):
    def one(dim, blocks):
        steps = jax.random.uniform(jax.random.fold_in(jax.random.fold_in(rng, 6), dim), (blocks,), jnp.float32, low / len(cuts), high / len(cuts))
        return jnp.repeat(jnp.exp(steps), shape[dim] // blocks).reshape((-1,) + (1,) * (len(shape) - dim - 1))

    factor_of = one(*cuts[0])
    for cut in cuts[1:]:
        factor_of = factor_of * one(*cut)
    return factor_of


def centred(stream_key, dims, spread, limit, pieces=(), kind=jnp.bfloat16):
    values = spread * jax.random.normal(stream_key, dims, jnp.float32)
    if pieces:
        values = values * block_levels(stream_key, dims, pieces, -0.22, 0.18)
    return jnp.clip(values, -limit, limit).astype(kind)


def setup_inputs(seed: int = 0, part: int = 0) -> dict:
    key_of = jax.random.split(jax.random.key(seed), 13)
    own_keys = jax.random.split(jax.random.fold_in(key_of[12], part), 13)
    reward_hidden = centred(own_keys[0], (RESP, SPAN, D), 1.0, 6.0, ((0, 2), (2, 8)))
    reward_gain = jnp.clip(1.0 + 0.1 * jax.random.normal(key_of[1], (D,), jnp.float32), 0.5, 1.5)
    reward_head = centred(key_of[2], (D,), (D // SPAN) ** -0.5, 1.0, ((0, 8),), jnp.float32)
    decode_inputs = centred(own_keys[3], (STEPS, RESP, D), 1.0, 6.0, ((1, 2), (2, 8)))
    attn_gain = jnp.clip(1.0 + 0.1 * jax.random.normal(key_of[4], (D,), jnp.float32), 0.5, 1.5)
    w_query = centred(key_of[5], (D, QH * HD), D ** -0.5, 0.0625, ((1, 8),))
    w_keyval = centred(key_of[6], (D, 2 * KVH * HD), D ** -0.5, 0.0625, ((1, 8),))
    w_out = centred(key_of[7], (QH * HD, D), (QH * HD // CACHE_LEN) ** -0.5, 3.0, ((0, 8),))
    cache_keys = draw_cache_keys(jax.random.fold_in(jax.random.fold_in(key_of[12], part), 71), part)
    cache_values = centred(own_keys[9], (RESP, CACHE_LEN, KVH * HD), 1.0, 6.0, ((0, 2), (1, 8)))
    lengths = draw_lengths(jax.random.fold_in(jax.random.fold_in(key_of[12], part), 71), part)
    slot_map = draw_slot_map(jax.random.fold_in(jax.random.fold_in(key_of[12], part), 71), part)
    return dict(reward_hidden=reward_hidden, reward_gain=reward_gain, reward_head=reward_head, decode_inputs=decode_inputs, attn_gain=attn_gain, w_query=w_query, w_keyval=w_keyval, w_out=w_out, cache_keys=cache_keys, cache_values=cache_values, lengths=lengths, slot_map=slot_map)


EPS = 1e-05
NEG = -1e+30

def reference(reward_hidden, reward_gain, reward_head, decode_inputs, attn_gain, w_query, w_keyval, w_out, cache_keys, cache_values, lengths, slot_map):
    hidden = reward_hidden.astype(jnp.float32)
    squares = lax.optimization_barrier(jnp.sum(hidden * hidden, axis=-1))
    head_dot = lax.optimization_barrier(jnp.sum(hidden * (reward_gain * reward_head), axis=-1))
    reward = lax.optimization_barrier(jnp.mean(head_dot * lax.rsqrt(squares / D + EPS), axis=-1))
    keys_now = jnp.take(cache_keys, slot_map, axis=0)
    values_now = jnp.take(cache_values, slot_map, axis=0)
    live = jnp.take(lengths, slot_map, axis=0)
    slots = keys_now.shape[0]
    group = QH // KVH
    keys5 = keys_now.reshape(slots, N_TENSOR, BLOCK_POS, KVH, HD).astype(jnp.float32)
    values5 = values_now.reshape(slots, N_TENSOR, BLOCK_POS, KVH, HD).astype(jnp.float32)
    places = jnp.arange(CACHE_LEN).reshape(N_TENSOR, BLOCK_POS)
    valid = (places[None, :, :] < live[:, None, None])[:, None, None, :, :]
    scale = HD ** (-0.5)
    new_keys = []
    new_values = []
    outputs = []
    for step in range(STEPS):
        xf = decode_inputs[step].astype(jnp.float32)
        normed = (xf * lax.rsqrt(lax.optimization_barrier(jnp.mean(xf * xf, axis=-1, keepdims=True)) + EPS) * attn_gain).astype(jnp.bfloat16)
        query = jnp.dot(normed, w_query, preferred_element_type=jnp.float32).astype(jnp.bfloat16)
        query = query.reshape(slots, KVH, group, HD).astype(jnp.float32)
        keyval = jnp.dot(normed, w_keyval, preferred_element_type=jnp.float32).astype(jnp.bfloat16).reshape(slots, 2, KVH, HD)
        new_keys.append(keyval[:, 0].astype(jnp.float32))
        new_values.append(keyval[:, 1].astype(jnp.float32))
        fresh_k = jnp.stack(new_keys, axis=1)
        fresh_v = jnp.stack(new_values, axis=1)
        scores = jnp.einsum('rkgd,rbwkd->rkgbw', query, keys5) * scale
        scores = jnp.where(valid, scores, NEG)
        block_max = lax.optimization_barrier(jnp.max(scores, axis=-1))
        expo = jnp.where(valid, jnp.exp(scores - block_max[..., None]), 0.0)
        block_total = lax.optimization_barrier(jnp.sum(expo, axis=-1))
        weights = expo.astype(jnp.bfloat16).astype(jnp.float32)
        block_acc = jnp.einsum('rkgbw,rbwkd->rkgbd', weights, values5)
        recent = jnp.einsum('rkgd,rjkd->rkgj', query, fresh_k) * scale
        recent_max = lax.optimization_barrier(jnp.max(recent, axis=-1))
        recent_exp = jnp.exp(recent - recent_max[..., None])
        recent_total = lax.optimization_barrier(jnp.sum(recent_exp, axis=-1))
        recent_w = recent_exp.astype(jnp.bfloat16).astype(jnp.float32)
        recent_acc = jnp.einsum('rkgj,rjkd->rkgd', recent_w, fresh_v)
        top = jnp.maximum(lax.optimization_barrier(jnp.max(block_max, axis=-1)), recent_max)
        block_scale = jnp.exp(block_max - top[..., None])
        recent_scale = jnp.exp(recent_max - top)
        total = lax.optimization_barrier(jnp.sum(block_scale * block_total, axis=-1)) + recent_scale * recent_total
        acc = lax.optimization_barrier(jnp.sum(block_scale[..., None] * block_acc, axis=3)) + recent_scale[..., None] * recent_acc
        attended = (acc / total[..., None]).astype(jnp.bfloat16).reshape(slots, QH * HD)
        outputs.append(jnp.dot(attended, w_out, preferred_element_type=jnp.float32).astype(jnp.bfloat16))
    return (reward, jnp.stack(outputs, axis=0))
```

```python
import functools

import jax
import jax.numpy as jnp
from jax import lax
from jax.experimental import pallas as pl
from jax.experimental.pallas import tpu as pltpu
from jax.sharding import PartitionSpec as P

HD = 128
KVH = 8
STEPS = 2
PAIR = 2
LANES = 128
EXT = 8
EPS = 1e-05
NEG = -1e30
SCALE = HD ** (-0.5)
NT = (((1,), (1,)), ((), ()))
TN = (((0,), (0,)), ((), ()))


def iota(shape, dim):
    return lax.broadcasted_iota(jnp.int32, shape, dim)


def dot(a, b, dims=(((1,), (0,)), ((), ()))):
    return lax.dot_general(a, b, dims, preferred_element_type=jnp.float32)


def head_major(shape, pages, per_page, heads):
    o, s = iota(shape, 0), iota(shape, 1)
    row = o % per_page
    head = (o // per_page) % heads
    page = o // (per_page * heads)
    return (s == (head * pages + page) * per_page + row).astype(jnp.bfloat16)


def project_kernel(pages, per_page, width, x_ref, gain_ref, wq_ref, wkv_ref, out_ref, inv, accq, acckv):
    n = pl.program_id(0)
    chunks, rows, depth = x_ref.shape

    @pl.when(n == 0)
    def _():
        total = jnp.zeros((rows, depth), jnp.float32)
        for chunk in range(chunks):
            part = x_ref[chunk].astype(jnp.float32)
            total = total + part * part
        mean = jnp.sum(total, axis=-1, keepdims=True) / width
        inv[...] = jnp.broadcast_to(lax.rsqrt(mean + EPS), inv.shape)
        accq[...] = jnp.zeros_like(accq)
        acckv[...] = jnp.zeros_like(acckv)

    normed = (x_ref[n].astype(jnp.float32) * inv[:, :1] * gain_ref[0]).astype(jnp.bfloat16)
    accq[...] += dot(normed, wq_ref[...])
    acckv[...] += dot(normed, wkv_ref[...])

    @pl.when(n == chunks - 1)
    def _():
        heads = accq.shape[1] // HD
        query = accq[...].astype(jnp.bfloat16)
        stacked = jnp.concatenate([query[:, h * HD : (h + 1) * HD] for h in range(heads)], axis=0)
        order = head_major((rows * heads, rows * heads), pages, per_page, heads)
        query = dot(order, stacked).astype(jnp.bfloat16)
        pieces = [query]
        columns = acckv.shape[1]
        keyval = acckv[...].astype(jnp.bfloat16)
        if columns < LANES:
            keyval = jnp.concatenate(
                [keyval, jnp.zeros((rows, LANES - columns), jnp.bfloat16)], axis=1
            )
        for v in range(keyval.shape[1] // LANES):
            pieces.append(keyval[:, v * LANES : (v + 1) * LANES])
        packed = jnp.concatenate(pieces, axis=0)
        for device in range(out_ref.shape[0]):
            out_ref[device] = packed


def attend_kernel(page_rows, meta_ref, q_ref, k_ref, v_ref, reward_ref, out_ref, spread):
    i = pl.program_id(0)
    pages = pl.num_programs(0)
    width = k_ref.shape[1]
    span = KVH * page_rows
    body = out_ref.shape[1] - 2 * EXT

    @pl.when(i == 0)
    def _():
        spread[...] = jnp.zeros_like(spread)
        if reward_ref.shape[0] == KVH:
            out_ref[:, body + EXT :, :] = reward_ref[...]
        else:
            out_ref[:, body + EXT :, :] = jnp.zeros((KVH, EXT, LANES), jnp.float32)

    start = pl.multiple_of(i * page_rows, page_rows)
    for k in range(KVH):
        spread[k * page_rows : (k + 1) * page_rows, k * HD : (k + 1) * HD] = q_ref[
            k, pl.ds(start, page_rows), :
        ]
    scores = dot(k_ref[0], spread[...], NT) * SCALE
    valid = meta_ref[2 * pages] + iota((width, span), 0) < meta_ref[pages + i]
    scores = jnp.where(valid, scores, NEG)
    top = jnp.max(scores, axis=0, keepdims=True)
    expo = jnp.where(valid, jnp.exp(scores - top), 0.0)
    total = jnp.sum(expo, axis=0, keepdims=True)
    acc = dot(expo.astype(jnp.bfloat16), v_ref[0], TN)
    for k in range(KVH):
        out_ref[k, pl.ds(start, page_rows), :] = acc[
            k * page_rows : (k + 1) * page_rows, k * HD : (k + 1) * HD
        ]
        lane = (k * page_rows) // LANES * LANES
        out_ref[k, pl.ds(body + i, 1), :] = top[:, lane : lane + LANES]
        out_ref[k, pl.ds(body + pages + i, 1), :] = total[:, lane : lane + LANES]


def merge_kernel(pages, per_page, width, span, meta_ref, part_ref, q_ref, fk_ref, fv_ref, w_ref, out_ref, att, mean):
    n = pl.program_id(0)
    chunks = part_ref.shape[0]
    body = part_ref.shape[1] - 2 * EXT
    page_rows = body // pages
    heads = page_rows // per_page
    rows = pages * per_page

    @pl.when(n == 0)
    def _():
        query = q_ref[0, :body, :]
        recent = dot(query, fk_ref[...], NT) * SCALE
        line, col = iota(recent.shape, 0), iota(recent.shape, 1)
        mine = (line // page_rows) * per_page + line % per_page
        seen = (mine // STEPS == col // STEPS) & (col <= mine)
        recent = jnp.where(seen, recent, NEG)
        recent_max = jnp.max(recent, axis=-1, keepdims=True)
        recent_exp = jnp.where(seen, jnp.exp(recent - recent_max), 0.0)
        recent_total = jnp.sum(recent_exp, axis=-1, keepdims=True)
        recent_acc = dot(recent_exp.astype(jnp.bfloat16), fv_ref[...])

        maxima = [part_ref[b, body : body + pages, :] for b in range(chunks)]
        totals = [part_ref[b, body + pages : body + 2 * pages, :] for b in range(chunks)]
        top = functools.reduce(jnp.maximum, maxima)
        factors = [jnp.exp(m - top) for m in maxima]
        total = functools.reduce(jnp.add, [f * t for f, t in zip(factors, totals)])

        line, lane = iota((page_rows, LANES), 0), iota((page_rows, LANES), 1)
        pick = lane == line + meta_ref[0]

        def column(packed):
            return jnp.concatenate(
                [
                    jnp.sum(
                        jnp.where(pick, jnp.broadcast_to(packed[i : i + 1], pick.shape), 0.0),
                        axis=-1,
                        keepdims=True,
                    )
                    for i in range(pages)
                ],
                axis=0,
            )

        acc = jnp.zeros((body, HD), jnp.float32)
        for b in range(chunks):
            acc = acc + column(factors[b]) * part_ref[b, :body, :]
        cache_top, cache_total = column(top), column(total)
        top = jnp.maximum(cache_top, recent_max)
        cache_factor = jnp.exp(cache_top - top)
        recent_factor = jnp.exp(recent_max - top)
        total = cache_factor * cache_total + recent_factor * recent_total
        acc = cache_factor * acc + recent_factor * recent_acc
        attended = (acc / total).astype(jnp.bfloat16)
        order = head_major((body, body), pages, per_page, heads)
        attended = dot(order, attended, TN).astype(jnp.bfloat16)
        for h in range(heads):
            att[:, h * HD : (h + 1) * HD] = attended[h * rows : (h + 1) * rows]

        tile = functools.reduce(jnp.add, [part_ref[b, body + EXT :, :] for b in range(chunks)])
        used = EXT // 2
        value = tile[used:] * lax.rsqrt(tile[:used] / width + EPS)
        mean[...] = jnp.broadcast_to(jnp.sum(value, keepdims=True) / span, mean.shape)

    product = dot(att[...], w_ref[...])
    for c in range(w_ref.shape[1] // LANES):
        out_ref[0, c * rows : (c + 1) * rows, :] = product[:, c * LANES : (c + 1) * LANES]
    out_ref[0, out_ref.shape[1] - EXT :, :] = jnp.where(
        iota((EXT, LANES), 0) == meta_ref[1], mean[...], 0.0
    )


def sum_kernel(rows, part_ref, out_ref, reward_ref):
    total = part_ref[0]
    for b in range(1, part_ref.shape[0]):
        total = total + part_ref[b]
    for c in range(out_ref.shape[1] // LANES):
        out_ref[:, c * LANES : (c + 1) * LANES] = total[c * rows : (c + 1) * rows].astype(
            jnp.bfloat16
        )
    reward_ref[...] = total[total.shape[0] - EXT :]


def whole(shape):
    return pl.BlockSpec(shape, lambda *_: (0,) * len(shape))


def exchange(x):
    return lax.all_to_all(x, "tensor", 0, 0, tiled=True)


def local(
    chunks,
    reward_hidden,
    reward_gain,
    reward_head,
    decode_inputs,
    attn_gain,
    w_query,
    w_keyval,
    w_out,
    cache_keys,
    cache_values,
    lengths,
    slot_map,
):
    slots, width = cache_keys.shape[:2]
    depth, qcols = w_query.shape
    kvcols = w_keyval.shape[1]
    part = decode_inputs.shape[-1]
    heads = qcols // HD
    group = heads * chunks // KVH
    split = group // heads
    pages = slots // PAIR
    per_page = PAIR * STEPS
    page_rows = per_page * group
    rows = slots * STEPS
    body = rows * heads
    mine, index = lax.axis_index("dp"), lax.axis_index("tensor")
    swap = [(0, 1), (1, 0)]

    ids = jnp.arange(slot_map.shape[0])
    kept = slot_map == ids
    home = slot_map // slots
    before = kept[None, :] & (ids[None, :] // slots == home[:, None]) & (ids[None, :] < slot_map[:, None])
    place = home * slots + PAIR * jnp.sum(before, axis=1) + (slot_map != ids)
    place_own = lax.dynamic_slice_in_dim(place, mine * slots, slots)
    place_far = lax.dynamic_slice_in_dim(place, (1 - mine) * slots, slots)
    lead = place[None, :] == (mine * slots + PAIR * jnp.arange(pages))[:, None]
    page = jnp.sum(jnp.where(lead, ids[None, :], 0), axis=1) - mine * slots
    live = jnp.sum(jnp.where(lead, lengths[None, :], 0), axis=1)
    work = jnp.arange(rows)
    steps = jnp.arange(STEPS)
    both = jnp.stack([place_own, place_far]) - mine * slots
    take = (both[None, None, :, None, :] == jnp.arange(slots)[:, None, None, None, None]) & (
        steps[None, :, None, None, None] == steps[None, None, None, :, None]
    )
    take = take.reshape(rows, 2 * rows).astype(jnp.bfloat16)
    bases = jnp.stack([mine, 1 - mine]) * slots
    give = (
        (place_own[None, :, None] - bases[None, None, :])[..., None, None]
        == jnp.arange(slots)[None, None, None, :, None]
    ) & (steps[:, None, None, None, None] == steps[None, None, None, None, :])
    give = give.reshape(rows, 2 * rows).astype(jnp.bfloat16)

    own = decode_inputs.reshape(rows, part)
    far = lax.ppermute(own, "dp", swap)
    tokens = dot(take, jnp.concatenate([own, far], axis=0)).astype(jnp.bfloat16)
    tokens = exchange(jnp.broadcast_to(tokens[None], (chunks, rows, part)))

    hidden = reward_hidden.astype(jnp.float32)
    squares = jnp.sum(hidden * hidden, axis=-1)
    head_dot = jnp.sum(hidden * (reward_gain * reward_head), axis=-1)
    span = squares.shape[1]

    def tile(values):
        values = values.reshape(chunks, -1)
        size = EXT // 2 * LANES
        return jnp.pad(values, ((0, 0), (0, size - values.shape[1]))).reshape(
            chunks, EXT // 2, LANES
        )

    reward_parts = jnp.concatenate([tile(squares), tile(head_dot)], axis=1)

    kv_rows = max(kvcols // LANES, 1) * rows
    packed = pl.pallas_call(
        functools.partial(project_kernel, pages, per_page, depth),
        grid=(chunks,),
        in_specs=[
            whole((chunks, rows, part)),
            pl.BlockSpec((1, 1, part), lambda n: (n, 0, 0)),
            pl.BlockSpec((part, qcols), lambda n: (n, 0)),
            pl.BlockSpec((part, kvcols), lambda n: (n, 0)),
        ],
        out_specs=whole((chunks, body + kv_rows, LANES)),
        out_shape=jax.ShapeDtypeStruct((chunks, body + kv_rows, LANES), jnp.bfloat16),
        scratch_shapes=[
            pltpu.VMEM((rows, LANES), jnp.float32),
            pltpu.VMEM((rows, qcols), jnp.float32),
            pltpu.VMEM((rows, kvcols), jnp.float32),
        ],
        name="project",
    )(tokens, attn_gain.reshape(chunks, 1, part), w_query, w_keyval)
    gathered = exchange(packed)

    fresh = gathered[:, body:]
    if kvcols < LANES:
        fresh = fresh[..., :kvcols].transpose(1, 0, 2).reshape(rows, 2 * KVH, HD).transpose(1, 0, 2)
    else:
        fresh = fresh.reshape(2 * KVH, rows, HD)
    kv_head = index * heads // group
    fresh_k = lax.dynamic_index_in_dim(fresh, kv_head, 0, keepdims=False)
    fresh_v = lax.dynamic_index_in_dim(fresh, KVH + kv_head, 0, keepdims=False)
    queries = gathered
    if split > 1:
        queries = (
            gathered[:, :body]
            .reshape(KVH, split, pages, heads * per_page, HD)
            .transpose(0, 2, 1, 3, 4)
            .reshape(KVH, pages * page_rows, HD)
        )

    meta = jnp.concatenate([page, live, (index * width)[None]]).astype(jnp.int32)
    big = pages * page_rows
    pieces = pl.pallas_call(
        functools.partial(attend_kernel, page_rows),
        grid_spec=pltpu.PrefetchScalarGridSpec(
            num_scalar_prefetch=1,
            grid=(pages,),
            in_specs=[
                pl.BlockSpec(queries.shape, lambda i, m: (0, 0, 0)),
                pl.BlockSpec((1, width, KVH * HD), lambda i, m: (m[i], 0, 0)),
                pl.BlockSpec((1, width, KVH * HD), lambda i, m: (m[i], 0, 0)),
                pl.BlockSpec(reward_parts.shape, lambda i, m: (0, 0, 0)),
            ],
            out_specs=pl.BlockSpec((KVH, big + 2 * EXT, HD), lambda i, m: (0, 0, 0)),
            scratch_shapes=[pltpu.VMEM((KVH * page_rows, KVH * HD), jnp.bfloat16)],
        ),
        out_shape=jax.ShapeDtypeStruct((KVH, big + 2 * EXT, HD), jnp.float32),
        name="attend",
    )(meta, queries, cache_keys, cache_values, reward_parts)
    if split > 1:
        acc = (
            pieces[:, :big]
            .reshape(KVH, pages, split, heads * per_page, HD)
            .transpose(0, 2, 1, 3, 4)
            .reshape(chunks, body, HD)
        )
        extra = jnp.repeat(pieces[:, big : big + EXT], split, axis=0)
        pieces = jnp.concatenate([acc, extra, reward_parts], axis=1)
    pieces = exchange(pieces)

    chunk_rows = part // LANES * rows + EXT
    own_row = index * (slots * span // chunks) // span
    meta = jnp.stack([(index * heads * per_page) % LANES, own_row]).astype(jnp.int32)
    partial = pl.pallas_call(
        functools.partial(merge_kernel, pages, per_page, depth, span),
        grid_spec=pltpu.PrefetchScalarGridSpec(
            num_scalar_prefetch=1,
            grid=(chunks,),
            in_specs=[
                pl.BlockSpec(pieces.shape, lambda n, m: (0, 0, 0)),
                pl.BlockSpec((1,) + packed.shape[1:], lambda n, m: (0, 0, 0)),
                pl.BlockSpec((rows, HD), lambda n, m: (0, 0)),
                pl.BlockSpec((rows, HD), lambda n, m: (0, 0)),
                pl.BlockSpec((qcols, part), lambda n, m: (0, n)),
            ],
            out_specs=pl.BlockSpec((1, chunk_rows, LANES), lambda n, m: (n, 0, 0)),
            scratch_shapes=[
                pltpu.VMEM((rows, qcols), jnp.bfloat16),
                pltpu.VMEM((EXT, LANES), jnp.float32),
            ],
        ),
        out_shape=jax.ShapeDtypeStruct((chunks, chunk_rows, LANES), jnp.float32),
        name="merge",
    )(meta, pieces, packed, fresh_k, fresh_v, w_out)
    partial = exchange(partial)

    decoded, reward = pl.pallas_call(
        functools.partial(sum_kernel, rows),
        out_shape=(
            jax.ShapeDtypeStruct((rows, part), jnp.bfloat16),
            jax.ShapeDtypeStruct((EXT, LANES), jnp.float32),
        ),
        name="total",
    )(partial)
    far = lax.ppermute(decoded, "dp", swap)
    decoded = dot(give, jnp.concatenate([decoded, far], axis=0)).astype(jnp.bfloat16)
    return (reward[:slots, 0], decoded.reshape(STEPS, slots, part))


def solution(mesh):
    return jax.shard_map(
        functools.partial(local, mesh.shape["tensor"]),
        mesh=mesh,
        in_specs=(
            P(("groups", "dp"), None, "tensor"),
            P("tensor"),
            P("tensor"),
            P(None, ("groups", "dp"), "tensor"),
            P(),
            P(None, "tensor"),
            P(None, "tensor"),
            P("tensor", None),
            P(("groups", "dp"), "tensor", None),
            P(("groups", "dp"), "tensor", None),
            P("groups"),
            P("groups"),
        ),
        out_specs=(P(("groups", "dp")), P(None, ("groups", "dp"), "tensor")),
        check_vma=False,
    )
```

```python
import functools

import jax
import jax.numpy as jnp
from jax import lax
from jax.experimental import pallas as pl
from jax.experimental.pallas import tpu as pltpu
from jax.sharding import PartitionSpec as P

HD = 128
KVH = 8
STEPS = 2
PAIR = 2
LANES = 128
EXT = 8
EPS = 1e-05
NEG = -1e30
SCALE = HD ** (-0.5)
NT = (((1,), (1,)), ((), ()))
TN = (((0,), (0,)), ((), ()))
MIB = 1 << 20
ANY = pl.BlockSpec(memory_space=pl.ANY)
VMEM = pl.BlockSpec(memory_space=pltpu.VMEM)
SMEM = pl.BlockSpec(memory_space=pltpu.SMEM)


def iota(shape, dim):
    return lax.broadcasted_iota(jnp.int32, shape, dim)


def dot(a, b, dims=(((1,), (0,)), ((), ()))):
    return lax.dot_general(a, b, dims, preferred_element_type=jnp.float32)


def head_major(shape, pages, per_page, heads):
    o, s = iota(shape, 0), iota(shape, 1)
    row = o % per_page
    head = (o // per_page) % heads
    page = o // (per_page * heads)
    return (s == (head * pages + page) * per_page + row).astype(jnp.bfloat16)


def aligned(index, size):
    return pl.ds(pl.multiple_of(index * size, size), size)


def project_kernel(pages, per_page, width, meta_ref, own_ref, far_ref, take_ref, gain_ref, wq_ref, wkv_ref, out_ref, tokens, wq, wkv, sems):
    me = meta_ref[0]
    chunks, rows, depth = own_ref.shape
    copies = []
    for r in range(chunks):
        source = aligned(me ^ r, depth)
        pair = (
            pltpu.make_async_copy(wq_ref.at[source], wq.at[r], sems.at[0, r]),
            pltpu.make_async_copy(wkv_ref.at[source], wkv.at[r], sems.at[1, r]),
        )
        for copy in pair:
            copy.start()
        copies.append(pair)

    total = jnp.zeros((rows, depth), jnp.float32)
    for r in range(chunks):
        both = jnp.concatenate([own_ref[r], far_ref[r]], axis=0)
        part = dot(take_ref[...], both)
        tokens[r] = part.astype(jnp.bfloat16)
        total = total + part * part
    inv = lax.rsqrt(jnp.sum(total, axis=-1, keepdims=True) / width + EPS)

    query = jnp.zeros((rows, wq.shape[2]), jnp.float32)
    keyval = jnp.zeros((rows, wkv.shape[2]), jnp.float32)
    for r in range(chunks):
        normed = (tokens[r].astype(jnp.float32) * inv * gain_ref[me ^ r]).astype(jnp.bfloat16)
        for copy in copies[r]:
            copy.wait()
        query = query + dot(normed, wq[r])
        keyval = keyval + dot(normed, wkv[r])

    heads = query.shape[1] // HD
    query = query.astype(jnp.bfloat16)
    stacked = jnp.concatenate([query[:, h * HD : (h + 1) * HD] for h in range(heads)], axis=0)
    order = head_major((rows * heads, rows * heads), pages, per_page, heads)
    body = rows * heads
    out_ref[:body] = dot(order, stacked).astype(jnp.bfloat16)
    keyval = keyval.astype(jnp.bfloat16)
    columns = keyval.shape[1]
    if columns < LANES:
        pad = jnp.zeros((rows, LANES - columns), jnp.bfloat16)
        keyval = jnp.concatenate([keyval, pad], axis=1)
    for v in range(keyval.shape[1] // LANES):
        out_ref[body + v * rows : body + (v + 1) * rows] = keyval[:, v * LANES : (v + 1) * LANES]


def attend_kernel(pages, page_rows, meta_ref, q_ref, k_ref, v_ref, reward_ref, *rest):
    outs, (spread, product, keys, values, sems) = rest[:-5], rest[-5:]
    width = k_ref.shape[1]
    span = KVH * page_rows
    body = pages * page_rows
    copies = []
    for i in range(pages):
        pair = (
            pltpu.make_async_copy(k_ref.at[meta_ref[i]], keys.at[i], sems.at[0, i]),
            pltpu.make_async_copy(v_ref.at[meta_ref[i]], values.at[i], sems.at[1, i]),
        )
        for copy in pair:
            copy.start()
        copies.append(pair)

    me = meta_ref[2 * pages + 1]
    spread[...] = jnp.zeros_like(spread)
    for i in range(pages):
        for r in range(KVH):
            spread[r * page_rows : (r + 1) * page_rows, aligned(me ^ r, HD)] = q_ref[
                r, i * page_rows : (i + 1) * page_rows, :
            ]
        copies[i][0].wait()
        scores = dot(keys[i], spread[...], NT) * SCALE
        valid = meta_ref[2 * pages] + iota((width, span), 0) < meta_ref[pages + i]
        scores = jnp.where(valid, scores, NEG)
        top = jnp.max(scores, axis=0, keepdims=True)
        expo = jnp.where(valid, jnp.exp(scores - top), 0.0)
        total = jnp.sum(expo, axis=0, keepdims=True)
        copies[i][1].wait()
        product[...] = dot(expo.astype(jnp.bfloat16), values[i], TN)
        for r in range(KVH):
            out = outs[r] if len(outs) > 1 else outs[0].at[r]
            out[i * page_rows : (i + 1) * page_rows, :] = product[
                r * page_rows : (r + 1) * page_rows, aligned(me ^ r, HD)
            ]
            lane = (r * page_rows) // LANES * LANES
            out[body + i : body + i + 1, :] = top[:, lane : lane + LANES]
            out[body + pages + i : body + pages + i + 1, :] = total[:, lane : lane + LANES]
    for r in range(KVH):
        if len(outs) > 1:
            outs[r][body + EXT :, :] = reward_ref[me ^ r]
        else:
            outs[0][r, body + EXT :, :] = jnp.zeros((EXT, LANES), jnp.float32)


def merge_kernel(pages, per_page, width, span, chunks, meta_ref, q_ref, fk_ref, fv_ref, w_ref, *rest):
    att = rest[-1]
    split = len(rest) > 3
    parts = rest[:chunks] if split else [rest[0].at[b] for b in range(chunks)]
    outs = rest[chunks:-1] if split else rest[1:-1]
    me = meta_ref[0]
    body = parts[0].shape[0] - 2 * EXT
    page_rows = body // pages
    heads = page_rows // per_page
    rows = pages * per_page

    query = q_ref[:body, :]
    recent = dot(query, fk_ref[...], NT) * SCALE
    line, col = iota(recent.shape, 0), iota(recent.shape, 1)
    mine = (line // page_rows) * per_page + line % per_page
    seen = (mine // STEPS == col // STEPS) & (col <= mine)
    recent = jnp.where(seen, recent, NEG)
    recent_max = jnp.max(recent, axis=-1, keepdims=True)
    recent_exp = jnp.where(seen, jnp.exp(recent - recent_max), 0.0)
    recent_total = jnp.sum(recent_exp, axis=-1, keepdims=True)
    recent_acc = dot(recent_exp.astype(jnp.bfloat16), fv_ref[...])

    extras = []
    for b in range(chunks):
        extra = parts[b][body : body + EXT, :]
        if split:
            shift = -(b * page_rows) % LANES
            extras.append(pltpu.roll(extra, shift, 1) if shift else extra)
        else:
            extras.append(pltpu.roll(extra, meta_ref[2], 1))
    maxima = [extra[:pages] for extra in extras]
    totals = [extra[pages : 2 * pages] for extra in extras]
    top = functools.reduce(jnp.maximum, maxima)
    factors = [jnp.exp(m - top) for m in maxima]
    total = functools.reduce(jnp.add, [f * t for f, t in zip(factors, totals)])

    pick = iota((page_rows, LANES), 0) == iota((page_rows, LANES), 1)

    def column(packed):
        return jnp.concatenate(
            [
                jnp.sum(
                    jnp.where(pick, jnp.broadcast_to(packed[i : i + 1], pick.shape), 0.0),
                    axis=-1,
                    keepdims=True,
                )
                for i in range(pages)
            ],
            axis=0,
        )

    acc = jnp.zeros((body, HD), jnp.float32)
    for b in range(chunks):
        acc = acc + column(factors[b]) * parts[b][:body, :]
    cache_top, cache_total = column(top), column(total)
    top = jnp.maximum(cache_top, recent_max)
    cache_factor = jnp.exp(cache_top - top)
    recent_factor = jnp.exp(recent_max - top)
    total = cache_factor * cache_total + recent_factor * recent_total
    acc = cache_factor * acc + recent_factor * recent_acc
    attended = (acc / total).astype(jnp.bfloat16)
    order = head_major((body, body), pages, per_page, heads)
    attended = dot(order, attended, TN).astype(jnp.bfloat16)
    for h in range(heads):
        att[:, h * HD : (h + 1) * HD] = attended[h * rows : (h + 1) * rows]

    tile = functools.reduce(jnp.add, [parts[b][body + EXT :, :] for b in range(chunks)])
    used = EXT // 2
    value = tile[used:] * lax.rsqrt(tile[:used] / width + EPS)
    mean = jnp.sum(value, keepdims=True) / span
    mean = jnp.where(iota((EXT, LANES), 0) == meta_ref[1], mean, 0.0)

    part = w_ref.shape[1] // chunks
    for r in range(chunks):
        out = outs[r] if split else outs[0].at[me ^ r]
        product = dot(att[...], w_ref[:, aligned(me ^ r, part)])
        for c in range(part // LANES):
            out[c * rows : (c + 1) * rows, :] = product[:, c * LANES : (c + 1) * LANES]
        out[out.shape[0] - EXT :, :] = mean


def sum_kernel(rows, *refs):
    parts, (out_ref, reward_ref) = refs[:-2], refs[-2:]
    if len(parts) == 1:
        parts = [parts[0].at[b] for b in range(parts[0].shape[0])]
    total = parts[0][...]
    for part in parts[1:]:
        total = total + part[...]
    for c in range(out_ref.shape[1] // LANES):
        out_ref[:, c * LANES : (c + 1) * LANES] = total[c * rows : (c + 1) * rows].astype(
            jnp.bfloat16
        )
    reward_ref[...] = total[total.shape[0] - EXT :]


def partner(x, chunks, bits):
    return lax.ppermute(x, "tensor", [(i, i ^ bits) for i in range(chunks)])


def spread_all(x, chunks, index):
    if chunks != KVH:
        every = lax.all_to_all(jnp.broadcast_to(x[None], (chunks,) + x.shape), "tensor", 0, 0, tiled=True)
        return jnp.take(every, index ^ jnp.arange(chunks), axis=0)
    pair = jnp.stack([x, partner(x, chunks, 1)])
    others = [partner(pair, chunks, bits) for bits in (2, 4, 6)]
    return jnp.stack([pair] + others).reshape((chunks,) + x.shape)


def trade(blocks, chunks):
    if len(blocks) == 1:
        return [lax.all_to_all(blocks[0], "tensor", 0, 0, tiled=True)]
    traded = {bits: partner(blocks[bits], chunks, bits) for bits in (4, 5, 6, 7, 2, 3, 1)}
    return [blocks[0]] + [traded[bits] for bits in range(1, chunks)]


def local(
    chunks,
    reward_hidden,
    reward_gain,
    reward_head,
    decode_inputs,
    attn_gain,
    w_query,
    w_keyval,
    w_out,
    cache_keys,
    cache_values,
    lengths,
    slot_map,
):
    slots, width = cache_keys.shape[:2]
    depth, qcols = w_query.shape
    kvcols = w_keyval.shape[1]
    part = decode_inputs.shape[-1]
    heads = qcols // HD
    group = heads * chunks // KVH
    split = group // heads
    pages = slots // PAIR
    per_page = PAIR * STEPS
    page_rows = per_page * group
    rows = slots * STEPS
    body = rows * heads
    mine, index = lax.axis_index("dp"), lax.axis_index("tensor")
    swap = [(0, 1), (1, 0)]

    ids = jnp.arange(slot_map.shape[0])
    kept = slot_map == ids
    home = slot_map // slots
    before = kept[None, :] & (ids[None, :] // slots == home[:, None]) & (ids[None, :] < slot_map[:, None])
    place = home * slots + PAIR * jnp.sum(before, axis=1) + (slot_map != ids)
    place_own = lax.dynamic_slice_in_dim(place, mine * slots, slots)
    place_far = lax.dynamic_slice_in_dim(place, (1 - mine) * slots, slots)
    lead = place[None, :] == (mine * slots + PAIR * jnp.arange(pages))[:, None]
    page = jnp.sum(jnp.where(lead, ids[None, :], 0), axis=1) - mine * slots
    live = jnp.sum(jnp.where(lead, lengths[None, :], 0), axis=1)
    work = jnp.arange(rows)
    steps = jnp.arange(STEPS)
    both = jnp.stack([place_own, place_far]) - mine * slots
    take = (both[None, None, :, None, :] == jnp.arange(slots)[:, None, None, None, None]) & (
        steps[None, :, None, None, None] == steps[None, None, None, :, None]
    )
    take = take.reshape(rows, 2 * rows).astype(jnp.bfloat16)
    bases = jnp.stack([mine, 1 - mine]) * slots
    give = (
        (place_own[None, :, None] - bases[None, None, :])[..., None, None]
        == jnp.arange(slots)[None, None, None, :, None]
    ) & (steps[:, None, None, None, None] == steps[None, None, None, None, :])
    give = give.reshape(rows, 2 * rows).astype(jnp.bfloat16)

    direct = chunks == KVH
    own = spread_all(decode_inputs.reshape(rows, part), chunks, index)
    far = lax.ppermute(own, "dp", swap)

    hidden = reward_hidden.astype(jnp.float32)
    squares = jnp.sum(hidden * hidden, axis=-1)
    head_dot = jnp.sum(hidden * (reward_gain * reward_head), axis=-1)
    span = squares.shape[1]

    def tile(values):
        values = values.reshape(chunks, -1)
        size = EXT // 2 * LANES
        return jnp.pad(values, ((0, 0), (0, size - values.shape[1]))).reshape(
            chunks, EXT // 2, LANES
        )

    reward_parts = jnp.concatenate([tile(squares), tile(head_dot)], axis=1)

    pieces = max(kvcols // LANES, 1)
    packed_rows = body + pieces * rows
    packed = pl.pallas_call(
        functools.partial(project_kernel, pages, per_page, depth),
        in_specs=[SMEM, VMEM, VMEM, VMEM, VMEM, ANY, ANY],
        out_specs=VMEM,
        out_shape=jax.ShapeDtypeStruct((packed_rows, LANES), jnp.bfloat16),
        scratch_shapes=[
            pltpu.VMEM((chunks, rows, part), jnp.bfloat16),
            pltpu.VMEM((chunks, part, qcols), jnp.bfloat16),
            pltpu.VMEM((chunks, part, kvcols), jnp.bfloat16),
            pltpu.SemaphoreType.DMA((2, chunks)),
        ],
        compiler_params=pltpu.CompilerParams(vmem_limit_bytes=28 * MIB),
        cost_estimate=pl.CostEstimate(
            flops=2 * rows * depth * (qcols + kvcols),
            bytes_accessed=2 * depth * (qcols + kvcols),
            transcendentals=0,
        ),
        name="project",
    )(index[None], own, far, take, attn_gain.reshape(chunks, 1, part), w_query, w_keyval)
    gathered = spread_all(packed, chunks, index)

    kv_head = index * heads // group
    if kvcols < LANES:
        fresh = jnp.take(gathered[:, body:, :kvcols], index ^ jnp.arange(chunks), axis=0)
        fresh = fresh.transpose(1, 0, 2).reshape(rows, 2 * KVH, HD).transpose(1, 0, 2)
        fresh_k = lax.dynamic_index_in_dim(fresh, kv_head, 0, keepdims=False)
        fresh_v = lax.dynamic_index_in_dim(fresh, KVH + kv_head, 0, keepdims=False)
    else:

        def fresh_of(column):
            start = (column // pieces) ^ index, body + column % pieces * rows, 0
            return lax.dynamic_slice(gathered, start, (1, rows, LANES))[0]

        fresh_k, fresh_v = fresh_of(kv_head), fresh_of(KVH + kv_head)
    queries = gathered
    if not direct:
        queries = (
            jnp.take(gathered[:, :body], index ^ jnp.arange(chunks), axis=0)
            .reshape(KVH, split, pages, heads * per_page, HD)
            .transpose(0, 2, 1, 3, 4)
            .reshape(KVH, pages * page_rows, HD)
        )

    base = index if direct else index * 0
    meta = jnp.concatenate([page, live, (index * width)[None], base[None]]).astype(jnp.int32)
    big = pages * page_rows
    block = (big + 2 * EXT, HD)
    attended = pl.pallas_call(
        functools.partial(attend_kernel, pages, page_rows),
        in_specs=[SMEM, VMEM, ANY, ANY, VMEM],
        out_specs=[VMEM] * (KVH if direct else 1),
        out_shape=(
            [jax.ShapeDtypeStruct(block, jnp.float32)] * KVH
            if direct
            else [jax.ShapeDtypeStruct((KVH,) + block, jnp.float32)]
        ),
        scratch_shapes=[
            pltpu.VMEM((KVH * page_rows, KVH * HD), jnp.bfloat16),
            pltpu.VMEM((KVH * page_rows, KVH * HD), jnp.float32),
            pltpu.VMEM((pages, width, KVH * HD), jnp.bfloat16),
            pltpu.VMEM((pages, width, KVH * HD), jnp.bfloat16),
            pltpu.SemaphoreType.DMA((2, pages)),
        ],
        compiler_params=pltpu.CompilerParams(vmem_limit_bytes=12 * MIB),
        cost_estimate=pl.CostEstimate(
            flops=4 * pages * width * KVH * HD * KVH * page_rows,
            bytes_accessed=4 * pages * width * KVH * HD,
            transcendentals=pages * width * KVH * page_rows,
        ),
        name="attend",
    )(meta, queries, cache_keys, cache_values, reward_parts)
    if not direct:
        acc = (
            attended[0][:, :big]
            .reshape(KVH, pages, split, heads * per_page, HD)
            .transpose(0, 2, 1, 3, 4)
            .reshape(chunks, body, HD)
        )
        extra = jnp.repeat(attended[0][:, big : big + EXT], split, axis=0)
        attended = [jnp.concatenate([acc, extra, reward_parts], axis=1)]
    parts = trade(attended, chunks)

    chunk_rows = part // LANES * rows + EXT
    own_row = index * (slots * span // chunks) // span
    shift = -(index * heads * per_page) % LANES
    meta = jnp.stack([index, own_row, shift]).astype(jnp.int32)
    partial = pl.pallas_call(
        functools.partial(merge_kernel, pages, per_page, depth, span, chunks),
        in_specs=[SMEM] + [VMEM] * (4 + len(parts)),
        out_specs=[VMEM] * len(parts),
        out_shape=(
            [jax.ShapeDtypeStruct((chunk_rows, LANES), jnp.float32)] * chunks
            if direct
            else [jax.ShapeDtypeStruct((chunks, chunk_rows, LANES), jnp.float32)]
        ),
        scratch_shapes=[pltpu.VMEM((rows, qcols), jnp.bfloat16)],
        compiler_params=pltpu.CompilerParams(vmem_limit_bytes=8 * MIB),
        cost_estimate=pl.CostEstimate(
            flops=2 * rows * qcols * depth, bytes_accessed=2 * qcols * depth, transcendentals=0
        ),
        name="merge",
    )(meta, packed, fresh_k, fresh_v, w_out, *parts)
    partial = trade(partial, chunks)

    decoded, reward = pl.pallas_call(
        functools.partial(sum_kernel, rows),
        out_shape=(
            jax.ShapeDtypeStruct((rows, part), jnp.bfloat16),
            jax.ShapeDtypeStruct((EXT, LANES), jnp.float32),
        ),
        compiler_params=pltpu.CompilerParams(vmem_limit_bytes=8 * MIB),
        name="total",
    )(*partial)
    far = lax.ppermute(decoded, "dp", swap)
    decoded = dot(give, jnp.concatenate([decoded, far], axis=0)).astype(jnp.bfloat16)
    return (reward[:slots, 0], decoded.reshape(STEPS, slots, part))


def solution(mesh):
    return jax.shard_map(
        functools.partial(local, mesh.shape["tensor"]),
        mesh=mesh,
        in_specs=(
            P(("groups", "dp"), None, "tensor"),
            P("tensor"),
            P("tensor"),
            P(None, ("groups", "dp"), "tensor"),
            P(),
            P(None, "tensor"),
            P(None, "tensor"),
            P("tensor", None),
            P(("groups", "dp"), "tensor", None),
            P(("groups", "dp"), "tensor", None),
            P("groups"),
            P("groups"),
        ),
        out_specs=(P(("groups", "dp")), P(None, ("groups", "dp"), "tensor")),
        check_vma=False,
    )
```

```python
import functools

import jax
import jax.numpy as jnp
from jax import lax
from jax.experimental import pallas as pl
from jax.experimental.pallas import tpu as pltpu
from jax.sharding import PartitionSpec as P

HD = 128
KVH = 8
STEPS = 2
PAIR = 2
LANES = 128
EXT = 8
EPS = 1e-05
NEG = -1e30
SCALE = HD ** (-0.5)
NT = (((1,), (1,)), ((), ()))
TN = (((0,), (0,)), ((), ()))
MIB = 1 << 20
ANY = pl.BlockSpec(memory_space=pl.ANY)
VMEM = pl.BlockSpec(memory_space=pltpu.VMEM)
SMEM = pl.BlockSpec(memory_space=pltpu.SMEM)


def iota(shape, dim):
    return lax.broadcasted_iota(jnp.int32, shape, dim)


def dot(a, b, dims=(((1,), (0,)), ((), ()))):
    return lax.dot_general(a, b, dims, preferred_element_type=jnp.float32)


def head_major(shape, pages, per_page, heads):
    o, s = iota(shape, 0), iota(shape, 1)
    row = o % per_page
    head = (o // per_page) % heads
    page = o // (per_page * heads)
    return (s == (head * pages + page) * per_page + row).astype(jnp.bfloat16)


def aligned(index, size):
    return pl.ds(pl.multiple_of(index * size, size), size)


def plan_kernel(slots, steps, map_ref, length_ref, meta_ref, take_ref, give_ref, before_ref, place_ref):
    count = map_ref.shape[0]
    mine = lax.axis_index("dp")
    base = mine * slots
    for block in range(count // slots):
        found = jnp.int32(0)
        for s in range(block * slots, (block + 1) * slots):
            before_ref[s] = found
            found = found + (map_ref[s] == s).astype(jnp.int32)
    for s in range(slots):
        own = map_ref[base + s] == base + s

        @pl.when(own)
        def _():
            slot = before_ref[base + s]
            meta_ref[slot] = jnp.int32(s)
            meta_ref[slots // PAIR + slot] = length_ref[base + s]

    for r in range(count):
        source = map_ref[r]
        place_ref[r] = (
            lax.div(source, slots) * slots
            + PAIR * before_ref[source]
            + (source != r).astype(jnp.int32)
        )
    rows = slots * steps
    line, col = iota((rows, 2 * rows), 0), iota((rows, 2 * rows), 1)
    same = line % steps == (col // slots) % steps
    take = jnp.zeros((rows, 2 * rows), jnp.bool_)
    give = jnp.zeros((rows, 2 * rows), jnp.bool_)
    for side in range(2):
        start = base if side == 0 else (1 - mine) * slots
        for s in range(slots):
            target = place_ref[start + s] - base
            column = (col // rows == side) & (col % slots == s)
            take = take | (same & column & (line // steps == target))
    for s in range(slots):
        place = place_ref[base + s]
        far = (lax.div(place, slots) != mine).astype(jnp.int32)
        target = far * rows + lax.rem(place, slots) * steps
        give = give | ((line % slots == s) & (col == line // slots + target))
    take_ref[...] = take.astype(jnp.float32).astype(jnp.bfloat16)
    give_ref[...] = give.astype(jnp.float32).astype(jnp.bfloat16)


def pull_kernel(after_ref, src_ref, out_ref, sems):
    parts = sems.shape[0]
    size = src_ref.shape[0] // parts
    copies = [
        pltpu.make_async_copy(
            src_ref.at[pl.ds(p * size, size)], out_ref.at[pl.ds(p * size, size)], sems.at[p]
        )
        for p in range(parts)
    ]
    for copy in copies:
        copy.start()
    for copy in copies:
        copy.wait()


def side_kernel(pages, after_ref, meta_ref, k_ref, v_ref, hidden_ref, gain_ref, head_ref, keys_ref, values_ref, squares_ref, dots_ref, buffer, sems, page_sems):
    slots = hidden_ref.shape[0]
    loads = [
        pltpu.make_async_copy(hidden_ref.at[s], buffer.at[s], sems.at[s]) for s in range(slots)
    ]
    for load in loads:
        load.start()
    copies = []
    for i in range(pages):
        page = meta_ref[i]
        copies.append(pltpu.make_async_copy(k_ref.at[page], keys_ref.at[i], page_sems.at[0, i]))
        copies.append(pltpu.make_async_copy(v_ref.at[page], values_ref.at[i], page_sems.at[1, i]))
    for copy in copies:
        copy.start()
    weight = gain_ref[...] * head_ref[...]
    for s in range(slots):
        loads[s].wait()
        hidden = buffer[s].astype(jnp.float32)
        squares_ref[s] = jnp.sum(hidden * hidden, axis=-1)
        dots_ref[s] = jnp.sum(hidden * weight, axis=-1)
    for copy in copies:
        copy.wait()


def project_kernel(pages, per_page, width, own_ref, far_ref, take_ref, gain_ref, wq_ref, wkv_ref, out_ref, tokens, wkv, sems):
    me = lax.axis_index("tensor")
    chunks, rows, depth = own_ref.shape
    copies = []
    for r in range(chunks):
        copy = pltpu.make_async_copy(wkv_ref.at[aligned(me ^ r, depth)], wkv.at[r], sems.at[r])
        copy.start()
        copies.append(copy)

    total = jnp.zeros((rows, depth), jnp.float32)
    for r in range(chunks):
        both = jnp.concatenate([own_ref[r], far_ref[r]], axis=0)
        part = dot(take_ref[...], both)
        tokens[r] = part.astype(jnp.bfloat16)
        total = total + part * part
    inv = lax.rsqrt(jnp.sum(total, axis=-1, keepdims=True) / width + EPS)

    query = jnp.zeros((rows, wq_ref.shape[1]), jnp.float32)
    keyval = jnp.zeros((rows, wkv.shape[2]), jnp.float32)
    for r in range(chunks):
        normed = (tokens[r].astype(jnp.float32) * inv * gain_ref[me ^ r]).astype(jnp.bfloat16)
        query = query + dot(normed, wq_ref[aligned(me ^ r, depth), :])
        copies[r].wait()
        keyval = keyval + dot(normed, wkv[r])

    heads = query.shape[1] // HD
    query = query.astype(jnp.bfloat16)
    stacked = jnp.concatenate([query[:, h * HD : (h + 1) * HD] for h in range(heads)], axis=0)
    order = head_major((rows * heads, rows * heads), pages, per_page, heads)
    body = rows * heads
    out_ref[:body] = dot(order, stacked).astype(jnp.bfloat16)
    keyval = keyval.astype(jnp.bfloat16)
    columns = keyval.shape[1]
    if columns < LANES:
        pad = jnp.zeros((rows, LANES - columns), jnp.bfloat16)
        keyval = jnp.concatenate([keyval, pad], axis=1)
    for v in range(keyval.shape[1] // LANES):
        out_ref[body + v * rows : body + (v + 1) * rows] = keyval[:, v * LANES : (v + 1) * LANES]


def attend_kernel(pages, page_rows, split, meta_ref, q_ref, k_ref, v_ref, squares_ref, dots_ref, *rest):
    outs, (spread, product) = rest[:-2], rest[-2:]
    width = k_ref.shape[1]
    span = KVH * page_rows
    body = pages * page_rows
    first = lax.axis_index("tensor") * width
    me = lax.axis_index("tensor") if len(outs) > 1 else 0
    spread[...] = jnp.zeros_like(spread)
    for i in range(pages):
        for r in range(KVH):
            spread[r * page_rows : (r + 1) * page_rows, aligned(me ^ r, HD)] = q_ref[
                r, i * page_rows : (i + 1) * page_rows, :
            ]
        scores = dot(k_ref[i], spread[...], NT) * SCALE
        valid = first + iota((width, span), 0) < meta_ref[pages + i]
        scores = jnp.where(valid, scores, NEG)
        top = jnp.max(scores, axis=0, keepdims=True)
        expo = jnp.where(valid, jnp.exp(scores - top), 0.0)
        total = jnp.sum(expo, axis=0, keepdims=True)
        product[...] = dot(expo.astype(jnp.bfloat16), v_ref[i], TN)
        for r in range(KVH):
            out = outs[r] if len(outs) > 1 else outs[0].at[r]
            out[i * page_rows : (i + 1) * page_rows, :] = product[
                r * page_rows : (r + 1) * page_rows, aligned(me ^ r, HD)
            ]
            lane = (r * page_rows) // LANES * LANES
            out[body + i : body + i + 1, :] = top[:, lane : lane + LANES]
            out[body + pages + i : body + pages + i + 1, :] = total[:, lane : lane + LANES]
    for r in range(KVH):
        if len(outs) > 1:
            outs[r][body + EXT :, :] = jnp.concatenate(
                [squares_ref[me ^ r], dots_ref[me ^ r]], axis=0
            )
        else:
            outs[0][r, body + EXT :, :] = jnp.zeros((EXT, LANES), jnp.float32)


def merge_kernel(pages, per_page, width, span, slots, chunks, q_ref, gathered_ref, w_ref, *rest):
    att = rest[-1]
    split = len(rest) > 3
    parts = rest[:chunks] if split else [rest[0].at[b] for b in range(chunks)]
    outs = rest[chunks:-1] if split else rest[1:-1]
    me = lax.axis_index("tensor")
    body = parts[0].shape[0] - 2 * EXT
    page_rows = body // pages
    heads = page_rows // per_page
    rows = pages * per_page

    kv_head = lax.div(me * heads, heads * chunks // KVH)
    if split:
        pieces = (gathered_ref.shape[1] - body) // rows

        def fresh_of(column):
            source = lax.div(column, pieces) ^ me
            start = pl.multiple_of(body + lax.rem(column, pieces) * rows, rows)
            return gathered_ref[source, pl.ds(start, rows), :]

        fresh_k, fresh_v = fresh_of(kv_head), fresh_of(KVH + kv_head)
    else:
        fresh_k, fresh_v = gathered_ref[kv_head], gathered_ref[KVH + kv_head]

    query = q_ref[:body, :]
    recent = dot(query, fresh_k, NT) * SCALE
    line, col = iota(recent.shape, 0), iota(recent.shape, 1)
    mine = (line // page_rows) * per_page + line % per_page
    seen = (mine // STEPS == col // STEPS) & (col <= mine)
    recent = jnp.where(seen, recent, NEG)
    recent_max = jnp.max(recent, axis=-1, keepdims=True)
    recent_exp = jnp.where(seen, jnp.exp(recent - recent_max), 0.0)
    recent_total = jnp.sum(recent_exp, axis=-1, keepdims=True)
    recent_acc = dot(recent_exp.astype(jnp.bfloat16), fresh_v)

    extras = []
    for b in range(chunks):
        extra = parts[b][body : body + EXT, :]
        if split:
            shift = -(b * page_rows) % LANES
            extras.append(pltpu.roll(extra, shift, 1) if shift else extra)
        else:
            shift = lax.rem(LANES - lax.rem(me * page_rows, LANES), LANES)
            extras.append(pltpu.roll(extra, shift, 1))
    maxima = [extra[:pages] for extra in extras]
    totals = [extra[pages : 2 * pages] for extra in extras]
    top = functools.reduce(jnp.maximum, maxima)
    factors = [jnp.exp(m - top) for m in maxima]
    total = functools.reduce(jnp.add, [f * t for f, t in zip(factors, totals)])

    pick = iota((page_rows, LANES), 0) == iota((page_rows, LANES), 1)

    def column(packed):
        return jnp.concatenate(
            [
                jnp.sum(
                    jnp.where(pick, jnp.broadcast_to(packed[i : i + 1], pick.shape), 0.0),
                    axis=-1,
                    keepdims=True,
                )
                for i in range(pages)
            ],
            axis=0,
        )

    acc = jnp.zeros((body, HD), jnp.float32)
    for b in range(chunks):
        acc = acc + column(factors[b]) * parts[b][:body, :]
    cache_top, cache_total = column(top), column(total)
    top = jnp.maximum(cache_top, recent_max)
    cache_factor = jnp.exp(cache_top - top)
    recent_factor = jnp.exp(recent_max - top)
    total = cache_factor * cache_total + recent_factor * recent_total
    acc = cache_factor * acc + recent_factor * recent_acc
    attended = (acc / total).astype(jnp.bfloat16)
    order = head_major((body, body), pages, per_page, heads)
    attended = dot(order, attended, TN).astype(jnp.bfloat16)
    for h in range(heads):
        att[:, h * HD : (h + 1) * HD] = attended[h * rows : (h + 1) * rows]

    tile = functools.reduce(jnp.add, [parts[b][body + EXT :, :] for b in range(chunks)])
    used = EXT // 2
    value = tile[used:] * lax.rsqrt(tile[:used] / width + EPS)
    mean = jnp.sum(value, keepdims=True) / span
    own = lax.div(me * (slots * span // chunks), span)
    mean = jnp.where(iota((EXT, LANES), 0) == own, mean, 0.0)

    part = w_ref.shape[1] // chunks
    for r in range(chunks):
        out = outs[r] if split else outs[0].at[me ^ r]
        product = dot(att[...], w_ref[:, aligned(me ^ r, part)])
        for c in range(part // LANES):
            out[c * rows : (c + 1) * rows, :] = product[:, c * LANES : (c + 1) * LANES]
        out[out.shape[0] - EXT :, :] = mean


def sum_kernel(rows, *refs):
    parts, (out_ref, reward_ref) = refs[:-2], refs[-2:]
    if len(parts) == 1:
        parts = [parts[0].at[b] for b in range(parts[0].shape[0])]
    total = parts[0][...]
    for part in parts[1:]:
        total = total + part[...]
    for c in range(out_ref.shape[1] // LANES):
        out_ref[:, c * LANES : (c + 1) * LANES] = total[c * rows : (c + 1) * rows].astype(
            jnp.bfloat16
        )
    reward_ref[...] = total[total.shape[0] - EXT :]


def partner(x, chunks, bits):
    return lax.ppermute(x, "tensor", [(i, i ^ bits) for i in range(chunks)])


def spread_all(x, chunks, index):
    if chunks != KVH:
        every = lax.all_to_all(jnp.broadcast_to(x[None], (chunks,) + x.shape), "tensor", 0, 0, tiled=True)
        return jnp.take(every, index ^ jnp.arange(chunks), axis=0), x
    pair = jnp.stack([x, partner(x, chunks, 1)])
    others = [partner(pair, chunks, bits) for bits in (2, 4, 6)]
    return jnp.stack([pair] + others).reshape((chunks,) + x.shape), pair


def trade(blocks, chunks):
    if len(blocks) == 1:
        return [lax.all_to_all(blocks[0], "tensor", 0, 0, tiled=True)]
    traded = {bits: partner(blocks[bits], chunks, bits) for bits in (4, 5, 6, 7, 2, 3, 1)}
    return [blocks[0]] + [traded[bits] for bits in range(1, chunks)]


def local(
    chunks,
    reward_hidden,
    reward_gain,
    reward_head,
    decode_inputs,
    attn_gain,
    w_query,
    w_keyval,
    w_out,
    cache_keys,
    cache_values,
    lengths,
    slot_map,
):
    slots, width = cache_keys.shape[:2]
    depth, qcols = w_query.shape
    kvcols = w_keyval.shape[1]
    part = decode_inputs.shape[-1]
    heads = qcols // HD
    group = heads * chunks // KVH
    split = group // heads
    pages = slots // PAIR
    per_page = PAIR * STEPS
    page_rows = per_page * group
    rows = slots * STEPS
    body = rows * heads
    index = lax.axis_index("tensor")
    swap = [(0, 1), (1, 0)]
    direct = chunks == KVH

    meta, take, give = pl.pallas_call(
        functools.partial(plan_kernel, slots, STEPS),
        in_specs=[SMEM, SMEM],
        out_specs=[SMEM, VMEM, VMEM],
        out_shape=(
            jax.ShapeDtypeStruct((2 * pages,), jnp.int32),
            jax.ShapeDtypeStruct((rows, 2 * rows), jnp.bfloat16),
            jax.ShapeDtypeStruct((rows, 2 * rows), jnp.bfloat16),
        ),
        scratch_shapes=[
            pltpu.SMEM(slot_map.shape, jnp.int32),
            pltpu.SMEM(slot_map.shape, jnp.int32),
        ],
        compiler_params=pltpu.CompilerParams(vmem_limit_bytes=MIB),
        name="plan",
    )(slot_map, lengths)

    own, after = spread_all(decode_inputs.reshape(rows, part), chunks, index)
    w_query = pl.pallas_call(
        pull_kernel,
        in_specs=[ANY, ANY],
        out_specs=VMEM,
        out_shape=pltpu.VMEM(w_query.shape, w_query.dtype),
        scratch_shapes=[pltpu.SemaphoreType.DMA((KVH,))],
        compiler_params=pltpu.CompilerParams(vmem_limit_bytes=46 * MIB),
        cost_estimate=pl.CostEstimate(
            flops=0, bytes_accessed=4 * depth * qcols, transcendentals=0
        ),
        name="pull",
    )(after, w_query)
    far = lax.ppermute(own, "dp", swap)

    pieces = max(kvcols // LANES, 1)
    packed_rows = body + pieces * rows
    packed = pl.pallas_call(
        functools.partial(project_kernel, pages, per_page, depth),
        in_specs=[VMEM, VMEM, VMEM, VMEM, VMEM, ANY],
        out_specs=VMEM,
        out_shape=jax.ShapeDtypeStruct((packed_rows, LANES), jnp.bfloat16),
        scratch_shapes=[
            pltpu.VMEM((chunks, rows, part), jnp.bfloat16),
            pltpu.VMEM((chunks, part, kvcols), jnp.bfloat16),
            pltpu.SemaphoreType.DMA((chunks,)),
        ],
        compiler_params=pltpu.CompilerParams(vmem_limit_bytes=46 * MIB),
        cost_estimate=pl.CostEstimate(
            flops=2 * rows * depth * (qcols + kvcols),
            bytes_accessed=2 * depth * (qcols + kvcols),
            transcendentals=0,
        ),
        name="project",
    )(own, far, take, attn_gain.reshape(chunks, 1, part), w_query, w_keyval)
    gathered, after = spread_all(packed, chunks, index)

    span = reward_hidden.shape[1]
    page_shape = (pages,) + cache_keys.shape[1:]
    keys, values, squares, dots = pl.pallas_call(
        functools.partial(side_kernel, pages),
        in_specs=[ANY, SMEM, ANY, ANY, ANY, VMEM, VMEM],
        out_specs=[VMEM] * 4,
        out_shape=(
            pltpu.VMEM(page_shape, cache_keys.dtype),
            pltpu.VMEM(page_shape, cache_values.dtype),
            jax.ShapeDtypeStruct((slots, span), jnp.float32),
            jax.ShapeDtypeStruct((slots, span), jnp.float32),
        ),
        scratch_shapes=[
            pltpu.VMEM(reward_hidden.shape, reward_hidden.dtype),
            pltpu.SemaphoreType.DMA((slots,)),
            pltpu.SemaphoreType.DMA((2, pages)),
        ],
        compiler_params=pltpu.CompilerParams(vmem_limit_bytes=40 * MIB),
        cost_estimate=pl.CostEstimate(
            flops=4 * reward_hidden.size,
            bytes_accessed=2 * reward_hidden.size + 8 * pages * width * KVH * HD,
            transcendentals=0,
        ),
        name="side",
    )(after, meta, cache_keys, cache_values, reward_hidden, reward_gain[None], reward_head[None])

    def tile(values):
        values = values.reshape(chunks, -1)
        size = EXT // 2 * LANES
        return jnp.pad(values, ((0, 0), (0, size - values.shape[1]))).reshape(
            chunks, EXT // 2, LANES
        )

    squares, dots = tile(squares), tile(dots)
    fresh = gathered
    if not direct:
        fresh = jnp.take(gathered[:, body:, :kvcols], index ^ jnp.arange(chunks), axis=0)
        fresh = fresh.transpose(1, 0, 2).reshape(rows, 2 * KVH, HD).transpose(1, 0, 2)
    queries = gathered
    if not direct:
        queries = (
            jnp.take(gathered[:, :body], index ^ jnp.arange(chunks), axis=0)
            .reshape(KVH, split, pages, heads * per_page, HD)
            .transpose(0, 2, 1, 3, 4)
            .reshape(KVH, pages * page_rows, HD)
        )

    big = pages * page_rows
    block = (big + 2 * EXT, HD)
    attended = pl.pallas_call(
        functools.partial(attend_kernel, pages, page_rows, split),
        in_specs=[SMEM] + [VMEM] * 5,
        out_specs=[VMEM] * (KVH if direct else 1),
        out_shape=(
            [jax.ShapeDtypeStruct(block, jnp.float32)] * KVH
            if direct
            else [jax.ShapeDtypeStruct((KVH,) + block, jnp.float32)]
        ),
        scratch_shapes=[
            pltpu.VMEM((KVH * page_rows, KVH * HD), jnp.bfloat16),
            pltpu.VMEM((KVH * page_rows, KVH * HD), jnp.float32),
        ],
        compiler_params=pltpu.CompilerParams(vmem_limit_bytes=12 * MIB),
        cost_estimate=pl.CostEstimate(
            flops=4 * pages * width * KVH * HD * KVH * page_rows,
            bytes_accessed=4 * pages * width * KVH * HD,
            transcendentals=pages * width * KVH * page_rows,
        ),
        name="attend",
    )(meta, queries, keys, values, squares, dots)
    if not direct:
        acc = (
            attended[0][:, :big]
            .reshape(KVH, pages, split, heads * per_page, HD)
            .transpose(0, 2, 1, 3, 4)
            .reshape(chunks, body, HD)
        )
        extra = jnp.repeat(attended[0][:, big : big + EXT], split, axis=0)
        attended = [jnp.concatenate([acc, extra, squares, dots], axis=1)]
    parts = trade(attended, chunks)

    chunk_rows = part // LANES * rows + EXT
    partial = pl.pallas_call(
        functools.partial(merge_kernel, pages, per_page, depth, span, slots, chunks),
        in_specs=[VMEM] * (3 + len(parts)),
        out_specs=[VMEM] * len(parts),
        out_shape=(
            [jax.ShapeDtypeStruct((chunk_rows, LANES), jnp.float32)] * chunks
            if direct
            else [jax.ShapeDtypeStruct((chunks, chunk_rows, LANES), jnp.float32)]
        ),
        scratch_shapes=[pltpu.VMEM((rows, qcols), jnp.bfloat16)],
        compiler_params=pltpu.CompilerParams(vmem_limit_bytes=8 * MIB),
        cost_estimate=pl.CostEstimate(
            flops=2 * rows * qcols * depth, bytes_accessed=2 * qcols * depth, transcendentals=0
        ),
        name="merge",
    )(packed, fresh, w_out, *parts)
    partial = trade(partial, chunks)

    decoded, reward = pl.pallas_call(
        functools.partial(sum_kernel, rows),
        out_shape=(
            jax.ShapeDtypeStruct((rows, part), jnp.bfloat16),
            jax.ShapeDtypeStruct((EXT, LANES), jnp.float32),
        ),
        compiler_params=pltpu.CompilerParams(vmem_limit_bytes=8 * MIB),
        name="total",
    )(*partial)
    far = lax.ppermute(decoded, "dp", swap)
    decoded = dot(give, jnp.concatenate([decoded, far], axis=0)).astype(jnp.bfloat16)
    return (reward[:slots, 0], decoded.reshape(STEPS, slots, part))


def solution(mesh):
    return jax.shard_map(
        functools.partial(local, mesh.shape["tensor"]),
        mesh=mesh,
        in_specs=(
            P(("groups", "dp"), None, "tensor"),
            P("tensor"),
            P("tensor"),
            P(None, ("groups", "dp"), "tensor"),
            P(),
            P(None, "tensor"),
            P(None, "tensor"),
            P("tensor", None),
            P(("groups", "dp"), "tensor", None),
            P(("groups", "dp"), "tensor", None),
            P("groups"),
            P("groups"),
        ),
        out_specs=(P(("groups", "dp")), P(None, ("groups", "dp"), "tensor")),
        check_vma=False,
    )
```

```python
import functools

import jax
import jax.numpy as jnp
from jax import lax
from jax.experimental import pallas as pl
from jax.experimental.pallas import tpu as pltpu
from jax.sharding import PartitionSpec as P

HD = 128
KVH = 8
STEPS = 2
PAIR = 2
LANES = 128
EXT = 8
EPS = 1e-05
NEG = -1e30
SCALE = HD ** (-0.5)
NT = (((1,), (1,)), ((), ()))
TN = (((0,), (0,)), ((), ()))
MIB = 1 << 20
ANY = pl.BlockSpec(memory_space=pl.ANY)
VMEM = pl.BlockSpec(memory_space=pltpu.VMEM)
SMEM = pl.BlockSpec(memory_space=pltpu.SMEM)


def iota(shape, dim):
    return lax.broadcasted_iota(jnp.int32, shape, dim)


def dot(a, b, dims=(((1,), (0,)), ((), ()))):
    return lax.dot_general(a, b, dims, preferred_element_type=jnp.float32)


def head_major(shape, pages, per_page, heads):
    o, s = iota(shape, 0), iota(shape, 1)
    row = o % per_page
    head = (o // per_page) % heads
    page = o // (per_page * heads)
    return (s == (head * pages + page) * per_page + row).astype(jnp.bfloat16)


def aligned(index, size):
    return pl.ds(pl.multiple_of(index * size, size), size)


def plan_kernel(slots, steps, map_ref, length_ref, *rest):
    meta_ref, take_ref, give_ref, before_ref, place_ref = rest[-5:]
    count = map_ref.shape[0]
    mine = lax.axis_index("dp")
    base = mine * slots
    for block in range(count // slots):
        found = jnp.int32(0)
        for s in range(block * slots, (block + 1) * slots):
            before_ref[s] = found
            found = found + (map_ref[s] == s).astype(jnp.int32)
    for s in range(slots):
        own = map_ref[base + s] == base + s

        @pl.when(own)
        def _():
            slot = before_ref[base + s]
            meta_ref[slot] = jnp.int32(s)
            meta_ref[slots // PAIR + slot] = length_ref[base + s]

    for r in range(count):
        source = map_ref[r]
        place_ref[r] = (
            lax.div(source, slots) * slots
            + PAIR * before_ref[source]
            + (source != r).astype(jnp.int32)
        )
    rows = slots * steps
    line, col = iota((rows, 2 * rows), 0), iota((rows, 2 * rows), 1)
    same = line % steps == (col // slots) % steps
    take = jnp.zeros((rows, 2 * rows), jnp.bool_)
    give = jnp.zeros((rows, 2 * rows), jnp.bool_)
    for side in range(2):
        start = base if side == 0 else (1 - mine) * slots
        for s in range(slots):
            target = place_ref[start + s] - base
            column = (col // rows == side) & (col % slots == s)
            take = take | (same & column & (line // steps == target))
    for s in range(slots):
        place = place_ref[base + s]
        far = (lax.div(place, slots) != mine).astype(jnp.int32)
        target = far * rows + lax.rem(place, slots) * steps
        give = give | ((line % slots == s) & (col == line // slots + target))
    take_ref[...] = take.astype(jnp.float32).astype(jnp.bfloat16)
    give_ref[...] = give.astype(jnp.float32).astype(jnp.bfloat16)


def reward_kernel(after_ref, hidden_ref, gain_ref, head_ref, *rest):
    out_ref, buffer, sems = rest[-3:]
    slots = hidden_ref.shape[0]
    loads = [
        pltpu.make_async_copy(hidden_ref.at[s], buffer.at[s], sems.at[s]) for s in range(slots)
    ]
    for load in loads:
        load.start()
    weight = gain_ref[...] * head_ref[...]
    for s in range(slots):
        loads[s].wait()
        hidden = buffer[s].astype(jnp.float32)
        for half, value in enumerate((hidden * hidden, hidden * weight)):
            sums = jnp.sum(value, axis=-1)
            if len(out_ref.shape) == 2:
                out_ref[half * slots + s] = sums
                continue
            for c in range(EXT // 2):
                piece = jnp.zeros((LANES,), jnp.float32)
                if c < sums.shape[0] // LANES:
                    piece = sums[c * LANES : (c + 1) * LANES]
                out_ref[s, half * (EXT // 2) + c] = piece


def project_kernel(pages, per_page, width, own_ref, far_ref, take_ref, gain_ref, wq_ref, wkv_ref, out_ref, tokens):
    me = lax.axis_index("tensor")
    chunks, rows, depth = own_ref.shape
    total = jnp.zeros((rows, depth), jnp.float32)
    for r in range(chunks):
        both = jnp.concatenate([own_ref[r], far_ref[r]], axis=0)
        part = dot(take_ref[...], both)
        tokens[r] = part.astype(jnp.bfloat16)
        total = total + part * part
    inv = lax.rsqrt(jnp.sum(total, axis=-1, keepdims=True) / width + EPS)

    query = jnp.zeros((rows, wq_ref.shape[1]), jnp.float32)
    keyval = jnp.zeros((rows, wkv_ref.shape[1]), jnp.float32)
    for r in range(chunks):
        normed = (tokens[r].astype(jnp.float32) * inv * gain_ref[me ^ r]).astype(jnp.bfloat16)
        query = query + dot(normed, wq_ref[aligned(me ^ r, depth), :])
        keyval = keyval + dot(normed, wkv_ref[aligned(me ^ r, depth), :])

    heads = query.shape[1] // HD
    query = query.astype(jnp.bfloat16)
    stacked = jnp.concatenate([query[:, h * HD : (h + 1) * HD] for h in range(heads)], axis=0)
    order = head_major((rows * heads, rows * heads), pages, per_page, heads)
    body = rows * heads
    out_ref[:body] = dot(order, stacked).astype(jnp.bfloat16)
    keyval = keyval.astype(jnp.bfloat16)
    columns = keyval.shape[1]
    if columns < LANES:
        pad = jnp.zeros((rows, LANES - columns), jnp.bfloat16)
        keyval = jnp.concatenate([keyval, pad], axis=1)
    for v in range(keyval.shape[1] // LANES):
        out_ref[body + v * rows : body + (v + 1) * rows] = keyval[:, v * LANES : (v + 1) * LANES]


def attend_kernel(pages, page_rows, split, meta_ref, q_ref, k_ref, v_ref, reward_ref, *rest):
    outs, (spread, product) = rest[:-2], rest[-2:]
    width = k_ref.shape[1]
    span = KVH * page_rows
    body = pages * page_rows
    first = lax.axis_index("tensor") * width
    me = lax.axis_index("tensor") if len(outs) > 1 else 0
    spread[...] = jnp.zeros_like(spread)
    for i in range(pages):
        for r in range(KVH):
            spread[r * page_rows : (r + 1) * page_rows, aligned(me ^ r, HD)] = q_ref[
                r, i * page_rows : (i + 1) * page_rows, :
            ]
        scores = dot(k_ref[meta_ref[i]], spread[...], NT) * SCALE
        valid = first + iota((width, span), 0) < meta_ref[pages + i]
        scores = jnp.where(valid, scores, NEG)
        top = jnp.max(scores, axis=0, keepdims=True)
        expo = jnp.where(valid, jnp.exp(scores - top), 0.0)
        total = jnp.sum(expo, axis=0, keepdims=True)
        product[...] = dot(expo.astype(jnp.bfloat16), v_ref[meta_ref[i]], TN)
        for r in range(KVH):
            out = outs[r] if len(outs) > 1 else outs[0].at[r]
            out[i * page_rows : (i + 1) * page_rows, :] = product[
                r * page_rows : (r + 1) * page_rows, aligned(me ^ r, HD)
            ]
            lane = (r * page_rows) // LANES * LANES
            out[body + i : body + i + 1, :] = top[:, lane : lane + LANES]
            out[body + pages + i : body + pages + i + 1, :] = total[:, lane : lane + LANES]
    for r in range(KVH):
        if len(outs) > 1:
            outs[r][body + EXT :, :] = reward_ref[me ^ r]
        else:
            outs[0][r, body + EXT :, :] = jnp.zeros((EXT, LANES), jnp.float32)


def merge_kernel(pages, per_page, width, span, slots, chunks, q_ref, gathered_ref, w_ref, *rest):
    att = rest[-1]
    split = len(rest) > 3
    parts = rest[:chunks] if split else [rest[0].at[b] for b in range(chunks)]
    outs = rest[chunks:-1] if split else rest[1:-1]
    me = lax.axis_index("tensor")
    body = parts[0].shape[0] - 2 * EXT
    page_rows = body // pages
    heads = page_rows // per_page
    rows = pages * per_page

    kv_head = lax.div(me * heads, heads * chunks // KVH)
    if split:
        pieces = (gathered_ref.shape[1] - body) // rows

        def fresh_of(column):
            source = lax.div(column, pieces) ^ me
            start = pl.multiple_of(body + lax.rem(column, pieces) * rows, rows)
            return gathered_ref[source, pl.ds(start, rows), :]

        fresh_k, fresh_v = fresh_of(kv_head), fresh_of(KVH + kv_head)
    else:
        fresh_k, fresh_v = gathered_ref[kv_head], gathered_ref[KVH + kv_head]

    query = q_ref[:body, :]
    recent = dot(query, fresh_k, NT) * SCALE
    line, col = iota(recent.shape, 0), iota(recent.shape, 1)
    mine = (line // page_rows) * per_page + line % per_page
    seen = (mine // STEPS == col // STEPS) & (col <= mine)
    recent = jnp.where(seen, recent, NEG)
    recent_max = jnp.max(recent, axis=-1, keepdims=True)
    recent_exp = jnp.where(seen, jnp.exp(recent - recent_max), 0.0)
    recent_total = jnp.sum(recent_exp, axis=-1, keepdims=True)
    recent_acc = dot(recent_exp.astype(jnp.bfloat16), fresh_v)

    extras = []
    for b in range(chunks):
        extra = parts[b][body : body + EXT, :]
        if split:
            shift = -(b * page_rows) % LANES
            extras.append(pltpu.roll(extra, shift, 1) if shift else extra)
        else:
            shift = lax.rem(LANES - lax.rem(me * page_rows, LANES), LANES)
            extras.append(pltpu.roll(extra, shift, 1))
    maxima = [extra[:pages] for extra in extras]
    totals = [extra[pages : 2 * pages] for extra in extras]
    top = functools.reduce(jnp.maximum, maxima)
    factors = [jnp.exp(m - top) for m in maxima]
    total = functools.reduce(jnp.add, [f * t for f, t in zip(factors, totals)])

    pick = iota((page_rows, LANES), 0) == iota((page_rows, LANES), 1)

    def column(packed):
        return jnp.concatenate(
            [
                jnp.sum(
                    jnp.where(pick, jnp.broadcast_to(packed[i : i + 1], pick.shape), 0.0),
                    axis=-1,
                    keepdims=True,
                )
                for i in range(pages)
            ],
            axis=0,
        )

    acc = jnp.zeros((body, HD), jnp.float32)
    for b in range(chunks):
        acc = acc + column(factors[b]) * parts[b][:body, :]
    cache_top, cache_total = column(top), column(total)
    top = jnp.maximum(cache_top, recent_max)
    cache_factor = jnp.exp(cache_top - top)
    recent_factor = jnp.exp(recent_max - top)
    total = cache_factor * cache_total + recent_factor * recent_total
    acc = cache_factor * acc + recent_factor * recent_acc
    attended = (acc / total).astype(jnp.bfloat16)
    order = head_major((body, body), pages, per_page, heads)
    attended = dot(order, attended, TN).astype(jnp.bfloat16)
    for h in range(heads):
        att[:, h * HD : (h + 1) * HD] = attended[h * rows : (h + 1) * rows]

    tile = functools.reduce(jnp.add, [parts[b][body + EXT :, :] for b in range(chunks)])
    used = EXT // 2
    value = tile[used:] * lax.rsqrt(tile[:used] / width + EPS)
    mean = jnp.sum(value, keepdims=True) / span
    own = lax.div(me * (slots * span // chunks), span)
    mean = jnp.where(iota((EXT, LANES), 0) == own, mean, 0.0)

    part = w_ref.shape[1] // chunks
    for r in range(chunks):
        out = outs[r] if split else outs[0].at[me ^ r]
        product = dot(att[...], w_ref[:, aligned(me ^ r, part)])
        for c in range(part // LANES):
            out[c * rows : (c + 1) * rows, :] = product[:, c * LANES : (c + 1) * LANES]
        out[out.shape[0] - EXT :, :] = mean


def sum_kernel(rows, *refs):
    parts, (out_ref, reward_ref) = refs[:-2], refs[-2:]
    if len(parts) == 1:
        parts = [parts[0].at[b] for b in range(parts[0].shape[0])]
    total = parts[0][...]
    for part in parts[1:]:
        total = total + part[...]
    for c in range(out_ref.shape[1] // LANES):
        out_ref[:, c * LANES : (c + 1) * LANES] = total[c * rows : (c + 1) * rows].astype(
            jnp.bfloat16
        )
    reward_ref[...] = total[total.shape[0] - EXT :]


def partner(x, chunks, bits):
    return lax.ppermute(x, "tensor", [(i, i ^ bits) for i in range(chunks)])


def spread_all(x, chunks, index, tie=None):
    if chunks != KVH:
        every = lax.all_to_all(jnp.broadcast_to(x[None], (chunks,) + x.shape), "tensor", 0, 0, tiled=True)
        return jnp.take(every, index ^ jnp.arange(chunks), axis=0), x
    pair = jnp.stack([x, partner(x, chunks, 1)])
    if tie is not None:
        pair, tie = lax.optimization_barrier((pair, tie))
    others = [partner(pair, chunks, bits) for bits in (2, 4, 6)]
    return jnp.stack([pair] + others).reshape((chunks,) + x.shape), pair


def trade(blocks, chunks):
    if len(blocks) == 1:
        return [lax.all_to_all(blocks[0], "tensor", 0, 0, tiled=True)]
    traded = {bits: partner(blocks[bits], chunks, bits) for bits in (4, 5, 6, 7, 2, 3, 1)}
    return [blocks[0]] + [traded[bits] for bits in range(1, chunks)]


def local(
    chunks,
    reward_hidden,
    reward_gain,
    reward_head,
    decode_inputs,
    attn_gain,
    w_query,
    w_keyval,
    w_out,
    cache_keys,
    cache_values,
    lengths,
    slot_map,
):
    slots, width = cache_keys.shape[:2]
    depth, qcols = w_query.shape
    kvcols = w_keyval.shape[1]
    part = decode_inputs.shape[-1]
    heads = qcols // HD
    group = heads * chunks // KVH
    split = group // heads
    pages = slots // PAIR
    per_page = PAIR * STEPS
    page_rows = per_page * group
    rows = slots * STEPS
    body = rows * heads
    index = lax.axis_index("tensor")
    swap = [(0, 1), (1, 0)]
    direct = chunks == KVH

    meta, take, give = pl.pallas_call(
        functools.partial(plan_kernel, slots, STEPS),
        in_specs=[SMEM, SMEM] + [ANY] * 3,
        out_specs=[SMEM, VMEM, VMEM],
        out_shape=(
            jax.ShapeDtypeStruct((2 * pages,), jnp.int32),
            jax.ShapeDtypeStruct((rows, 2 * rows), jnp.bfloat16),
            jax.ShapeDtypeStruct((rows, 2 * rows), jnp.bfloat16),
        ),
        scratch_shapes=[
            pltpu.SMEM(slot_map.shape, jnp.int32),
            pltpu.SMEM(slot_map.shape, jnp.int32),
        ],
        compiler_params=pltpu.CompilerParams(vmem_limit_bytes=42 * MIB),
        cost_estimate=pl.CostEstimate(flops=0, bytes_accessed=1000, transcendentals=0),
        name="plan",
    )(slot_map, lengths, w_out, w_out, w_out)

    own, _ = spread_all(decode_inputs.reshape(rows, part), chunks, index, take)
    far = lax.ppermute(own, "dp", swap)

    pieces = max(kvcols // LANES, 1)
    packed_rows = body + pieces * rows
    packed = pl.pallas_call(
        functools.partial(project_kernel, pages, per_page, depth),
        in_specs=[VMEM] * 6,
        out_specs=VMEM,
        out_shape=jax.ShapeDtypeStruct((packed_rows, LANES), jnp.bfloat16),
        scratch_shapes=[
            pltpu.VMEM((chunks, rows, part), jnp.bfloat16),
        ],
        compiler_params=pltpu.CompilerParams(vmem_limit_bytes=4 * MIB),
        cost_estimate=pl.CostEstimate(
            flops=2 * rows * depth * (qcols + kvcols),
            bytes_accessed=2 * depth * (qcols + kvcols),
            transcendentals=0,
        ),
        name="project",
    )(own, far, take, attn_gain.reshape(chunks, 1, part), w_query, w_keyval)
    gathered, after = spread_all(packed, chunks, index)

    span = reward_hidden.shape[1]
    tiled = direct and slots == chunks
    reward_parts = pl.pallas_call(
        reward_kernel,
        in_specs=[ANY, ANY, VMEM, VMEM] + [ANY] * 0,
        out_specs=VMEM,
        out_shape=jax.ShapeDtypeStruct(
            (slots, EXT, LANES) if tiled else (2 * slots, span), jnp.float32
        ),
        scratch_shapes=[
            pltpu.VMEM(reward_hidden.shape, reward_hidden.dtype),
            pltpu.SemaphoreType.DMA((slots,)),
        ],
        compiler_params=pltpu.CompilerParams(vmem_limit_bytes=8 * MIB),
        cost_estimate=pl.CostEstimate(
            flops=4 * reward_hidden.size,
            bytes_accessed=2 * reward_hidden.size,
            transcendentals=0,
        ),
        name="reward",
    )(after, reward_hidden, reward_gain[None], reward_head[None])

    def tile(values):
        values = values.reshape(chunks, -1)
        size = EXT // 2 * LANES
        return jnp.pad(values, ((0, 0), (0, size - values.shape[1]))).reshape(
            chunks, EXT // 2, LANES
        )

    if not tiled:
        reward_parts = jnp.concatenate(
            [tile(reward_parts[:slots]), tile(reward_parts[slots:])], axis=1
        )
    fresh = gathered
    if not direct:
        fresh = jnp.take(gathered[:, body:, :kvcols], index ^ jnp.arange(chunks), axis=0)
        fresh = fresh.transpose(1, 0, 2).reshape(rows, 2 * KVH, HD).transpose(1, 0, 2)
    queries = gathered
    if not direct:
        queries = (
            jnp.take(gathered[:, :body], index ^ jnp.arange(chunks), axis=0)
            .reshape(KVH, split, pages, heads * per_page, HD)
            .transpose(0, 2, 1, 3, 4)
            .reshape(KVH, pages * page_rows, HD)
        )

    big = pages * page_rows
    block = (big + 2 * EXT, HD)
    attended = pl.pallas_call(
        functools.partial(attend_kernel, pages, page_rows, split),
        in_specs=[SMEM] + [VMEM] * 4,
        out_specs=[VMEM] * (KVH if direct else 1),
        out_shape=(
            [jax.ShapeDtypeStruct(block, jnp.float32)] * KVH
            if direct
            else [jax.ShapeDtypeStruct((KVH,) + block, jnp.float32)]
        ),
        scratch_shapes=[
            pltpu.VMEM((KVH * page_rows, KVH * HD), jnp.bfloat16),
            pltpu.VMEM((KVH * page_rows, KVH * HD), jnp.float32),
        ],
        compiler_params=pltpu.CompilerParams(vmem_limit_bytes=6 * MIB),
        cost_estimate=pl.CostEstimate(
            flops=4 * pages * width * KVH * HD * KVH * page_rows,
            bytes_accessed=4 * pages * width * KVH * HD,
            transcendentals=pages * width * KVH * page_rows,
        ),
        name="attend",
    )(meta, queries, cache_keys, cache_values, reward_parts)
    if not direct:
        acc = (
            attended[0][:, :big]
            .reshape(KVH, pages, split, heads * per_page, HD)
            .transpose(0, 2, 1, 3, 4)
            .reshape(chunks, body, HD)
        )
        extra = jnp.repeat(attended[0][:, big : big + EXT], split, axis=0)
        attended = [jnp.concatenate([acc, extra, reward_parts], axis=1)]
    parts = trade(attended, chunks)

    chunk_rows = part // LANES * rows + EXT
    partial = pl.pallas_call(
        functools.partial(merge_kernel, pages, per_page, depth, span, slots, chunks),
        in_specs=[VMEM] * (3 + len(parts)),
        out_specs=[VMEM] * len(parts),
        out_shape=(
            [jax.ShapeDtypeStruct((chunk_rows, LANES), jnp.float32)] * chunks
            if direct
            else [jax.ShapeDtypeStruct((chunks, chunk_rows, LANES), jnp.float32)]
        ),
        scratch_shapes=[pltpu.VMEM((rows, qcols), jnp.bfloat16)],
        compiler_params=pltpu.CompilerParams(vmem_limit_bytes=8 * MIB),
        cost_estimate=pl.CostEstimate(
            flops=2 * rows * qcols * depth, bytes_accessed=2 * qcols * depth, transcendentals=0
        ),
        name="merge",
    )(packed, fresh, w_out, *parts)
    partial = trade(partial, chunks)

    decoded, reward = pl.pallas_call(
        functools.partial(sum_kernel, rows),
        out_shape=(
            jax.ShapeDtypeStruct((rows, part), jnp.bfloat16),
            jax.ShapeDtypeStruct((EXT, LANES), jnp.float32),
        ),
        compiler_params=pltpu.CompilerParams(vmem_limit_bytes=8 * MIB),
        name="total",
    )(*partial)
    far = lax.ppermute(decoded, "dp", swap)
    decoded = dot(give, jnp.concatenate([decoded, far], axis=0)).astype(jnp.bfloat16)
    return (reward[:slots, 0], decoded.reshape(STEPS, slots, part))


def solution(mesh):
    return jax.shard_map(
        functools.partial(local, mesh.shape["tensor"]),
        mesh=mesh,
        in_specs=(
            P(("groups", "dp"), None, "tensor"),
            P("tensor"),
            P("tensor"),
            P(None, ("groups", "dp"), "tensor"),
            P(),
            P(None, "tensor"),
            P(None, "tensor"),
            P("tensor", None),
            P(("groups", "dp"), "tensor", None),
            P(("groups", "dp"), "tensor", None),
            P("groups"),
            P("groups"),
        ),
        out_specs=(P(("groups", "dp")), P(None, ("groups", "dp"), "tensor")),
        check_vma=False,
    )
```

```python
import functools

import jax
import jax.numpy as jnp
from jax import lax
from jax.experimental import pallas as pl
from jax.experimental.pallas import tpu as pltpu
from jax.sharding import PartitionSpec as P

HD = 128
KVH = 8
STEPS = 2
PAIR = 2
LANES = 128
EXT = 8
EPS = 1e-05
NEG = -1e30
SCALE = HD ** (-0.5)
NT = (((1,), (1,)), ((), ()))
TN = (((0,), (0,)), ((), ()))
MIB = 1 << 20
ANY = pl.BlockSpec(memory_space=pl.ANY)
VMEM = pl.BlockSpec(memory_space=pltpu.VMEM)
SMEM = pl.BlockSpec(memory_space=pltpu.SMEM)


def iota(shape, dim):
    return lax.broadcasted_iota(jnp.int32, shape, dim)


def dot(a, b, dims=(((1,), (0,)), ((), ()))):
    return lax.dot_general(a, b, dims, preferred_element_type=jnp.float32)


def head_major(shape, pages, per_page, heads):
    o, s = iota(shape, 0), iota(shape, 1)
    row = o % per_page
    head = (o // per_page) % heads
    page = o // (per_page * heads)
    return (s == (head * pages + page) * per_page + row).astype(jnp.bfloat16)


def aligned(index, size):
    return pl.ds(pl.multiple_of(index * size, size), size)


def early_kernel(*refs):
    refs[-1][...] = jnp.zeros_like(refs[-1])


def plan_kernel(slots, steps, map_ref, length_ref, meta_ref, take_ref, give_ref, before_ref, place_ref):
    count = map_ref.shape[0]
    mine = lax.axis_index("dp")
    base = mine * slots
    for block in range(count // slots):
        found = jnp.int32(0)
        for s in range(block * slots, (block + 1) * slots):
            before_ref[s] = found
            found = found + (map_ref[s] == s).astype(jnp.int32)
    for s in range(slots):
        own = map_ref[base + s] == base + s

        @pl.when(own)
        def _():
            slot = before_ref[base + s]
            meta_ref[slot] = jnp.int32(s)
            meta_ref[slots // PAIR + slot] = length_ref[base + s]

    for r in range(count):
        source = map_ref[r]
        place_ref[r] = (
            lax.div(source, slots) * slots
            + PAIR * before_ref[source]
            + (source != r).astype(jnp.int32)
        )
    rows = slots * steps
    line, col = iota((rows, 2 * rows), 0), iota((rows, 2 * rows), 1)
    same = line % steps == (col // slots) % steps
    take = jnp.zeros((rows, 2 * rows), jnp.bool_)
    give = jnp.zeros((rows, 2 * rows), jnp.bool_)
    for side in range(2):
        start = base if side == 0 else (1 - mine) * slots
        for s in range(slots):
            target = place_ref[start + s] - base
            column = (col // rows == side) & (col % slots == s)
            take = take | (same & column & (line // steps == target))
    for s in range(slots):
        place = place_ref[base + s]
        far = (lax.div(place, slots) != mine).astype(jnp.int32)
        target = far * rows + lax.rem(place, slots) * steps
        give = give | ((line % slots == s) & (col == line // slots + target))
    take_ref[...] = take.astype(jnp.float32).astype(jnp.bfloat16)
    give_ref[...] = give.astype(jnp.float32).astype(jnp.bfloat16)


def reward_kernel(after_ref, hidden_ref, gain_ref, head_ref, *rest):
    out_ref, buffer, sems = rest[-3:]
    slots = hidden_ref.shape[0]
    loads = [
        pltpu.make_async_copy(hidden_ref.at[s], buffer.at[s], sems.at[s]) for s in range(slots)
    ]
    for load in loads:
        load.start()
    weight = gain_ref[...] * head_ref[...]
    for s in range(slots):
        loads[s].wait()
        hidden = buffer[s].astype(jnp.float32)
        for half, value in enumerate((hidden * hidden, hidden * weight)):
            sums = jnp.sum(value, axis=-1)
            if len(out_ref.shape) == 2:
                out_ref[half * slots + s] = sums
                continue
            for c in range(EXT // 2):
                piece = jnp.zeros((LANES,), jnp.float32)
                if c < sums.shape[0] // LANES:
                    piece = sums[c * LANES : (c + 1) * LANES]
                out_ref[s, half * (EXT // 2) + c] = piece


def project_kernel(pages, per_page, width, after_ref, own_ref, far_ref, take_ref, gain_ref, wq_ref, wkv_ref, out_ref, tokens):
    me = lax.axis_index("tensor")
    chunks, rows, depth = own_ref.shape
    total = jnp.zeros((rows, depth), jnp.float32)
    for r in range(chunks):
        both = jnp.concatenate([own_ref[r], far_ref[r]], axis=0)
        part = dot(take_ref[...], both)
        tokens[r] = part.astype(jnp.bfloat16)
        total = total + part * part
    inv = lax.rsqrt(jnp.sum(total, axis=-1, keepdims=True) / width + EPS)

    query = jnp.zeros((rows, wq_ref.shape[1]), jnp.float32)
    keyval = jnp.zeros((rows, wkv_ref.shape[1]), jnp.float32)
    for r in range(chunks):
        normed = (tokens[r].astype(jnp.float32) * inv * gain_ref[me ^ r]).astype(jnp.bfloat16)
        query = query + dot(normed, wq_ref[aligned(me ^ r, depth), :])
        keyval = keyval + dot(normed, wkv_ref[aligned(me ^ r, depth), :])

    heads = query.shape[1] // HD
    query = query.astype(jnp.bfloat16)
    stacked = jnp.concatenate([query[:, h * HD : (h + 1) * HD] for h in range(heads)], axis=0)
    order = head_major((rows * heads, rows * heads), pages, per_page, heads)
    body = rows * heads
    out_ref[:body] = dot(order, stacked).astype(jnp.bfloat16)
    keyval = keyval.astype(jnp.bfloat16)
    columns = keyval.shape[1]
    if columns < LANES:
        pad = jnp.zeros((rows, LANES - columns), jnp.bfloat16)
        keyval = jnp.concatenate([keyval, pad], axis=1)
    for v in range(keyval.shape[1] // LANES):
        out_ref[body + v * rows : body + (v + 1) * rows] = keyval[:, v * LANES : (v + 1) * LANES]


def attend_kernel(pages, page_rows, meta_ref, q_ref, k_ref, v_ref, reward_ref, *rest):
    outs, (spread, product) = rest[:-2], rest[-2:]
    width = k_ref.shape[1]
    span = KVH * page_rows
    body = pages * page_rows
    first = lax.axis_index("tensor") * width
    me = lax.axis_index("tensor") if len(outs) > 1 else 0
    spread[...] = jnp.zeros_like(spread)
    for i in range(pages):
        for r in range(KVH):
            spread[r * page_rows : (r + 1) * page_rows, aligned(me ^ r, HD)] = q_ref[
                r, i * page_rows : (i + 1) * page_rows, :
            ]
        scores = dot(k_ref[meta_ref[i]], spread[...], NT) * SCALE
        valid = first + iota((width, span), 0) < meta_ref[pages + i]
        scores = jnp.where(valid, scores, NEG)
        top = jnp.max(scores, axis=0, keepdims=True)
        expo = jnp.where(valid, jnp.exp(scores - top), 0.0)
        total = jnp.sum(expo, axis=0, keepdims=True)
        product[...] = dot(expo.astype(jnp.bfloat16), v_ref[meta_ref[i]], TN)
        for r in range(KVH):
            out = outs[r] if len(outs) > 1 else outs[0].at[r]
            out[i * page_rows : (i + 1) * page_rows, :] = product[
                r * page_rows : (r + 1) * page_rows, aligned(me ^ r, HD)
            ]
            lane = (r * page_rows) // LANES * LANES
            out[body + i : body + i + 1, :] = top[:, lane : lane + LANES]
            out[body + pages + i : body + pages + i + 1, :] = total[:, lane : lane + LANES]
    for r in range(KVH):
        if len(outs) > 1:
            outs[r][body + EXT :, :] = reward_ref[me ^ r]
        else:
            outs[0][r, body + EXT :, :] = jnp.zeros((EXT, LANES), jnp.float32)


def merge_kernel(pages, per_page, width, span, slots, chunks, q_ref, gathered_ref, w_ref, *rest):
    att = rest[-1]
    split = len(rest) > 3
    parts = rest[:chunks] if split else [rest[0].at[b] for b in range(chunks)]
    outs = rest[chunks:-1] if split else rest[1:-1]
    me = lax.axis_index("tensor")
    body = parts[0].shape[0] - 2 * EXT
    page_rows = body // pages
    heads = page_rows // per_page
    rows = pages * per_page

    kv_head = lax.div(me * heads, heads * chunks // KVH)
    if split:
        pieces = (gathered_ref.shape[1] - body) // rows

        def fresh_of(column):
            source = lax.div(column, pieces) ^ me
            start = pl.multiple_of(body + lax.rem(column, pieces) * rows, rows)
            return gathered_ref[source, pl.ds(start, rows), :]

        fresh_k, fresh_v = fresh_of(kv_head), fresh_of(KVH + kv_head)
    else:
        fresh_k, fresh_v = gathered_ref[kv_head], gathered_ref[KVH + kv_head]

    query = q_ref[:body, :]
    recent = dot(query, fresh_k, NT) * SCALE
    line, col = iota(recent.shape, 0), iota(recent.shape, 1)
    mine = (line // page_rows) * per_page + line % per_page
    seen = (mine // STEPS == col // STEPS) & (col <= mine)
    recent = jnp.where(seen, recent, NEG)
    recent_max = jnp.max(recent, axis=-1, keepdims=True)
    recent_exp = jnp.where(seen, jnp.exp(recent - recent_max), 0.0)
    recent_total = jnp.sum(recent_exp, axis=-1, keepdims=True)
    recent_acc = dot(recent_exp.astype(jnp.bfloat16), fresh_v)

    extras = []
    for b in range(chunks):
        extra = parts[b][body : body + EXT, :]
        if split:
            shift = -(b * page_rows) % LANES
            extras.append(pltpu.roll(extra, shift, 1) if shift else extra)
        else:
            shift = lax.rem(LANES - lax.rem(me * page_rows, LANES), LANES)
            extras.append(pltpu.roll(extra, shift, 1))
    maxima = [extra[:pages] for extra in extras]
    totals = [extra[pages : 2 * pages] for extra in extras]
    top = functools.reduce(jnp.maximum, maxima)
    factors = [jnp.exp(m - top) for m in maxima]
    total = functools.reduce(jnp.add, [f * t for f, t in zip(factors, totals)])

    pick = iota((page_rows, LANES), 0) == iota((page_rows, LANES), 1)

    def column(packed):
        return jnp.concatenate(
            [
                jnp.sum(
                    jnp.where(pick, jnp.broadcast_to(packed[i : i + 1], pick.shape), 0.0),
                    axis=-1,
                    keepdims=True,
                )
                for i in range(pages)
            ],
            axis=0,
        )

    acc = jnp.zeros((body, HD), jnp.float32)
    for b in range(chunks):
        acc = acc + column(factors[b]) * parts[b][:body, :]
    cache_top, cache_total = column(top), column(total)
    top = jnp.maximum(cache_top, recent_max)
    cache_factor = jnp.exp(cache_top - top)
    recent_factor = jnp.exp(recent_max - top)
    total = cache_factor * cache_total + recent_factor * recent_total
    acc = cache_factor * acc + recent_factor * recent_acc
    attended = (acc / total).astype(jnp.bfloat16)
    order = head_major((body, body), pages, per_page, heads)
    attended = dot(order, attended, TN).astype(jnp.bfloat16)
    for h in range(heads):
        att[:, h * HD : (h + 1) * HD] = attended[h * rows : (h + 1) * rows]

    tile = functools.reduce(jnp.add, [parts[b][body + EXT :, :] for b in range(chunks)])
    used = EXT // 2
    value = tile[used:] * lax.rsqrt(tile[:used] / width + EPS)
    mean = jnp.sum(value, keepdims=True) / span
    own = lax.div(me * (slots * span // chunks), span)
    mean = jnp.where(iota((EXT, LANES), 0) == own, mean, 0.0)

    part = w_ref.shape[1] // chunks
    for r in range(chunks):
        out = outs[r] if split else outs[0].at[me ^ r]
        product = dot(att[...], w_ref[:, aligned(me ^ r, part)])
        for c in range(part // LANES):
            out[c * rows : (c + 1) * rows, :] = product[:, c * LANES : (c + 1) * LANES]
        out[out.shape[0] - EXT :, :] = mean


def sum_kernel(rows, *refs):
    parts, (out_ref, reward_ref) = refs[:-2], refs[-2:]
    if len(parts) == 1:
        parts = [parts[0].at[b] for b in range(parts[0].shape[0])]
    total = parts[0][...]
    for part in parts[1:]:
        total = total + part[...]
    for c in range(out_ref.shape[1] // LANES):
        out_ref[:, c * LANES : (c + 1) * LANES] = total[c * rows : (c + 1) * rows].astype(
            jnp.bfloat16
        )
    reward_ref[...] = total[total.shape[0] - EXT :]


def partner(x, chunks, bits):
    return lax.ppermute(x, "tensor", [(i, i ^ bits) for i in range(chunks)])


def spread_all(x, chunks, index, tie=None):
    if chunks != KVH:
        every = lax.all_to_all(jnp.broadcast_to(x[None], (chunks,) + x.shape), "tensor", 0, 0, tiled=True)
        return jnp.take(every, index ^ jnp.arange(chunks), axis=0), x
    pair = jnp.stack([x, partner(x, chunks, 1)])
    if tie is not None:
        pair, tie = lax.optimization_barrier((pair, tie))
        after = tie
    else:
        after = pair
    others = [partner(pair, chunks, bits) for bits in (2, 4, 6)]
    return jnp.stack([pair] + others).reshape((chunks,) + x.shape), after


def trade(blocks, chunks):
    if len(blocks) == 1:
        return [lax.all_to_all(blocks[0], "tensor", 0, 0, tiled=True)]
    traded = {bits: partner(blocks[bits], chunks, bits) for bits in (6, 1, 7, 2, 5, 3, 4)}
    return [blocks[0]] + [traded[bits] for bits in range(1, chunks)]


def local(
    chunks,
    reward_hidden,
    reward_gain,
    reward_head,
    decode_inputs,
    attn_gain,
    w_query,
    w_keyval,
    w_out,
    cache_keys,
    cache_values,
    lengths,
    slot_map,
):
    slots, width = cache_keys.shape[:2]
    depth, qcols = w_query.shape
    kvcols = w_keyval.shape[1]
    part = decode_inputs.shape[-1]
    heads = qcols // HD
    group = heads * chunks // KVH
    split = group // heads
    pages = slots // PAIR
    per_page = PAIR * STEPS
    page_rows = per_page * group
    rows = slots * STEPS
    body = rows * heads
    index = lax.axis_index("tensor")
    swap = [(0, 1), (1, 0)]
    direct = chunks == KVH

    meta, take, give = pl.pallas_call(
        functools.partial(plan_kernel, slots, STEPS),
        in_specs=[SMEM, SMEM],
        out_specs=[SMEM, VMEM, VMEM],
        out_shape=(
            jax.ShapeDtypeStruct((2 * pages,), jnp.int32),
            jax.ShapeDtypeStruct((rows, 2 * rows), jnp.bfloat16),
            jax.ShapeDtypeStruct((rows, 2 * rows), jnp.bfloat16),
        ),
        scratch_shapes=[
            pltpu.SMEM(slot_map.shape, jnp.int32),
            pltpu.SMEM(slot_map.shape, jnp.int32),
        ],
        compiler_params=pltpu.CompilerParams(vmem_limit_bytes=MIB),
        name="plan",
    )(slot_map, lengths)

    early = pl.pallas_call(
        early_kernel,
        in_specs=[ANY] * 3,
        out_specs=VMEM,
        out_shape=jax.ShapeDtypeStruct((EXT, LANES), jnp.float32),
        compiler_params=pltpu.CompilerParams(vmem_limit_bytes=38 * MIB),
        name="early",
    )(w_out, w_out, w_out)
    own, after = spread_all(decode_inputs.reshape(rows, part), chunks, index, early)
    far = lax.ppermute(own, "dp", swap)

    pieces = max(kvcols // LANES, 1)
    packed_rows = body + pieces * rows
    packed = pl.pallas_call(
        functools.partial(project_kernel, pages, per_page, depth),
        in_specs=[ANY] + [VMEM] * 6,
        out_specs=VMEM,
        out_shape=jax.ShapeDtypeStruct((packed_rows, LANES), jnp.bfloat16),
        scratch_shapes=[
            pltpu.VMEM((chunks, rows, part), jnp.bfloat16),
        ],
        compiler_params=pltpu.CompilerParams(vmem_limit_bytes=4 * MIB),
        cost_estimate=pl.CostEstimate(
            flops=2 * rows * depth * (qcols + kvcols),
            bytes_accessed=2 * depth * (qcols + kvcols),
            transcendentals=0,
        ),
        name="project",
    )(after, own, far, take, attn_gain.reshape(chunks, 1, part), w_query, w_keyval)
    gathered, after = spread_all(packed, chunks, index)

    span = reward_hidden.shape[1]
    tiled = direct and slots == chunks
    reward_parts = pl.pallas_call(
        reward_kernel,
        in_specs=[ANY, ANY, VMEM, VMEM] + [ANY] * 0,
        out_specs=VMEM,
        out_shape=jax.ShapeDtypeStruct(
            (slots, EXT, LANES) if tiled else (2 * slots, span), jnp.float32
        ),
        scratch_shapes=[
            pltpu.VMEM(reward_hidden.shape, reward_hidden.dtype),
            pltpu.SemaphoreType.DMA((slots,)),
        ],
        compiler_params=pltpu.CompilerParams(vmem_limit_bytes=8 * MIB),
        cost_estimate=pl.CostEstimate(
            flops=4 * reward_hidden.size,
            bytes_accessed=2 * reward_hidden.size,
            transcendentals=0,
        ),
        name="reward",
    )(after, reward_hidden, reward_gain[None], reward_head[None])

    def tile(values):
        values = values.reshape(chunks, -1)
        size = EXT // 2 * LANES
        return jnp.pad(values, ((0, 0), (0, size - values.shape[1]))).reshape(
            chunks, EXT // 2, LANES
        )

    if not tiled:
        reward_parts = jnp.concatenate(
            [tile(reward_parts[:slots]), tile(reward_parts[slots:])], axis=1
        )
    fresh = gathered
    if not direct:
        fresh = jnp.take(gathered[:, body:, :kvcols], index ^ jnp.arange(chunks), axis=0)
        fresh = fresh.transpose(1, 0, 2).reshape(rows, 2 * KVH, HD).transpose(1, 0, 2)
    queries = gathered
    if not direct:
        queries = (
            jnp.take(gathered[:, :body], index ^ jnp.arange(chunks), axis=0)
            .reshape(KVH, split, pages, heads * per_page, HD)
            .transpose(0, 2, 1, 3, 4)
            .reshape(KVH, pages * page_rows, HD)
        )

    big = pages * page_rows
    block = (big + 2 * EXT, HD)
    attended = pl.pallas_call(
        functools.partial(attend_kernel, pages, page_rows),
        in_specs=[SMEM] + [VMEM] * 4,
        out_specs=[VMEM] * (KVH if direct else 1),
        out_shape=(
            [jax.ShapeDtypeStruct(block, jnp.float32)] * KVH
            if direct
            else [jax.ShapeDtypeStruct((KVH,) + block, jnp.float32)]
        ),
        scratch_shapes=[
            pltpu.VMEM((KVH * page_rows, KVH * HD), jnp.bfloat16),
            pltpu.VMEM((KVH * page_rows, KVH * HD), jnp.float32),
        ],
        compiler_params=pltpu.CompilerParams(vmem_limit_bytes=6 * MIB),
        cost_estimate=pl.CostEstimate(
            flops=4 * pages * width * KVH * HD * KVH * page_rows,
            bytes_accessed=4 * pages * width * KVH * HD,
            transcendentals=pages * width * KVH * page_rows,
        ),
        name="attend",
    )(meta, queries, cache_keys, cache_values, reward_parts)
    if not direct:
        acc = (
            attended[0][:, :big]
            .reshape(KVH, pages, split, heads * per_page, HD)
            .transpose(0, 2, 1, 3, 4)
            .reshape(chunks, body, HD)
        )
        extra = jnp.repeat(attended[0][:, big : big + EXT], split, axis=0)
        attended = [jnp.concatenate([acc, extra, reward_parts], axis=1)]
    parts = trade(attended, chunks)

    chunk_rows = part // LANES * rows + EXT
    partial = pl.pallas_call(
        functools.partial(merge_kernel, pages, per_page, depth, span, slots, chunks),
        in_specs=[VMEM] * (3 + len(parts)),
        out_specs=[VMEM] * len(parts),
        out_shape=(
            [jax.ShapeDtypeStruct((chunk_rows, LANES), jnp.float32)] * chunks
            if direct
            else [jax.ShapeDtypeStruct((chunks, chunk_rows, LANES), jnp.float32)]
        ),
        scratch_shapes=[pltpu.VMEM((rows, qcols), jnp.bfloat16)],
        compiler_params=pltpu.CompilerParams(vmem_limit_bytes=8 * MIB),
        cost_estimate=pl.CostEstimate(
            flops=2 * rows * qcols * depth, bytes_accessed=2 * qcols * depth, transcendentals=0
        ),
        name="merge",
    )(packed, fresh, w_out, *parts)
    partial = trade(partial, chunks)

    decoded, reward = pl.pallas_call(
        functools.partial(sum_kernel, rows),
        out_shape=(
            jax.ShapeDtypeStruct((rows, part), jnp.bfloat16),
            jax.ShapeDtypeStruct((EXT, LANES), jnp.float32),
        ),
        compiler_params=pltpu.CompilerParams(vmem_limit_bytes=8 * MIB),
        name="total",
    )(*partial)
    far = lax.ppermute(decoded, "dp", swap)
    decoded = dot(give, jnp.concatenate([decoded, far], axis=0)).astype(jnp.bfloat16)
    return (reward[:slots, 0], decoded.reshape(STEPS, slots, part))


def solution(mesh):
    return jax.shard_map(
        functools.partial(local, mesh.shape["tensor"]),
        mesh=mesh,
        in_specs=(
            P(("groups", "dp"), None, "tensor"),
            P("tensor"),
            P("tensor"),
            P(None, ("groups", "dp"), "tensor"),
            P(),
            P(None, "tensor"),
            P(None, "tensor"),
            P("tensor", None),
            P(("groups", "dp"), "tensor", None),
            P(("groups", "dp"), "tensor", None),
            P("groups"),
            P("groups"),
        ),
        out_specs=(P(("groups", "dp")), P(None, ("groups", "dp"), "tensor")),
        check_vma=False,
    )
```

```python
import functools

import jax
import jax.numpy as jnp
from jax import lax
from jax.experimental import pallas as pl
from jax.experimental.pallas import tpu as pltpu
from jax.sharding import PartitionSpec as P


HD = 128
KVH = 8
STEPS = 2
PAIR = 2
LANES = 128
EXT = 8
EPS = 1e-05
NEG = -1e30
SCALE = HD ** (-0.5)
NT = (((1,), (1,)), ((), ()))
TN = (((0,), (0,)), ((), ()))
MIB = 1 << 20
ANY = pl.BlockSpec(memory_space=pl.ANY)
VMEM = pl.BlockSpec(memory_space=pltpu.VMEM)
SMEM = pl.BlockSpec(memory_space=pltpu.SMEM)


def iota(shape, dim):
    return lax.broadcasted_iota(jnp.int32, shape, dim)


def dot(a, b, dims=(((1,), (0,)), ((), ()))):
    return lax.dot_general(a, b, dims, preferred_element_type=jnp.float32)


def head_major(shape, pages, per_page, heads):
    o, s = iota(shape, 0), iota(shape, 1)
    row = o % per_page
    head = (o // per_page) % heads
    page = o // (per_page * heads)
    return (s == (head * pages + page) * per_page + row).astype(jnp.bfloat16)


def aligned(index, size):
    return pl.ds(pl.multiple_of(index * size, size), size)


def early_kernel(*refs):
    refs[-1][...] = jnp.zeros_like(refs[-1])


def plan_kernel(slots, steps, map_ref, length_ref, meta_ref, take_ref, give_ref, before_ref, place_ref):
    count = map_ref.shape[0]
    mine = lax.axis_index("dp")
    base = mine * slots
    for block in range(count // slots):
        found = jnp.int32(0)
        for s in range(block * slots, (block + 1) * slots):
            before_ref[s] = found
            found = found + (map_ref[s] == s).astype(jnp.int32)
    for s in range(slots):
        own = map_ref[base + s] == base + s

        @pl.when(own)
        def _():
            slot = before_ref[base + s]
            meta_ref[slot] = jnp.int32(s)
            meta_ref[slots // PAIR + slot] = length_ref[base + s]

    for r in range(count):
        source = map_ref[r]
        place_ref[r] = (
            lax.div(source, slots) * slots
            + PAIR * before_ref[source]
            + (source != r).astype(jnp.int32)
        )
    rows = slots * steps
    line, col = iota((rows, 2 * rows), 0), iota((rows, 2 * rows), 1)
    same = line % steps == (col // slots) % steps
    take = jnp.zeros((rows, 2 * rows), jnp.bool_)
    give = jnp.zeros((rows, 2 * rows), jnp.bool_)
    for side in range(2):
        start = base if side == 0 else (1 - mine) * slots
        for s in range(slots):
            target = place_ref[start + s] - base
            column = (col // rows == side) & (col % slots == s)
            take = take | (same & column & (line // steps == target))
    for s in range(slots):
        place = place_ref[base + s]
        far = (lax.div(place, slots) != mine).astype(jnp.int32)
        target = far * rows + lax.rem(place, slots) * steps
        give = give | ((line % slots == s) & (col == line // slots + target))
    take_ref[...] = take.astype(jnp.float32).astype(jnp.bfloat16)
    give_ref[...] = give.astype(jnp.float32).astype(jnp.bfloat16)


def reward_kernel(after_ref, hidden_ref, gain_ref, head_ref, *rest):
    out_ref, buffer, sems = rest[-3:]
    slots = hidden_ref.shape[0]
    loads = [
        pltpu.make_async_copy(hidden_ref.at[s], buffer.at[s], sems.at[s]) for s in range(slots)
    ]
    for load in loads:
        load.start()
    weight = gain_ref[...] * head_ref[...]
    for s in range(slots):
        loads[s].wait()
        hidden = buffer[s].astype(jnp.float32)
        for half, value in enumerate((hidden * hidden, hidden * weight)):
            sums = jnp.sum(value, axis=-1)
            if len(out_ref.shape) == 2:
                out_ref[half * slots + s] = sums
                continue
            for c in range(EXT // 2):
                piece = jnp.zeros((LANES,), jnp.float32)
                if c < sums.shape[0] // LANES:
                    piece = sums[c * LANES : (c + 1) * LANES]
                out_ref[s, half * (EXT // 2) + c] = piece


def project_kernel(pages, per_page, width, after_ref, own_ref, far_ref, take_ref, gain_ref, wq_ref, wkv_ref, out_ref, tokens):
    me = lax.axis_index("tensor")
    chunks, rows, depth = own_ref.shape
    total = jnp.zeros((rows, depth), jnp.float32)
    for r in range(chunks):
        both = jnp.concatenate([own_ref[r], far_ref[r]], axis=0)
        part = dot(take_ref[...], both)
        tokens[r] = part.astype(jnp.bfloat16)
        total = total + part * part
    inv = lax.rsqrt(jnp.sum(total, axis=-1, keepdims=True) / width + EPS)

    query = jnp.zeros((rows, wq_ref.shape[1]), jnp.float32)
    keyval = jnp.zeros((rows, wkv_ref.shape[1]), jnp.float32)
    for r in range(chunks):
        normed = (tokens[r].astype(jnp.float32) * inv * gain_ref[me ^ r]).astype(jnp.bfloat16)
        query = query + dot(normed, wq_ref[aligned(me ^ r, depth), :])
        keyval = keyval + dot(normed, wkv_ref[aligned(me ^ r, depth), :])

    heads = query.shape[1] // HD
    query = query.astype(jnp.bfloat16)
    stacked = jnp.concatenate([query[:, h * HD : (h + 1) * HD] for h in range(heads)], axis=0)
    order = head_major((rows * heads, rows * heads), pages, per_page, heads)
    body = rows * heads
    out_ref[:body] = dot(order, stacked).astype(jnp.bfloat16)
    keyval = keyval.astype(jnp.bfloat16)
    columns = keyval.shape[1]
    if columns < LANES:
        pad = jnp.zeros((rows, LANES - columns), jnp.bfloat16)
        keyval = jnp.concatenate([keyval, pad], axis=1)
    for v in range(keyval.shape[1] // LANES):
        out_ref[body + v * rows : body + (v + 1) * rows] = keyval[:, v * LANES : (v + 1) * LANES]


def attend_kernel(pages, page_rows, meta_ref, q_ref, k_ref, v_ref, reward_ref, *rest):
    outs, (spread, product) = rest[:-2], rest[-2:]
    width = k_ref.shape[1]
    span = KVH * page_rows
    body = pages * page_rows
    first = lax.axis_index("tensor") * width
    me = lax.axis_index("tensor") if len(outs) > 1 else 0
    spread[...] = jnp.zeros_like(spread)
    for i in range(pages):
        for r in range(KVH):
            spread[r * page_rows : (r + 1) * page_rows, aligned(me ^ r, HD)] = q_ref[
                r, i * page_rows : (i + 1) * page_rows, :
            ]
        scores = dot(k_ref[meta_ref[i]], spread[...], NT) * SCALE
        valid = first + iota((width, span), 0) < meta_ref[pages + i]
        scores = jnp.where(valid, scores, NEG)
        top = jnp.max(scores, axis=0, keepdims=True)
        expo = jnp.where(valid, jnp.exp(scores - top), 0.0)
        total = jnp.sum(expo, axis=0, keepdims=True)
        product[...] = dot(expo.astype(jnp.bfloat16), v_ref[meta_ref[i]], TN)
        for r in range(KVH):
            out = outs[r] if len(outs) > 1 else outs[0].at[r]
            out[i * page_rows : (i + 1) * page_rows, :] = product[
                r * page_rows : (r + 1) * page_rows, aligned(me ^ r, HD)
            ]
            lane = (r * page_rows) // LANES * LANES
            out[body + i : body + i + 1, :] = top[:, lane : lane + LANES]
            out[body + pages + i : body + pages + i + 1, :] = total[:, lane : lane + LANES]
    for r in range(KVH):
        if len(outs) > 1:
            outs[r][body + EXT :, :] = reward_ref[me ^ r]
        else:
            outs[0][r, body + EXT :, :] = jnp.zeros((EXT, LANES), jnp.float32)


def merge_kernel(pages, per_page, width, span, slots, chunks, q_ref, gathered_ref, w_ref, *rest):
    att = rest[-1]
    split = len(rest) > 3
    parts = rest[:chunks] if split else [rest[0].at[b] for b in range(chunks)]
    outs = rest[chunks:-1] if split else rest[1:-1]
    me = lax.axis_index("tensor")
    body = parts[0].shape[0] - 2 * EXT
    page_rows = body // pages
    heads = page_rows // per_page
    rows = pages * per_page

    kv_head = lax.div(me * heads, heads * chunks // KVH)
    if split:
        pieces = (gathered_ref.shape[1] - body) // rows

        def fresh_of(column):
            source = lax.div(column, pieces) ^ me
            start = pl.multiple_of(body + lax.rem(column, pieces) * rows, rows)
            return gathered_ref[source, pl.ds(start, rows), :]

        fresh_k, fresh_v = fresh_of(kv_head), fresh_of(KVH + kv_head)
    else:
        fresh_k, fresh_v = gathered_ref[kv_head], gathered_ref[KVH + kv_head]

    query = q_ref[:body, :]
    recent = dot(query, fresh_k, NT) * SCALE
    line, col = iota(recent.shape, 0), iota(recent.shape, 1)
    mine = (line // page_rows) * per_page + line % per_page
    seen = (mine // STEPS == col // STEPS) & (col <= mine)
    recent = jnp.where(seen, recent, NEG)
    recent_max = jnp.max(recent, axis=-1, keepdims=True)
    recent_exp = jnp.where(seen, jnp.exp(recent - recent_max), 0.0)
    recent_total = jnp.sum(recent_exp, axis=-1, keepdims=True)
    recent_acc = dot(recent_exp.astype(jnp.bfloat16), fresh_v)

    extras = []
    for b in range(chunks):
        extra = parts[b][body : body + EXT, :]
        if split:
            shift = -(b * page_rows) % LANES
            extras.append(pltpu.roll(extra, shift, 1) if shift else extra)
        else:
            shift = lax.rem(LANES - lax.rem(me * page_rows, LANES), LANES)
            extras.append(pltpu.roll(extra, shift, 1))
    maxima = [extra[:pages] for extra in extras]
    totals = [extra[pages : 2 * pages] for extra in extras]
    top = functools.reduce(jnp.maximum, maxima)
    factors = [jnp.exp(m - top) for m in maxima]
    total = functools.reduce(jnp.add, [f * t for f, t in zip(factors, totals)])

    pick = iota((page_rows, LANES), 0) == iota((page_rows, LANES), 1)

    def column(packed):
        return jnp.concatenate(
            [
                jnp.sum(
                    jnp.where(pick, jnp.broadcast_to(packed[i : i + 1], pick.shape), 0.0),
                    axis=-1,
                    keepdims=True,
                )
                for i in range(pages)
            ],
            axis=0,
        )

    acc = jnp.zeros((body, HD), jnp.float32)
    for b in range(chunks):
        acc = acc + column(factors[b]) * parts[b][:body, :]
    cache_top, cache_total = column(top), column(total)
    top = jnp.maximum(cache_top, recent_max)
    cache_factor = jnp.exp(cache_top - top)
    recent_factor = jnp.exp(recent_max - top)
    total = cache_factor * cache_total + recent_factor * recent_total
    acc = cache_factor * acc + recent_factor * recent_acc
    attended = (acc / total).astype(jnp.bfloat16)
    order = head_major((body, body), pages, per_page, heads)
    attended = dot(order, attended, TN).astype(jnp.bfloat16)
    for h in range(heads):
        att[:, h * HD : (h + 1) * HD] = attended[h * rows : (h + 1) * rows]

    tile = functools.reduce(jnp.add, [parts[b][body + EXT :, :] for b in range(chunks)])
    used = EXT // 2
    value = tile[used:] * lax.rsqrt(tile[:used] / width + EPS)
    mean = jnp.sum(value, keepdims=True) / span
    own = lax.div(me * (slots * span // chunks), span)
    mean = jnp.where(iota((EXT, LANES), 0) == own, mean, 0.0)

    part = w_ref.shape[1] // chunks
    for r in range(chunks):
        out = outs[r] if split else outs[0].at[me ^ r]
        product = dot(att[...], w_ref[:, aligned(me ^ r, part)])
        for c in range(part // LANES):
            out[c * rows : (c + 1) * rows, :] = product[:, c * LANES : (c + 1) * LANES]
        out[out.shape[0] - EXT :, :] = mean


def sum_kernel(rows, *refs):
    parts, (out_ref, reward_ref) = refs[:-2], refs[-2:]
    if len(parts) == 1:
        parts = [parts[0].at[b] for b in range(parts[0].shape[0])]
    total = parts[0][...]
    for part in parts[1:]:
        total = total + part[...]
    for c in range(out_ref.shape[1] // LANES):
        out_ref[:, c * LANES : (c + 1) * LANES] = total[c * rows : (c + 1) * rows].astype(
            jnp.bfloat16
        )
    reward_ref[...] = total[total.shape[0] - EXT :]


LINE = (6, 2, 4)
ALL = (6, 1, 7, 2, 5, 3, 4)


def partner(x, chunks, bits):
    return lax.ppermute(x, "tensor", [(i, i ^ bits) for i in range(chunks)])


def spread_all(x, chunks, index, tie=None):
    if chunks != KVH:
        every = lax.all_to_all(jnp.broadcast_to(x[None], (chunks,) + x.shape), "tensor", 0, 0, tiled=True)
        return jnp.take(every, index ^ jnp.arange(chunks), axis=0), x
    pair = jnp.stack([x, partner(x, chunks, 1)])
    if tie is not None:
        pair, tie = lax.optimization_barrier((pair, tie))
        after = tie
    else:
        after = pair
    others = {bits: partner(pair, chunks, bits) for bits in LINE}
    return jnp.stack([pair] + [others[bits] for bits in sorted(LINE)]).reshape((chunks,) + x.shape), after


def trade(blocks, chunks):
    if len(blocks) == 1:
        return [lax.all_to_all(blocks[0], "tensor", 0, 0, tiled=True)]
    traded = {bits: partner(blocks[bits], chunks, bits) for bits in ALL}
    return [blocks[0]] + [traded[bits] for bits in range(1, chunks)]


def local(
    chunks,
    reward_hidden,
    reward_gain,
    reward_head,
    decode_inputs,
    attn_gain,
    w_query,
    w_keyval,
    w_out,
    cache_keys,
    cache_values,
    lengths,
    slot_map,
):
    slots, width = cache_keys.shape[:2]
    depth, qcols = w_query.shape
    kvcols = w_keyval.shape[1]
    part = decode_inputs.shape[-1]
    heads = qcols // HD
    group = heads * chunks // KVH
    split = group // heads
    pages = slots // PAIR
    per_page = PAIR * STEPS
    page_rows = per_page * group
    rows = slots * STEPS
    body = rows * heads
    index = lax.axis_index("tensor")
    swap = [(0, 1), (1, 0)]
    direct = chunks == KVH

    meta, take, give = pl.pallas_call(
        functools.partial(plan_kernel, slots, STEPS),
        in_specs=[SMEM, SMEM],
        out_specs=[SMEM, VMEM, VMEM],
        out_shape=(
            jax.ShapeDtypeStruct((2 * pages,), jnp.int32),
            jax.ShapeDtypeStruct((rows, 2 * rows), jnp.bfloat16),
            jax.ShapeDtypeStruct((rows, 2 * rows), jnp.bfloat16),
        ),
        scratch_shapes=[
            pltpu.SMEM(slot_map.shape, jnp.int32),
            pltpu.SMEM(slot_map.shape, jnp.int32),
        ],
        compiler_params=pltpu.CompilerParams(vmem_limit_bytes=MIB),
        name="plan",
    )(slot_map, lengths)

    early = pl.pallas_call(
        early_kernel,
        in_specs=[ANY] * 3,
        out_specs=VMEM,
        out_shape=jax.ShapeDtypeStruct((EXT, LANES), jnp.float32),
        compiler_params=pltpu.CompilerParams(vmem_limit_bytes=38 * MIB),
        name="early",
    )(w_out, w_out, w_out)
    own, after = spread_all(decode_inputs.reshape(rows, part), chunks, index, early)
    far = lax.ppermute(own, "dp", swap)

    pieces = max(kvcols // LANES, 1)
    packed_rows = body + pieces * rows
    packed = pl.pallas_call(
        functools.partial(project_kernel, pages, per_page, depth),
        in_specs=[ANY] + [VMEM] * 6,
        out_specs=VMEM,
        out_shape=jax.ShapeDtypeStruct((packed_rows, LANES), jnp.bfloat16),
        scratch_shapes=[
            pltpu.VMEM((chunks, rows, part), jnp.bfloat16),
        ],
        compiler_params=pltpu.CompilerParams(vmem_limit_bytes=4 * MIB),
        cost_estimate=pl.CostEstimate(
            flops=2 * rows * depth * (qcols + kvcols),
            bytes_accessed=2 * depth * (qcols + kvcols),
            transcendentals=0,
        ),
        name="project",
    )(after, own, far, take, attn_gain.reshape(chunks, 1, part), w_query, w_keyval)
    gathered, after = spread_all(packed, chunks, index)

    span = reward_hidden.shape[1]
    tiled = direct and slots == chunks
    reward_parts = pl.pallas_call(
        reward_kernel,
        in_specs=[ANY, ANY, VMEM, VMEM] + [ANY] * 0,
        out_specs=VMEM,
        out_shape=jax.ShapeDtypeStruct(
            (slots, EXT, LANES) if tiled else (2 * slots, span), jnp.float32
        ),
        scratch_shapes=[
            pltpu.VMEM(reward_hidden.shape, reward_hidden.dtype),
            pltpu.SemaphoreType.DMA((slots,)),
        ],
        compiler_params=pltpu.CompilerParams(vmem_limit_bytes=8 * MIB),
        cost_estimate=pl.CostEstimate(
            flops=4 * reward_hidden.size,
            bytes_accessed=2 * reward_hidden.size,
            transcendentals=0,
        ),
        name="reward",
    )(after, reward_hidden, reward_gain[None], reward_head[None])

    def tile(values):
        values = values.reshape(chunks, -1)
        size = EXT // 2 * LANES
        return jnp.pad(values, ((0, 0), (0, size - values.shape[1]))).reshape(
            chunks, EXT // 2, LANES
        )

    if not tiled:
        reward_parts = jnp.concatenate(
            [tile(reward_parts[:slots]), tile(reward_parts[slots:])], axis=1
        )
    fresh = gathered
    if not direct:
        fresh = jnp.take(gathered[:, body:, :kvcols], index ^ jnp.arange(chunks), axis=0)
        fresh = fresh.transpose(1, 0, 2).reshape(rows, 2 * KVH, HD).transpose(1, 0, 2)
    queries = gathered
    if not direct:
        queries = (
            jnp.take(gathered[:, :body], index ^ jnp.arange(chunks), axis=0)
            .reshape(KVH, split, pages, heads * per_page, HD)
            .transpose(0, 2, 1, 3, 4)
            .reshape(KVH, pages * page_rows, HD)
        )

    big = pages * page_rows
    block = (big + 2 * EXT, HD)
    attended = pl.pallas_call(
        functools.partial(attend_kernel, pages, page_rows),
        in_specs=[SMEM] + [VMEM] * 4,
        out_specs=[VMEM] * (KVH if direct else 1),
        out_shape=(
            [jax.ShapeDtypeStruct(block, jnp.float32)] * KVH
            if direct
            else [jax.ShapeDtypeStruct((KVH,) + block, jnp.float32)]
        ),
        scratch_shapes=[
            pltpu.VMEM((KVH * page_rows, KVH * HD), jnp.bfloat16),
            pltpu.VMEM((KVH * page_rows, KVH * HD), jnp.float32),
        ],
        compiler_params=pltpu.CompilerParams(vmem_limit_bytes=6 * MIB),
        cost_estimate=pl.CostEstimate(
            flops=4 * pages * width * KVH * HD * KVH * page_rows,
            bytes_accessed=4 * pages * width * KVH * HD,
            transcendentals=pages * width * KVH * page_rows,
        ),
        name="attend",
    )(meta, queries, cache_keys, cache_values, reward_parts)
    if not direct:
        acc = (
            attended[0][:, :big]
            .reshape(KVH, pages, split, heads * per_page, HD)
            .transpose(0, 2, 1, 3, 4)
            .reshape(chunks, body, HD)
        )
        extra = jnp.repeat(attended[0][:, big : big + EXT], split, axis=0)
        attended = [jnp.concatenate([acc, extra, reward_parts], axis=1)]
    parts = trade(attended, chunks)

    chunk_rows = part // LANES * rows + EXT
    partial = pl.pallas_call(
        functools.partial(merge_kernel, pages, per_page, depth, span, slots, chunks),
        in_specs=[VMEM] * (3 + len(parts)),
        out_specs=[VMEM] * len(parts),
        out_shape=(
            [jax.ShapeDtypeStruct((chunk_rows, LANES), jnp.float32)] * chunks
            if direct
            else [jax.ShapeDtypeStruct((chunks, chunk_rows, LANES), jnp.float32)]
        ),
        scratch_shapes=[pltpu.VMEM((rows, qcols), jnp.bfloat16)],
        compiler_params=pltpu.CompilerParams(vmem_limit_bytes=8 * MIB),
        cost_estimate=pl.CostEstimate(
            flops=2 * rows * qcols * depth, bytes_accessed=2 * qcols * depth, transcendentals=0
        ),
        name="merge",
    )(packed, fresh, w_out, *parts)
    partial = trade(partial, chunks)

    decoded, reward = pl.pallas_call(
        functools.partial(sum_kernel, rows),
        out_shape=(
            jax.ShapeDtypeStruct((rows, part), jnp.bfloat16),
            jax.ShapeDtypeStruct((EXT, LANES), jnp.float32),
        ),
        compiler_params=pltpu.CompilerParams(vmem_limit_bytes=8 * MIB),
        name="total",
    )(*partial)
    far = lax.ppermute(decoded, "dp", swap)
    decoded = dot(give, jnp.concatenate([decoded, far], axis=0)).astype(jnp.bfloat16)
    return (reward[:slots, 0], decoded.reshape(STEPS, slots, part))


def solution(mesh):
    chunks = mesh.shape["tensor"]

    def body(*arrays):
        return local(chunks, *arrays)

    return jax.shard_map(
        body,
        mesh=mesh,
        in_specs=(
            P(("groups", "dp"), None, "tensor"),
            P("tensor"),
            P("tensor"),
            P(None, ("groups", "dp"), "tensor"),
            P(),
            P(None, "tensor"),
            P(None, "tensor"),
            P("tensor", None),
            P(("groups", "dp"), "tensor", None),
            P(("groups", "dp"), "tensor", None),
            P("groups"),
            P("groups"),
        ),
        out_specs=(P(("groups", "dp")), P(None, ("groups", "dp"), "tensor")),
        check_vma=False,
    )
```

```python
import functools

import jax
import jax.numpy as jnp
from jax import lax
from jax.experimental import pallas as pl
from jax.experimental.pallas import tpu as pltpu
from jax.sharding import PartitionSpec as P


HD = 128
KVH = 8
STEPS = 2
PAIR = 2
LANES = 128
EXT = 8
EPS = 1e-05
NEG = -1e30
SCALE = HD ** (-0.5)
NT = (((1,), (1,)), ((), ()))
TN = (((0,), (0,)), ((), ()))
MIB = 1 << 20
ANY = pl.BlockSpec(memory_space=pl.ANY)
VMEM = pl.BlockSpec(memory_space=pltpu.VMEM)
SMEM = pl.BlockSpec(memory_space=pltpu.SMEM)


def iota(shape, dim):
    return lax.broadcasted_iota(jnp.int32, shape, dim)


def dot(a, b, dims=(((1,), (0,)), ((), ()))):
    return lax.dot_general(a, b, dims, preferred_element_type=jnp.float32)


def head_major(shape, pages, per_page, heads):
    o, s = iota(shape, 0), iota(shape, 1)
    row = o % per_page
    head = (o // per_page) % heads
    page = o // (per_page * heads)
    return (s == (head * pages + page) * per_page + row).astype(jnp.bfloat16)


def aligned(index, size):
    return pl.ds(pl.multiple_of(index * size, size), size)


def early_kernel(*refs):
    refs[-1][...] = jnp.zeros_like(refs[-1])


def plan_kernel(slots, steps, map_ref, length_ref, meta_ref, take_ref, give_ref, before_ref, place_ref):
    count = map_ref.shape[0]
    mine = lax.axis_index("dp")
    base = mine * slots
    for block in range(count // slots):
        found = jnp.int32(0)
        for s in range(block * slots, (block + 1) * slots):
            before_ref[s] = found
            found = found + (map_ref[s] == s).astype(jnp.int32)
    for s in range(slots):
        own = map_ref[base + s] == base + s

        @pl.when(own)
        def _():
            slot = before_ref[base + s]
            meta_ref[slot] = jnp.int32(s)
            meta_ref[slots // PAIR + slot] = length_ref[base + s]

    for r in range(count):
        source = map_ref[r]
        place_ref[r] = (
            lax.div(source, slots) * slots
            + PAIR * before_ref[source]
            + (source != r).astype(jnp.int32)
        )
    rows = slots * steps
    line, col = iota((rows, 2 * rows), 0), iota((rows, 2 * rows), 1)
    same = line % steps == (col // slots) % steps
    take = jnp.zeros((rows, 2 * rows), jnp.bool_)
    give = jnp.zeros((rows, 2 * rows), jnp.bool_)
    for side in range(2):
        start = base if side == 0 else (1 - mine) * slots
        for s in range(slots):
            target = place_ref[start + s] - base
            column = (col // rows == side) & (col % slots == s)
            take = take | (same & column & (line // steps == target))
    for s in range(slots):
        place = place_ref[base + s]
        far = (lax.div(place, slots) != mine).astype(jnp.int32)
        target = far * rows + lax.rem(place, slots) * steps
        give = give | ((line % slots == s) & (col == line // slots + target))
    take_ref[...] = take.astype(jnp.float32).astype(jnp.bfloat16)
    give_ref[...] = give.astype(jnp.float32).astype(jnp.bfloat16)


def reward_kernel(after_ref, hidden_ref, gain_ref, head_ref, *rest):
    out_ref, buffer, sems = rest[-3:]
    slots = hidden_ref.shape[0]
    loads = [
        pltpu.make_async_copy(hidden_ref.at[s], buffer.at[s], sems.at[s]) for s in range(slots)
    ]
    for load in loads:
        load.start()
    weight = gain_ref[...] * head_ref[...]
    for s in range(slots):
        loads[s].wait()
        hidden = buffer[s].astype(jnp.float32)
        for half, value in enumerate((hidden * hidden, hidden * weight)):
            sums = jnp.sum(value, axis=-1)
            if len(out_ref.shape) == 2:
                out_ref[half * slots + s] = sums
                continue
            for c in range(EXT // 4):
                piece = jnp.zeros((LANES,), jnp.float32)
                if c < sums.shape[0] // LANES:
                    piece = sums[c * LANES : (c + 1) * LANES]
                out_ref[s, half * (EXT // 4) + c] = piece


def project_kernel(pages, per_page, width, after_ref, own_ref, far_ref, take_ref, gain_ref, wq_ref, wkv_ref, out_ref, tokens):
    me = lax.axis_index("tensor")
    chunks, rows, depth = own_ref.shape
    total = jnp.zeros((rows, depth), jnp.float32)
    for r in range(chunks):
        both = jnp.concatenate([own_ref[r], far_ref[r]], axis=0)
        part = dot(take_ref[...], both)
        tokens[r] = part.astype(jnp.bfloat16)
        total = total + part * part
    inv = lax.rsqrt(jnp.sum(total, axis=-1, keepdims=True) / width + EPS)

    query = jnp.zeros((rows, wq_ref.shape[1]), jnp.float32)
    keyval = jnp.zeros((rows, wkv_ref.shape[1]), jnp.float32)
    for r in range(chunks):
        normed = (tokens[r].astype(jnp.float32) * inv * gain_ref[me ^ r]).astype(jnp.bfloat16)
        query = query + dot(normed, wq_ref[aligned(me ^ r, depth), :])
        keyval = keyval + dot(normed, wkv_ref[aligned(me ^ r, depth), :])

    heads = query.shape[1] // HD
    query = query.astype(jnp.bfloat16)
    stacked = jnp.concatenate([query[:, h * HD : (h + 1) * HD] for h in range(heads)], axis=0)
    order = head_major((rows * heads, rows * heads), pages, per_page, heads)
    body = rows * heads
    out_ref[:body] = dot(order, stacked).astype(jnp.bfloat16)
    keyval = keyval.astype(jnp.bfloat16)
    columns = keyval.shape[1]
    if columns < LANES:
        pad = jnp.zeros((rows, LANES - columns), jnp.bfloat16)
        keyval = jnp.concatenate([keyval, pad], axis=1)
    for v in range(keyval.shape[1] // LANES):
        out_ref[body + v * rows : body + (v + 1) * rows] = keyval[:, v * LANES : (v + 1) * LANES]


def attend_kernel(pages, page_rows, meta_ref, q_ref, k_ref, v_ref, reward_ref, *rest):
    outs, (spread, product) = rest[:-2], rest[-2:]
    width = k_ref.shape[1]
    span = KVH * page_rows
    body = pages * page_rows
    first = lax.axis_index("tensor") * width
    me = lax.axis_index("tensor") if len(outs) > 1 else 0
    spread[...] = jnp.zeros_like(spread)
    stats = [[jnp.zeros((1, LANES), jnp.float32)] * 2 for _ in range(KVH)]
    for i in range(pages):
        for r in range(KVH):
            spread[r * page_rows : (r + 1) * page_rows, aligned(me ^ r, HD)] = q_ref[
                r, i * page_rows : (i + 1) * page_rows, :
            ]
        scores = dot(k_ref[meta_ref[i]], spread[...], NT) * SCALE
        valid = first + iota((width, span), 0) < meta_ref[pages + i]
        scores = jnp.where(valid, scores, NEG)
        top = jnp.max(scores, axis=0, keepdims=True)
        expo = jnp.where(valid, jnp.exp(scores - top), 0.0)
        total = jnp.sum(expo, axis=0, keepdims=True)
        weights = expo.astype(jnp.bfloat16)
        rows = 2 * page_rows
        for pair in range(KVH // 2):
            values = v_ref[meta_ref[i], :, aligned(pair ^ lax.div(me, 2), 2 * HD)]
            product[pair * rows : (pair + 1) * rows] = dot(
                weights[:, pair * rows : (pair + 1) * rows], values, TN
            )
        for r in range(KVH):
            out = outs[r] if len(outs) > 1 else outs[0].at[r]
            out[i * page_rows : (i + 1) * page_rows, :] = product[
                r * page_rows : (r + 1) * page_rows, aligned((me ^ r) & 1, HD)
            ]
            start = r * page_rows
            lane = start // LANES * LANES
            shift = (i * page_rows - start) % LANES
            mask = iota((1, LANES), 1) // page_rows == i
            for k, packed in enumerate((top, total)):
                packed = packed[:, lane : lane + LANES]
                if shift:
                    packed = pltpu.roll(packed, shift, 1)
                stats[r][k] = jnp.where(mask, packed, stats[r][k])
    for r in range(KVH):
        out = outs[r] if len(outs) > 1 else outs[0].at[r]
        out[body : body + 2, :] = jnp.concatenate(stats[r], axis=0)
        if len(outs) > 1:
            out[body + 2 : body + 4, :] = jnp.zeros((2, LANES), jnp.float32)
            out[body + 4 :, :] = reward_ref[me ^ r]
        else:
            out[body + 2 :, :] = jnp.zeros((EXT - 2, LANES), jnp.float32)


def merge_kernel(pages, per_page, width, span, slots, chunks, q_ref, gathered_ref, w_ref, *rest):
    att = rest[-1]
    split = len(rest) > 3
    parts = rest[:chunks] if split else [rest[0].at[b] for b in range(chunks)]
    outs = rest[chunks:-1] if split else rest[1:-1]
    me = lax.axis_index("tensor")
    body = parts[0].shape[0] - EXT
    page_rows = body // pages
    heads = page_rows // per_page
    rows = pages * per_page

    kv_head = lax.div(me * heads, heads * chunks // KVH)
    if split:
        pieces = (gathered_ref.shape[1] - body) // rows

        def fresh_of(column):
            source = lax.div(column, pieces) ^ me
            start = pl.multiple_of(body + lax.rem(column, pieces) * rows, rows)
            return gathered_ref[source, pl.ds(start, rows), :]

        fresh_k, fresh_v = fresh_of(kv_head), fresh_of(KVH + kv_head)
    else:
        fresh_k, fresh_v = gathered_ref[kv_head], gathered_ref[KVH + kv_head]

    query = q_ref[:body, :]
    recent = dot(query, fresh_k, NT) * SCALE
    line, col = iota(recent.shape, 0), iota(recent.shape, 1)
    mine = (line // page_rows) * per_page + line % per_page
    seen = (mine // STEPS == col // STEPS) & (col <= mine)
    recent = jnp.where(seen, recent, NEG)
    recent_max = jnp.max(recent, axis=-1, keepdims=True)
    recent_exp = jnp.where(seen, jnp.exp(recent - recent_max), 0.0)
    recent_total = jnp.sum(recent_exp, axis=-1, keepdims=True)
    recent_acc = dot(recent_exp.astype(jnp.bfloat16), fresh_v)

    maxima = [parts[b][body : body + 1, :] for b in range(chunks)]
    totals = [parts[b][body + 1 : body + 2, :] for b in range(chunks)]
    top = functools.reduce(jnp.maximum, maxima)
    factors = [jnp.exp(m - top) for m in maxima]
    total = functools.reduce(jnp.add, [f * t for f, t in zip(factors, totals)])

    pick = iota((body, LANES), 0) == iota((body, LANES), 1)

    def column(packed):
        wide = jnp.where(pick, jnp.broadcast_to(packed, pick.shape), 0.0)
        return jnp.sum(wide, axis=-1, keepdims=True)

    acc = jnp.zeros((body, HD), jnp.float32)
    for b in range(chunks):
        acc = acc + column(factors[b]) * parts[b][:body, :]
    cache_top, cache_total = column(top), column(total)
    top = jnp.maximum(cache_top, recent_max)
    cache_factor = jnp.exp(cache_top - top)
    recent_factor = jnp.exp(recent_max - top)
    total = cache_factor * cache_total + recent_factor * recent_total
    acc = cache_factor * acc + recent_factor * recent_acc
    attended = (acc / total).astype(jnp.bfloat16)
    order = head_major((body, body), pages, per_page, heads)
    attended = dot(order, attended, TN).astype(jnp.bfloat16)
    for h in range(heads):
        att[:, h * HD : (h + 1) * HD] = attended[h * rows : (h + 1) * rows]

    tile = functools.reduce(jnp.add, [parts[b][body + EXT // 2 :, :] for b in range(chunks)])
    used = EXT // 4
    value = tile[used:] * lax.rsqrt(tile[:used] / width + EPS)
    mean = jnp.sum(value, keepdims=True) / span
    own = lax.div(me * (slots * span // chunks), span)
    mean = jnp.where(iota((EXT, LANES), 0) == own, mean, 0.0)

    part = w_ref.shape[1] // chunks
    for r in range(chunks):
        out = outs[r] if split else outs[0].at[me ^ r]
        product = dot(att[...], w_ref[:, aligned(me ^ r, part)])
        for c in range(part // LANES):
            out[c * rows : (c + 1) * rows, :] = product[:, c * LANES : (c + 1) * LANES]
        out[out.shape[0] - EXT :, :] = mean


def sum_kernel(rows, *refs):
    parts, (out_ref, reward_ref) = refs[:-2], refs[-2:]
    if len(parts) == 1:
        parts = [parts[0].at[b] for b in range(parts[0].shape[0])]
    total = parts[0][...]
    for part in parts[1:]:
        total = total + part[...]
    for c in range(out_ref.shape[1] // LANES):
        out_ref[:, c * LANES : (c + 1) * LANES] = total[c * rows : (c + 1) * rows].astype(
            jnp.bfloat16
        )
    reward_ref[...] = total[total.shape[0] - EXT :]


LINE = (6, 2, 4)
ALL = (6, 1, 7, 2, 5, 3, 4)


def partner(x, chunks, bits):
    return lax.ppermute(x, "tensor", [(i, i ^ bits) for i in range(chunks)])


def spread_all(x, chunks, index, tie=None):
    if chunks != KVH:
        every = lax.all_to_all(jnp.broadcast_to(x[None], (chunks,) + x.shape), "tensor", 0, 0, tiled=True)
        return jnp.take(every, index ^ jnp.arange(chunks), axis=0), x
    pair = jnp.stack([x, partner(x, chunks, 1)])
    if tie is not None:
        pair, tie = lax.optimization_barrier((pair, tie))
        after = tie
    else:
        after = pair
    others = {bits: partner(pair, chunks, bits) for bits in LINE}
    return jnp.stack([pair] + [others[bits] for bits in sorted(LINE)]).reshape((chunks,) + x.shape), after


def trade(blocks, chunks):
    if len(blocks) == 1:
        return [lax.all_to_all(blocks[0], "tensor", 0, 0, tiled=True)]
    traded = {bits: partner(blocks[bits], chunks, bits) for bits in ALL}
    return [blocks[0]] + [traded[bits] for bits in range(1, chunks)]


def local(
    chunks,
    reward_hidden,
    reward_gain,
    reward_head,
    decode_inputs,
    attn_gain,
    w_query,
    w_keyval,
    w_out,
    cache_keys,
    cache_values,
    lengths,
    slot_map,
):
    slots, width = cache_keys.shape[:2]
    depth, qcols = w_query.shape
    kvcols = w_keyval.shape[1]
    part = decode_inputs.shape[-1]
    heads = qcols // HD
    group = heads * chunks // KVH
    split = group // heads
    pages = slots // PAIR
    per_page = PAIR * STEPS
    page_rows = per_page * group
    rows = slots * STEPS
    body = rows * heads
    index = lax.axis_index("tensor")
    swap = [(0, 1), (1, 0)]
    direct = chunks == KVH

    meta, take, give = pl.pallas_call(
        functools.partial(plan_kernel, slots, STEPS),
        in_specs=[SMEM, SMEM],
        out_specs=[SMEM, VMEM, VMEM],
        out_shape=(
            jax.ShapeDtypeStruct((2 * pages,), jnp.int32),
            jax.ShapeDtypeStruct((rows, 2 * rows), jnp.bfloat16),
            jax.ShapeDtypeStruct((rows, 2 * rows), jnp.bfloat16),
        ),
        scratch_shapes=[
            pltpu.SMEM(slot_map.shape, jnp.int32),
            pltpu.SMEM(slot_map.shape, jnp.int32),
        ],
        compiler_params=pltpu.CompilerParams(vmem_limit_bytes=MIB),
        name="plan",
    )(slot_map, lengths)

    early = pl.pallas_call(
        early_kernel,
        in_specs=[ANY] * 3,
        out_specs=VMEM,
        out_shape=jax.ShapeDtypeStruct((EXT, LANES), jnp.float32),
        compiler_params=pltpu.CompilerParams(vmem_limit_bytes=38 * MIB),
        name="early",
    )(w_out, w_out, w_out)
    own, after = spread_all(decode_inputs.reshape(rows, part), chunks, index, early)
    far = lax.ppermute(own, "dp", swap)

    pieces = max(kvcols // LANES, 1)
    packed_rows = body + pieces * rows
    packed = pl.pallas_call(
        functools.partial(project_kernel, pages, per_page, depth),
        in_specs=[ANY] + [VMEM] * 6,
        out_specs=VMEM,
        out_shape=jax.ShapeDtypeStruct((packed_rows, LANES), jnp.bfloat16),
        scratch_shapes=[
            pltpu.VMEM((chunks, rows, part), jnp.bfloat16),
        ],
        compiler_params=pltpu.CompilerParams(vmem_limit_bytes=4 * MIB),
        cost_estimate=pl.CostEstimate(
            flops=2 * rows * depth * (qcols + kvcols),
            bytes_accessed=2 * depth * (qcols + kvcols),
            transcendentals=0,
        ),
        name="project",
    )(after, own, far, take, attn_gain.reshape(chunks, 1, part), w_query, w_keyval)
    gathered, after = spread_all(packed, chunks, index)

    span = reward_hidden.shape[1]
    tiled = direct and slots == chunks and span <= EXT // 4 * LANES
    reward_parts = pl.pallas_call(
        reward_kernel,
        in_specs=[ANY, ANY, VMEM, VMEM] + [ANY] * 0,
        out_specs=VMEM,
        out_shape=jax.ShapeDtypeStruct(
            (slots, EXT // 2, LANES) if tiled else (2 * slots, span), jnp.float32
        ),
        scratch_shapes=[
            pltpu.VMEM(reward_hidden.shape, reward_hidden.dtype),
            pltpu.SemaphoreType.DMA((slots,)),
        ],
        compiler_params=pltpu.CompilerParams(vmem_limit_bytes=8 * MIB),
        cost_estimate=pl.CostEstimate(
            flops=4 * reward_hidden.size,
            bytes_accessed=2 * reward_hidden.size,
            transcendentals=0,
        ),
        name="reward",
    )(after, reward_hidden, reward_gain[None], reward_head[None])

    def tile(values):
        values = values.reshape(chunks, -1)
        size = EXT // 4 * LANES
        return jnp.pad(values, ((0, 0), (0, size - values.shape[1]))).reshape(
            chunks, EXT // 4, LANES
        )

    if not tiled:
        reward_parts = jnp.concatenate(
            [tile(reward_parts[:slots]), tile(reward_parts[slots:])], axis=1
        )
    fresh = gathered
    if not direct:
        fresh = jnp.take(gathered[:, body:, :kvcols], index ^ jnp.arange(chunks), axis=0)
        fresh = fresh.transpose(1, 0, 2).reshape(rows, 2 * KVH, HD).transpose(1, 0, 2)
    queries = gathered
    if not direct:
        queries = (
            jnp.take(gathered[:, :body], index ^ jnp.arange(chunks), axis=0)
            .reshape(KVH, split, pages, heads * per_page, HD)
            .transpose(0, 2, 1, 3, 4)
            .reshape(KVH, pages * page_rows, HD)
        )

    big = pages * page_rows
    block = (big + EXT, HD)
    attended = pl.pallas_call(
        functools.partial(attend_kernel, pages, page_rows),
        in_specs=[SMEM] + [VMEM] * 4,
        out_specs=[VMEM] * (KVH if direct else 1),
        out_shape=(
            [jax.ShapeDtypeStruct(block, jnp.float32)] * KVH
            if direct
            else [jax.ShapeDtypeStruct((KVH,) + block, jnp.float32)]
        ),
        scratch_shapes=[
            pltpu.VMEM((KVH * page_rows, KVH * HD), jnp.bfloat16),
            pltpu.VMEM((KVH * page_rows, 2 * HD), jnp.float32),
        ],
        compiler_params=pltpu.CompilerParams(vmem_limit_bytes=6 * MIB),
        cost_estimate=pl.CostEstimate(
            flops=4 * pages * width * KVH * HD * KVH * page_rows,
            bytes_accessed=4 * pages * width * KVH * HD,
            transcendentals=pages * width * KVH * page_rows,
        ),
        name="attend",
    )(meta, queries, cache_keys, cache_values, reward_parts)
    if not direct:
        acc = (
            attended[0][:, :big]
            .reshape(KVH, pages, split, heads * per_page, HD)
            .transpose(0, 2, 1, 3, 4)
            .reshape(chunks, body, HD)
        )
        extra = attended[0][:, big : big + 2].reshape(KVH, 2, pages, split, heads * per_page)
        extra = extra.transpose(0, 3, 1, 2, 4).reshape(chunks, 2, body)
        extra = jnp.pad(extra, ((0, 0), (0, 2), (0, LANES - body)))
        attended = [jnp.concatenate([acc, extra, reward_parts], axis=1)]
    parts = trade(attended, chunks)

    chunk_rows = part // LANES * rows + EXT
    partial = pl.pallas_call(
        functools.partial(merge_kernel, pages, per_page, depth, span, slots, chunks),
        in_specs=[VMEM] * (3 + len(parts)),
        out_specs=[VMEM] * len(parts),
        out_shape=(
            [jax.ShapeDtypeStruct((chunk_rows, LANES), jnp.float32)] * chunks
            if direct
            else [jax.ShapeDtypeStruct((chunks, chunk_rows, LANES), jnp.float32)]
        ),
        scratch_shapes=[pltpu.VMEM((rows, qcols), jnp.bfloat16)],
        compiler_params=pltpu.CompilerParams(vmem_limit_bytes=8 * MIB),
        cost_estimate=pl.CostEstimate(
            flops=2 * rows * qcols * depth, bytes_accessed=2 * qcols * depth, transcendentals=0
        ),
        name="merge",
    )(packed, fresh, w_out, *parts)
    partial = trade(partial, chunks)

    decoded, reward = pl.pallas_call(
        functools.partial(sum_kernel, rows),
        out_shape=(
            jax.ShapeDtypeStruct((rows, part), jnp.bfloat16),
            jax.ShapeDtypeStruct((EXT, LANES), jnp.float32),
        ),
        compiler_params=pltpu.CompilerParams(vmem_limit_bytes=8 * MIB),
        name="total",
    )(*partial)
    far = lax.ppermute(decoded, "dp", swap)
    decoded = dot(give, jnp.concatenate([decoded, far], axis=0)).astype(jnp.bfloat16)
    return (reward[:slots, 0], decoded.reshape(STEPS, slots, part))


def solution(mesh):
    chunks = mesh.shape["tensor"]

    def body(*arrays):
        return local(chunks, *arrays)

    return jax.shard_map(
        body,
        mesh=mesh,
        in_specs=(
            P(("groups", "dp"), None, "tensor"),
            P("tensor"),
            P("tensor"),
            P(None, ("groups", "dp"), "tensor"),
            P(),
            P(None, "tensor"),
            P(None, "tensor"),
            P("tensor", None),
            P(("groups", "dp"), "tensor", None),
            P(("groups", "dp"), "tensor", None),
            P("groups"),
            P("groups"),
        ),
        out_specs=(P(("groups", "dp")), P(None, ("groups", "dp"), "tensor")),
        check_vma=False,
    )
```

```python
import functools

import jax
import jax.numpy as jnp
from jax import lax
from jax.experimental import pallas as pl
from jax.experimental.pallas import tpu as pltpu
from jax.sharding import PartitionSpec as P


HD = 128
KVH = 8
STEPS = 2
PAIR = 2
LANES = 128
EXT = 8
EPS = 1e-05
NEG = -1e30
SCALE = HD ** (-0.5)
NT = (((1,), (1,)), ((), ()))
TN = (((0,), (0,)), ((), ()))
MIB = 1 << 20
ANY = pl.BlockSpec(memory_space=pl.ANY)
VMEM = pl.BlockSpec(memory_space=pltpu.VMEM)
SMEM = pl.BlockSpec(memory_space=pltpu.SMEM)


def iota(shape, dim):
    return lax.broadcasted_iota(jnp.int32, shape, dim)


def dot(a, b, dims=(((1,), (0,)), ((), ()))):
    return lax.dot_general(a, b, dims, preferred_element_type=jnp.float32)


def head_major(shape, pages, per_page, heads):
    o, s = iota(shape, 0), iota(shape, 1)
    row = o % per_page
    head = (o // per_page) % heads
    page = o // (per_page * heads)
    return (s == (head * pages + page) * per_page + row).astype(jnp.bfloat16)


def aligned(index, size):
    return pl.ds(pl.multiple_of(index * size, size), size)


def early_kernel(*refs):
    refs[-1][...] = jnp.zeros_like(refs[-1])


def plan_kernel(slots, steps, map_ref, length_ref, meta_ref, take_ref, give_ref, before_ref, place_ref):
    count = map_ref.shape[0]
    mine = lax.axis_index("dp")
    base = mine * slots
    for block in range(count // slots):
        found = jnp.int32(0)
        for s in range(block * slots, (block + 1) * slots):
            before_ref[s] = found
            found = found + (map_ref[s] == s).astype(jnp.int32)
    for s in range(slots):
        own = map_ref[base + s] == base + s

        @pl.when(own)
        def _():
            slot = before_ref[base + s]
            meta_ref[slot] = jnp.int32(s)
            meta_ref[slots // PAIR + slot] = length_ref[base + s]

    for r in range(count):
        source = map_ref[r]
        place_ref[r] = (
            lax.div(source, slots) * slots
            + PAIR * before_ref[source]
            + (source != r).astype(jnp.int32)
        )
    rows = slots * steps
    line, col = iota((rows, 2 * rows), 0), iota((rows, 2 * rows), 1)
    same = line % steps == (col // slots) % steps
    take = jnp.zeros((rows, 2 * rows), jnp.bool_)
    give = jnp.zeros((rows, 2 * rows), jnp.bool_)
    for side in range(2):
        start = base if side == 0 else (1 - mine) * slots
        for s in range(slots):
            target = place_ref[start + s] - base
            column = (col // rows == side) & (col % slots == s)
            take = take | (same & column & (line // steps == target))
    for s in range(slots):
        place = place_ref[base + s]
        far = (lax.div(place, slots) != mine).astype(jnp.int32)
        target = far * rows + lax.rem(place, slots) * steps
        give = give | ((line % slots == s) & (col == line // slots + target))
    take_ref[...] = take.astype(jnp.float32).astype(jnp.bfloat16)
    give_ref[...] = give.astype(jnp.float32).astype(jnp.bfloat16)


def reward_kernel(after_ref, hidden_ref, gain_ref, head_ref, *rest):
    out_ref, buffer, sems = rest[-3:]
    slots = hidden_ref.shape[0]
    loads = [
        pltpu.make_async_copy(hidden_ref.at[s], buffer.at[s], sems.at[s]) for s in range(slots)
    ]
    for load in loads:
        load.start()
    weight = gain_ref[...] * head_ref[...]
    for s in range(slots):
        loads[s].wait()
        hidden = buffer[s].astype(jnp.float32)
        for half, value in enumerate((hidden * hidden, hidden * weight)):
            sums = jnp.sum(value, axis=-1)
            if len(out_ref.shape) == 2:
                out_ref[half * slots + s] = sums
                continue
            for c in range(EXT // 4):
                piece = jnp.zeros((LANES,), jnp.float32)
                if c < sums.shape[0] // LANES:
                    piece = sums[c * LANES : (c + 1) * LANES]
                out_ref[s, half * (EXT // 4) + c] = piece


def choose_kernel(after_ref, take_ref, own_ref, far_ref, near_ref, both_ref, out_ref):
    for w, (a, b) in enumerate(((own_ref, far_ref), (near_ref, both_ref))):
        rows = jnp.concatenate([a[...], b[...]], axis=0)
        out_ref[w] = dot(take_ref[...], rows).astype(jnp.bfloat16)


def project_kernel(pages, per_page, width, x_ref, gain_ref, wq_ref, wkv_ref, out_ref):
    me = lax.axis_index("tensor")
    chunks, rows, depth = x_ref.shape
    total = jnp.zeros((rows, depth), jnp.float32)
    for r in range(chunks):
        part = x_ref[r].astype(jnp.float32)
        total = total + part * part
    inv = lax.rsqrt(jnp.sum(total, axis=-1, keepdims=True) / width + EPS)

    query = jnp.zeros((rows, wq_ref.shape[1]), jnp.float32)
    keyval = jnp.zeros((rows, wkv_ref.shape[1]), jnp.float32)
    for r in range(chunks):
        normed = (x_ref[r].astype(jnp.float32) * inv * gain_ref[me ^ r]).astype(jnp.bfloat16)
        query = query + dot(normed, wq_ref[aligned(me ^ r, depth), :])
        keyval = keyval + dot(normed, wkv_ref[aligned(me ^ r, depth), :])

    heads = query.shape[1] // HD
    query = query.astype(jnp.bfloat16)
    stacked = jnp.concatenate([query[:, h * HD : (h + 1) * HD] for h in range(heads)], axis=0)
    order = head_major((rows * heads, rows * heads), pages, per_page, heads)
    body = rows * heads
    out_ref[:body] = dot(order, stacked).astype(jnp.bfloat16)
    keyval = keyval.astype(jnp.bfloat16)
    columns = keyval.shape[1]
    if columns < LANES:
        pad = jnp.zeros((rows, LANES - columns), jnp.bfloat16)
        keyval = jnp.concatenate([keyval, pad], axis=1)
    for v in range(keyval.shape[1] // LANES):
        out_ref[body + v * rows : body + (v + 1) * rows] = keyval[:, v * LANES : (v + 1) * LANES]


def attend_kernel(pages, page_rows, meta_ref, q_ref, k_ref, v_ref, reward_ref, *rest):
    outs, (spread, product) = rest[:-2], rest[-2:]
    width = k_ref.shape[1]
    span = KVH * page_rows
    body = pages * page_rows
    first = lax.axis_index("tensor") * width
    me = lax.axis_index("tensor") if len(outs) > 1 else 0
    spread[...] = jnp.zeros_like(spread)
    share = LANES // page_rows
    tops, totals = [], []
    for i in range(pages):
        for r in range(KVH):
            spread[i, r * page_rows : (r + 1) * page_rows, aligned(me ^ r, HD)] = q_ref[
                r, i * page_rows : (i + 1) * page_rows, :
            ]
        scores = dot(k_ref[meta_ref[i]], spread[i], NT) * SCALE
        valid = first + iota((width, span), 0) < meta_ref[pages + i]
        scores = jnp.where(valid, scores, NEG)
        top = jnp.max(scores, axis=0, keepdims=True)
        expo = jnp.where(valid, jnp.exp(scores - top), 0.0)
        total = jnp.sum(expo, axis=0, keepdims=True)
        weights = expo.astype(jnp.bfloat16)
        for part in range(KVH // share):
            values = v_ref[meta_ref[i], :, aligned(part ^ lax.div(me, share), share * HD)]
            lines = slice(part * share * page_rows, (part + 1) * share * page_rows)
            product[i, lines] = dot(weights[:, lines], values, TN)
        for r in range(KVH):
            out = outs[r] if len(outs) > 1 else outs[0].at[r]
            out[i * page_rows : (i + 1) * page_rows, :] = product[
                i, r * page_rows : (r + 1) * page_rows, aligned((me ^ r) & (share - 1), HD)
            ]
        tops.append(top)
        totals.append(total)
    held = iota((1, LANES), 1) // page_rows
    stats = []
    for part in range(KVH // share):
        lanes = slice(part * LANES, (part + 1) * LANES)
        tile = jnp.concatenate([x[:, lanes] for x in tops + totals], axis=0)
        turned = [tile] + [pltpu.roll(tile, t * page_rows, 1) for t in range(1, share)]
        for q in range(share):
            for skip in (0, pages):
                line = jnp.zeros((1, LANES), jnp.float32)
                for i in range(pages):
                    row = turned[(i - q) % share][skip + i : skip + i + 1]
                    line = jnp.where(held == i, row, line)
                stats.append(line)
    for r in range(KVH):
        out = outs[r] if len(outs) > 1 else outs[0].at[r]
        out[body : body + 2, :] = jnp.concatenate(stats[2 * r : 2 * r + 2], axis=0)
        if len(outs) > 1:
            out[body + 2 : body + 4, :] = jnp.zeros((2, LANES), jnp.float32)
            out[body + 4 :, :] = reward_ref[me ^ r]
        else:
            out[body + 2 :, :] = jnp.zeros((EXT - 2, LANES), jnp.float32)


def merge_kernel(pages, per_page, width, span, slots, chunks, q_ref, gathered_ref, w_ref, *rest):
    att = rest[-1]
    split = len(rest) > 3
    parts = rest[:chunks] if split else [rest[0].at[b] for b in range(chunks)]
    outs = rest[chunks:-1] if split else rest[1:-1]
    me = lax.axis_index("tensor")
    body = parts[0].shape[0] - EXT
    page_rows = body // pages
    heads = page_rows // per_page
    rows = pages * per_page

    kv_head = lax.div(me * heads, heads * chunks // KVH)
    if split:
        pieces = (gathered_ref.shape[1] - body) // rows

        def fresh_of(column):
            source = lax.div(column, pieces) ^ me
            start = pl.multiple_of(body + lax.rem(column, pieces) * rows, rows)
            return gathered_ref[source, pl.ds(start, rows), :]

        fresh_k, fresh_v = fresh_of(kv_head), fresh_of(KVH + kv_head)
    else:
        fresh_k, fresh_v = gathered_ref[kv_head], gathered_ref[KVH + kv_head]

    query = q_ref[:body, :]
    recent = dot(query, fresh_k, NT) * SCALE
    line, col = iota(recent.shape, 0), iota(recent.shape, 1)
    mine = (line // page_rows) * per_page + line % per_page
    seen = (mine // STEPS == col // STEPS) & (col <= mine)
    recent = jnp.where(seen, recent, NEG)
    recent_max = jnp.max(recent, axis=-1, keepdims=True)
    recent_exp = jnp.where(seen, jnp.exp(recent - recent_max), 0.0)
    recent_total = jnp.sum(recent_exp, axis=-1, keepdims=True)
    recent_acc = dot(recent_exp.astype(jnp.bfloat16), fresh_v)

    maxima = [parts[b][body : body + 1, :] for b in range(chunks)]
    totals = [parts[b][body + 1 : body + 2, :] for b in range(chunks)]
    top = functools.reduce(jnp.maximum, maxima)
    factors = [jnp.exp(m - top) for m in maxima]
    total = functools.reduce(jnp.add, [f * t for f, t in zip(factors, totals)])

    pick = iota((body, LANES), 0) == iota((body, LANES), 1)

    def column(packed):
        wide = jnp.where(pick, jnp.broadcast_to(packed, pick.shape), 0.0)
        return jnp.sum(wide, axis=-1, keepdims=True)

    acc = jnp.zeros((body, HD), jnp.float32)
    for b in range(chunks):
        acc = acc + column(factors[b]) * parts[b][:body, :]
    cache_top, cache_total = column(top), column(total)
    top = jnp.maximum(cache_top, recent_max)
    cache_factor = jnp.exp(cache_top - top)
    recent_factor = jnp.exp(recent_max - top)
    total = cache_factor * cache_total + recent_factor * recent_total
    acc = cache_factor * acc + recent_factor * recent_acc
    attended = (acc / total).astype(jnp.bfloat16)
    order = head_major((body, body), pages, per_page, heads)
    attended = dot(order, attended, TN).astype(jnp.bfloat16)
    for h in range(heads):
        att[:, h * HD : (h + 1) * HD] = attended[h * rows : (h + 1) * rows]

    tile = functools.reduce(jnp.add, [parts[b][body + EXT // 2 :, :] for b in range(chunks)])
    used = EXT // 4
    value = tile[used:] * lax.rsqrt(tile[:used] / width + EPS)
    mean = jnp.sum(value, keepdims=True) / span
    own = lax.div(me * (slots * span // chunks), span)
    mean = jnp.where(iota((EXT, LANES), 0) == own, mean, 0.0)

    part = w_ref.shape[1] // chunks
    for r in range(chunks):
        out = outs[r] if split else outs[0].at[me ^ r]
        product = dot(att[...], w_ref[:, aligned(me ^ r, part)])
        for c in range(part // LANES):
            out[c * rows : (c + 1) * rows, :] = product[:, c * LANES : (c + 1) * LANES]
        out[out.shape[0] - EXT :, :] = mean


def sum_kernel(rows, *refs):
    parts, (out_ref, reward_ref) = refs[:-2], refs[-2:]
    if len(parts) == 1:
        parts = [parts[0].at[b] for b in range(parts[0].shape[0])]
    total = parts[0][...]
    for part in parts[1:]:
        total = total + part[...]
    for c in range(out_ref.shape[1] // LANES):
        out_ref[:, c * LANES : (c + 1) * LANES] = total[c * rows : (c + 1) * rows].astype(
            jnp.bfloat16
        )
    reward_ref[...] = total[total.shape[0] - EXT :]


LINE = (6, 2, 4)
ALL = (6, 1, 7, 2, 5, 3, 4)


def partner(x, chunks, bits):
    return lax.ppermute(x, "tensor", [(i, i ^ bits) for i in range(chunks)])


def spread_line(pair, chunks):
    others = {bits: partner(pair, chunks, bits) for bits in LINE}
    stacked = jnp.stack([pair] + [others[bits] for bits in sorted(LINE)])
    return stacked.reshape((chunks,) + pair.shape[1:])


def spread_all(x, chunks, index):
    if chunks != KVH:
        every = jnp.broadcast_to(x[None], (chunks,) + x.shape)
        every = lax.all_to_all(every, "tensor", 0, 0, tiled=True)
        return jnp.take(every, index ^ jnp.arange(chunks), axis=0), x
    pair = jnp.stack([x, partner(x, chunks, 1)])
    return spread_line(pair, chunks), pair


def trade(blocks, chunks):
    if len(blocks) == 1:
        return [lax.all_to_all(blocks[0], "tensor", 0, 0, tiled=True)]
    traded = {bits: partner(blocks[bits], chunks, bits) for bits in ALL}
    return [blocks[0]] + [traded[bits] for bits in range(1, chunks)]


def local(
    chunks,
    reward_hidden,
    reward_gain,
    reward_head,
    decode_inputs,
    attn_gain,
    w_query,
    w_keyval,
    w_out,
    cache_keys,
    cache_values,
    lengths,
    slot_map,
):
    slots, width = cache_keys.shape[:2]
    depth, qcols = w_query.shape
    kvcols = w_keyval.shape[1]
    part = decode_inputs.shape[-1]
    heads = qcols // HD
    group = heads * chunks // KVH
    split = group // heads
    pages = slots // PAIR
    per_page = PAIR * STEPS
    page_rows = per_page * group
    rows = slots * STEPS
    body = rows * heads
    index = lax.axis_index("tensor")
    swap = [(0, 1), (1, 0)]
    direct = chunks == KVH

    meta, take, give = pl.pallas_call(
        functools.partial(plan_kernel, slots, STEPS),
        in_specs=[SMEM, SMEM],
        out_specs=[SMEM, VMEM, VMEM],
        out_shape=(
            jax.ShapeDtypeStruct((2 * pages,), jnp.int32),
            jax.ShapeDtypeStruct((rows, 2 * rows), jnp.bfloat16),
            jax.ShapeDtypeStruct((rows, 2 * rows), jnp.bfloat16),
        ),
        scratch_shapes=[
            pltpu.SMEM(slot_map.shape, jnp.int32),
            pltpu.SMEM(slot_map.shape, jnp.int32),
        ],
        compiler_params=pltpu.CompilerParams(vmem_limit_bytes=MIB),
        name="plan",
    )(slot_map, lengths)

    early = pl.pallas_call(
        early_kernel,
        in_specs=[ANY] * 3,
        out_specs=VMEM,
        out_shape=jax.ShapeDtypeStruct((EXT, LANES), jnp.float32),
        compiler_params=pltpu.CompilerParams(vmem_limit_bytes=38 * MIB),
        name="early",
    )(w_out, w_out, w_out)
    own = decode_inputs.reshape(rows, part)
    far = lax.ppermute(own, "dp", swap)
    if direct:
        near = partner(own, chunks, 1)
        cross = [
            (d * chunks + t, (1 - d) * chunks + (t ^ 1)) for d in range(2) for t in range(chunks)
        ]
        both = lax.ppermute(own, ("dp", "tensor"), cross)
        pair = pl.pallas_call(
            choose_kernel,
            in_specs=[ANY] + [VMEM] * 5,
            out_specs=VMEM,
            out_shape=jax.ShapeDtypeStruct((2, rows, part), jnp.bfloat16),
            compiler_params=pltpu.CompilerParams(vmem_limit_bytes=MIB),
            name="choose",
        )(early, take, own, far, near, both)
        tokens = spread_line(pair, chunks)
    else:
        chosen = dot(take, jnp.concatenate([own, far], axis=0)).astype(jnp.bfloat16)
        tokens, _ = spread_all(chosen, chunks, index)

    pieces = max(kvcols // LANES, 1)
    packed_rows = body + pieces * rows
    packed = pl.pallas_call(
        functools.partial(project_kernel, pages, per_page, depth),
        in_specs=[VMEM] * 4,
        out_specs=VMEM,
        out_shape=jax.ShapeDtypeStruct((packed_rows, LANES), jnp.bfloat16),
        compiler_params=pltpu.CompilerParams(vmem_limit_bytes=4 * MIB),
        cost_estimate=pl.CostEstimate(
            flops=2 * rows * depth * (qcols + kvcols),
            bytes_accessed=2 * depth * (qcols + kvcols),
            transcendentals=0,
        ),
        name="project",
    )(tokens, attn_gain.reshape(chunks, 1, part), w_query, w_keyval)
    gathered, after = spread_all(packed, chunks, index)

    span = reward_hidden.shape[1]
    tiled = direct and slots == chunks and span <= EXT // 4 * LANES
    reward_parts = pl.pallas_call(
        reward_kernel,
        in_specs=[ANY, ANY, VMEM, VMEM] + [ANY] * 0,
        out_specs=VMEM,
        out_shape=jax.ShapeDtypeStruct(
            (slots, EXT // 2, LANES) if tiled else (2 * slots, span), jnp.float32
        ),
        scratch_shapes=[
            pltpu.VMEM(reward_hidden.shape, reward_hidden.dtype),
            pltpu.SemaphoreType.DMA((slots,)),
        ],
        compiler_params=pltpu.CompilerParams(vmem_limit_bytes=8 * MIB),
        cost_estimate=pl.CostEstimate(
            flops=4 * reward_hidden.size,
            bytes_accessed=2 * reward_hidden.size,
            transcendentals=0,
        ),
        name="reward",
    )(after, reward_hidden, reward_gain[None], reward_head[None])

    def tile(values):
        values = values.reshape(chunks, -1)
        size = EXT // 4 * LANES
        return jnp.pad(values, ((0, 0), (0, size - values.shape[1]))).reshape(
            chunks, EXT // 4, LANES
        )

    if not tiled:
        reward_parts = jnp.concatenate(
            [tile(reward_parts[:slots]), tile(reward_parts[slots:])], axis=1
        )
    fresh = gathered
    if not direct:
        fresh = jnp.take(gathered[:, body:, :kvcols], index ^ jnp.arange(chunks), axis=0)
        fresh = fresh.transpose(1, 0, 2).reshape(rows, 2 * KVH, HD).transpose(1, 0, 2)
    queries = gathered
    if not direct:
        queries = (
            jnp.take(gathered[:, :body], index ^ jnp.arange(chunks), axis=0)
            .reshape(KVH, split, pages, heads * per_page, HD)
            .transpose(0, 2, 1, 3, 4)
            .reshape(KVH, pages * page_rows, HD)
        )

    big = pages * page_rows
    block = (big + EXT, HD)
    attended = pl.pallas_call(
        functools.partial(attend_kernel, pages, page_rows),
        in_specs=[SMEM] + [VMEM] * 4,
        out_specs=[VMEM] * (KVH if direct else 1),
        out_shape=(
            [jax.ShapeDtypeStruct(block, jnp.float32)] * KVH
            if direct
            else [jax.ShapeDtypeStruct((KVH,) + block, jnp.float32)]
        ),
        scratch_shapes=[
            pltpu.VMEM((pages, KVH * page_rows, KVH * HD), jnp.bfloat16),
            pltpu.VMEM((pages, KVH * page_rows, LANES // page_rows * HD), jnp.float32),
        ],
        compiler_params=pltpu.CompilerParams(vmem_limit_bytes=10 * MIB),
        cost_estimate=pl.CostEstimate(
            flops=4 * pages * width * KVH * HD * KVH * page_rows,
            bytes_accessed=4 * pages * width * KVH * HD,
            transcendentals=pages * width * KVH * page_rows,
        ),
        name="attend",
    )(meta, queries, cache_keys, cache_values, reward_parts)
    if not direct:
        acc = (
            attended[0][:, :big]
            .reshape(KVH, pages, split, heads * per_page, HD)
            .transpose(0, 2, 1, 3, 4)
            .reshape(chunks, body, HD)
        )
        extra = attended[0][:, big : big + 2].reshape(KVH, 2, pages, split, heads * per_page)
        extra = extra.transpose(0, 3, 1, 2, 4).reshape(chunks, 2, body)
        extra = jnp.pad(extra, ((0, 0), (0, 2), (0, LANES - body)))
        attended = [jnp.concatenate([acc, extra, reward_parts], axis=1)]
    parts = trade(attended, chunks)

    chunk_rows = part // LANES * rows + EXT
    partial = pl.pallas_call(
        functools.partial(merge_kernel, pages, per_page, depth, span, slots, chunks),
        in_specs=[VMEM] * (3 + len(parts)),
        out_specs=[VMEM] * len(parts),
        out_shape=(
            [jax.ShapeDtypeStruct((chunk_rows, LANES), jnp.float32)] * chunks
            if direct
            else [jax.ShapeDtypeStruct((chunks, chunk_rows, LANES), jnp.float32)]
        ),
        scratch_shapes=[pltpu.VMEM((rows, qcols), jnp.bfloat16)],
        compiler_params=pltpu.CompilerParams(vmem_limit_bytes=8 * MIB),
        cost_estimate=pl.CostEstimate(
            flops=2 * rows * qcols * depth, bytes_accessed=2 * qcols * depth, transcendentals=0
        ),
        name="merge",
    )(packed, fresh, w_out, *parts)
    partial = trade(partial, chunks)

    decoded, reward = pl.pallas_call(
        functools.partial(sum_kernel, rows),
        out_shape=(
            jax.ShapeDtypeStruct((rows, part), jnp.bfloat16),
            jax.ShapeDtypeStruct((EXT, LANES), jnp.float32),
        ),
        compiler_params=pltpu.CompilerParams(vmem_limit_bytes=8 * MIB),
        name="total",
    )(*partial)
    far = lax.ppermute(decoded, "dp", swap)
    decoded = dot(give, jnp.concatenate([decoded, far], axis=0)).astype(jnp.bfloat16)
    return (reward[:slots, 0], decoded.reshape(STEPS, slots, part))


def solution(mesh):
    chunks = mesh.shape["tensor"]

    def body(*arrays):
        return local(chunks, *arrays)

    return jax.shard_map(
        body,
        mesh=mesh,
        in_specs=(
            P(("groups", "dp"), None, "tensor"),
            P("tensor"),
            P("tensor"),
            P(None, ("groups", "dp"), "tensor"),
            P(),
            P(None, "tensor"),
            P(None, "tensor"),
            P("tensor", None),
            P(("groups", "dp"), "tensor", None),
            P(("groups", "dp"), "tensor", None),
            P("groups"),
            P("groups"),
        ),
        out_specs=(P(("groups", "dp")), P(None, ("groups", "dp"), "tensor")),
        check_vma=False,
    )
```

```python
import functools

import jax
import jax.numpy as jnp
from jax import lax
from jax.experimental import pallas as pl
from jax.experimental.pallas import tpu as pltpu
from jax.sharding import PartitionSpec as P


HD = 128
KVH = 8
STEPS = 2
PAIR = 2
LANES = 128
EXT = 8
EPS = 1e-05
NEG = -1e30
SCALE = HD ** (-0.5)
NT = (((1,), (1,)), ((), ()))
TN = (((0,), (0,)), ((), ()))
MIB = 1 << 20
ANY = pl.BlockSpec(memory_space=pl.ANY)
VMEM = pl.BlockSpec(memory_space=pltpu.VMEM)
SMEM = pl.BlockSpec(memory_space=pltpu.SMEM)


def iota(shape, dim):
    return lax.broadcasted_iota(jnp.int32, shape, dim)


def dot(a, b, dims=(((1,), (0,)), ((), ()))):
    return lax.dot_general(a, b, dims, preferred_element_type=jnp.float32)


def head_major(shape, pages, per_page, heads):
    o, s = iota(shape, 0), iota(shape, 1)
    row = o % per_page
    head = (o // per_page) % heads
    page = o // (per_page * heads)
    return (s == (head * pages + page) * per_page + row).astype(jnp.bfloat16)


def aligned(index, size):
    return pl.ds(pl.multiple_of(index * size, size), size)


def early_kernel(*refs):
    refs[-1][...] = jnp.zeros_like(refs[-1])


def plan_kernel(slots, steps, map_ref, length_ref, meta_ref, take_ref, give_ref, before_ref, place_ref):
    count = map_ref.shape[0]
    mine = lax.axis_index("dp")
    base = mine * slots
    for block in range(count // slots):
        found = jnp.int32(0)
        for s in range(block * slots, (block + 1) * slots):
            before_ref[s] = found
            found = found + (map_ref[s] == s).astype(jnp.int32)
    for s in range(slots):
        own = map_ref[base + s] == base + s

        @pl.when(own)
        def _():
            slot = before_ref[base + s]
            meta_ref[slot] = jnp.int32(s)
            meta_ref[slots // PAIR + slot] = length_ref[base + s]

    for r in range(count):
        source = map_ref[r]
        place_ref[r] = (
            lax.div(source, slots) * slots
            + PAIR * before_ref[source]
            + (source != r).astype(jnp.int32)
        )
    rows = slots * steps
    line, col = iota((rows, 2 * rows), 0), iota((rows, 2 * rows), 1)
    same = line % steps == (col // slots) % steps
    take = jnp.zeros((rows, 2 * rows), jnp.bool_)
    give = jnp.zeros((rows, 2 * rows), jnp.bool_)
    for side in range(2):
        start = base if side == 0 else (1 - mine) * slots
        for s in range(slots):
            target = place_ref[start + s] - base
            column = (col // rows == side) & (col % slots == s)
            take = take | (same & column & (line // steps == target))
    for s in range(slots):
        place = place_ref[base + s]
        far = (lax.div(place, slots) != mine).astype(jnp.int32)
        target = far * rows + lax.rem(place, slots) * steps
        give = give | ((line % slots == s) & (col == line // slots + target))
    take_ref[...] = take.astype(jnp.float32).astype(jnp.bfloat16)
    give_ref[...] = give.astype(jnp.float32).astype(jnp.bfloat16)


def reward_kernel(after_ref, hidden_ref, gain_ref, head_ref, *rest):
    out_ref, buffer, sems = rest[-3:]
    slots = hidden_ref.shape[0]
    loads = [
        pltpu.make_async_copy(hidden_ref.at[s], buffer.at[s], sems.at[s]) for s in range(slots)
    ]
    for load in loads:
        load.start()
    weight = gain_ref[...] * head_ref[...]
    for s in range(slots):
        loads[s].wait()
        hidden = buffer[s].astype(jnp.float32)
        for half, value in enumerate((hidden * hidden, hidden * weight)):
            sums = jnp.sum(value, axis=-1)
            if len(out_ref.shape) == 2:
                out_ref[half * slots + s] = sums
                continue
            for c in range(EXT // 4):
                piece = jnp.zeros((LANES,), jnp.float32)
                if c < sums.shape[0] // LANES:
                    piece = sums[c * LANES : (c + 1) * LANES]
                out_ref[s, half * (EXT // 4) + c] = piece


def choose_kernel(after_ref, take_ref, own_ref, far_ref, near_ref, both_ref, out_ref):
    for w, (a, b) in enumerate(((own_ref, far_ref), (near_ref, both_ref))):
        rows = jnp.concatenate([a[...], b[...]], axis=0)
        out_ref[w] = dot(take_ref[...], rows).astype(jnp.bfloat16)


def project_kernel(pages, per_page, width, x_ref, gain_ref, wq_ref, wkv_ref, out_ref):
    me = lax.axis_index("tensor")
    chunks, rows, depth = x_ref.shape
    total = jnp.zeros((rows, depth), jnp.float32)
    for r in range(chunks):
        part = x_ref[r].astype(jnp.float32)
        total = total + part * part
    inv = lax.rsqrt(jnp.sum(total, axis=-1, keepdims=True) / width + EPS)

    query = jnp.zeros((rows, wq_ref.shape[1]), jnp.float32)
    keyval = jnp.zeros((rows, wkv_ref.shape[1]), jnp.float32)
    for r in range(chunks):
        normed = (x_ref[r].astype(jnp.float32) * inv * gain_ref[me ^ r]).astype(jnp.bfloat16)
        query = query + dot(normed, wq_ref[aligned(me ^ r, depth), :])
        keyval = keyval + dot(normed, wkv_ref[aligned(me ^ r, depth), :])

    heads = query.shape[1] // HD
    query = query.astype(jnp.bfloat16)
    stacked = jnp.concatenate([query[:, h * HD : (h + 1) * HD] for h in range(heads)], axis=0)
    order = head_major((rows * heads, rows * heads), pages, per_page, heads)
    body = rows * heads
    out_ref[:body] = dot(order, stacked).astype(jnp.bfloat16)
    keyval = keyval.astype(jnp.bfloat16)
    columns = keyval.shape[1]
    if columns < LANES:
        pad = jnp.zeros((rows, LANES - columns), jnp.bfloat16)
        keyval = jnp.concatenate([keyval, pad], axis=1)
    for v in range(keyval.shape[1] // LANES):
        out_ref[body + v * rows : body + (v + 1) * rows] = keyval[:, v * LANES : (v + 1) * LANES]


def attend_kernel(pages, page_rows, meta_ref, q_ref, k_ref, v_ref, reward_ref, *rest):
    outs, (spread, product) = rest[:-2], rest[-2:]
    width = k_ref.shape[1]
    span = KVH * page_rows
    body = pages * page_rows
    first = lax.axis_index("tensor") * width
    me = lax.axis_index("tensor") if len(outs) > 1 else 0
    spread[...] = jnp.zeros_like(spread)
    share = LANES // page_rows
    tops, totals = [], []
    for i in range(pages):
        for r in range(KVH):
            spread[r * page_rows : (r + 1) * page_rows, aligned(me ^ r, HD)] = q_ref[
                r, i * page_rows : (i + 1) * page_rows, :
            ]
        scores = dot(k_ref[meta_ref[i]], spread[...], NT) * SCALE
        valid = first + iota((width, span), 0) < meta_ref[pages + i]
        scores = jnp.where(valid, scores, NEG)
        top = jnp.max(scores, axis=0, keepdims=True)
        expo = jnp.where(valid, jnp.exp(scores - top), 0.0)
        total = jnp.sum(expo, axis=0, keepdims=True)
        weights = expo.astype(jnp.bfloat16)
        for part in range(KVH // share):
            values = v_ref[meta_ref[i], :, aligned(part ^ lax.div(me, share), share * HD)]
            lines = slice(part * share * page_rows, (part + 1) * share * page_rows)
            product[lines] = dot(weights[:, lines], values, TN)
        for r in range(KVH):
            out = outs[r] if len(outs) > 1 else outs[0].at[r]
            out[i * page_rows : (i + 1) * page_rows, :] = product[
                r * page_rows : (r + 1) * page_rows, aligned((me ^ r) & (share - 1), HD)
            ]
        tops.append(top)
        totals.append(total)
    held = iota((1, LANES), 1) // page_rows
    stats = []
    for part in range(KVH // share):
        lanes = slice(part * LANES, (part + 1) * LANES)
        tile = jnp.concatenate([x[:, lanes] for x in tops + totals], axis=0)
        turned = [tile] + [pltpu.roll(tile, t * page_rows, 1) for t in range(1, share)]
        for q in range(share):
            for skip in (0, pages):
                line = jnp.zeros((1, LANES), jnp.float32)
                for i in range(pages):
                    row = turned[(i - q) % share][skip + i : skip + i + 1]
                    line = jnp.where(held == i, row, line)
                stats.append(line)
    for r in range(KVH):
        out = outs[r] if len(outs) > 1 else outs[0].at[r]
        out[body : body + 2, :] = jnp.concatenate(stats[2 * r : 2 * r + 2], axis=0)
        if len(outs) > 1:
            out[body + 2 : body + 4, :] = jnp.zeros((2, LANES), jnp.float32)
            out[body + 4 :, :] = reward_ref[me ^ r]
        else:
            out[body + 2 :, :] = jnp.zeros((EXT - 2, LANES), jnp.float32)


def merge_kernel(pages, per_page, width, span, slots, chunks, q_ref, gathered_ref, w_ref, *rest):
    att = rest[-1]
    split = len(rest) > 3
    parts = rest[:chunks] if split else [rest[0].at[b] for b in range(chunks)]
    outs = rest[chunks:-1] if split else rest[1:-1]
    me = lax.axis_index("tensor")
    body = parts[0].shape[0] - EXT
    page_rows = body // pages
    heads = page_rows // per_page
    rows = pages * per_page

    kv_head = lax.div(me * heads, heads * chunks // KVH)
    if split:
        pieces = (gathered_ref.shape[1] - body) // rows

        def fresh_of(column):
            source = lax.div(column, pieces) ^ me
            start = pl.multiple_of(body + lax.rem(column, pieces) * rows, rows)
            return gathered_ref[source, pl.ds(start, rows), :]

        fresh_k, fresh_v = fresh_of(kv_head), fresh_of(KVH + kv_head)
    else:
        fresh_k, fresh_v = gathered_ref[kv_head], gathered_ref[KVH + kv_head]

    query = q_ref[:body, :]
    recent = dot(query, fresh_k, NT) * SCALE
    line, col = iota(recent.shape, 0), iota(recent.shape, 1)
    mine = (line // page_rows) * per_page + line % per_page
    seen = (mine // STEPS == col // STEPS) & (col <= mine)
    recent = jnp.where(seen, recent, NEG)
    recent_max = jnp.max(recent, axis=-1, keepdims=True)
    recent_exp = jnp.where(seen, jnp.exp(recent - recent_max), 0.0)
    recent_total = jnp.sum(recent_exp, axis=-1, keepdims=True)
    recent_acc = dot(recent_exp.astype(jnp.bfloat16), fresh_v)

    maxima = [parts[b][body : body + 1, :] for b in range(chunks)]
    totals = [parts[b][body + 1 : body + 2, :] for b in range(chunks)]
    top = functools.reduce(jnp.maximum, maxima)
    factors = [jnp.exp(m - top) for m in maxima]
    total = functools.reduce(jnp.add, [f * t for f, t in zip(factors, totals)])

    pick = iota((body, LANES), 0) == iota((body, LANES), 1)

    def column(packed):
        wide = jnp.where(pick, jnp.broadcast_to(packed, pick.shape), 0.0)
        return jnp.sum(wide, axis=-1, keepdims=True)

    acc = jnp.zeros((body, HD), jnp.float32)
    for b in range(chunks):
        acc = acc + column(factors[b]) * parts[b][:body, :]
    cache_top, cache_total = column(top), column(total)
    top = jnp.maximum(cache_top, recent_max)
    cache_factor = jnp.exp(cache_top - top)
    recent_factor = jnp.exp(recent_max - top)
    total = cache_factor * cache_total + recent_factor * recent_total
    acc = cache_factor * acc + recent_factor * recent_acc
    attended = (acc / total).astype(jnp.bfloat16)
    order = head_major((body, body), pages, per_page, heads)
    attended = dot(order, attended, TN).astype(jnp.bfloat16)
    for h in range(heads):
        att[:, h * HD : (h + 1) * HD] = attended[h * rows : (h + 1) * rows]

    tile = functools.reduce(jnp.add, [parts[b][body + EXT // 2 :, :] for b in range(chunks)])
    used = EXT // 4
    value = tile[used:] * lax.rsqrt(tile[:used] / width + EPS)
    mean = jnp.sum(value, keepdims=True) / span
    own = lax.div(me * (slots * span // chunks), span)
    mean = jnp.where(iota((EXT, LANES), 0) == own, mean, 0.0)

    part = w_ref.shape[1] // chunks
    for r in range(chunks):
        out = outs[r] if split else outs[0].at[me ^ r]
        product = dot(att[...], w_ref[:, aligned(me ^ r, part)])
        for c in range(part // LANES):
            out[c * rows : (c + 1) * rows, :] = product[:, c * LANES : (c + 1) * LANES]
        out[out.shape[0] - EXT :, :] = mean


def sum_kernel(rows, *refs):
    parts, (out_ref, reward_ref) = refs[:-2], refs[-2:]
    if len(parts) == 1:
        parts = [parts[0].at[b] for b in range(parts[0].shape[0])]
    total = parts[0][...]
    for part in parts[1:]:
        total = total + part[...]
    for c in range(out_ref.shape[1] // LANES):
        out_ref[:, c * LANES : (c + 1) * LANES] = total[c * rows : (c + 1) * rows].astype(
            jnp.bfloat16
        )
    reward_ref[...] = total[total.shape[0] - EXT :]


LINE = (6, 2, 4)
ALL = (6, 1, 7, 2, 5, 3, 4)


def partner(x, chunks, bits):
    return lax.ppermute(x, "tensor", [(i, i ^ bits) for i in range(chunks)])


def spread_line(pair, chunks):
    others = {bits: partner(pair, chunks, bits) for bits in LINE}
    stacked = jnp.stack([pair] + [others[bits] for bits in sorted(LINE)])
    return stacked.reshape((chunks,) + pair.shape[1:])


def spread_all(x, chunks, index):
    if chunks != KVH:
        every = jnp.broadcast_to(x[None], (chunks,) + x.shape)
        every = lax.all_to_all(every, "tensor", 0, 0, tiled=True)
        return jnp.take(every, index ^ jnp.arange(chunks), axis=0), x
    pair = jnp.stack([x, partner(x, chunks, 1)])
    return spread_line(pair, chunks), pair


def trade(blocks, chunks):
    if len(blocks) == 1:
        return [lax.all_to_all(blocks[0], "tensor", 0, 0, tiled=True)]
    traded = {bits: partner(blocks[bits], chunks, bits) for bits in ALL}
    return [blocks[0]] + [traded[bits] for bits in range(1, chunks)]


def local(
    chunks,
    reward_hidden,
    reward_gain,
    reward_head,
    decode_inputs,
    attn_gain,
    w_query,
    w_keyval,
    w_out,
    cache_keys,
    cache_values,
    lengths,
    slot_map,
):
    slots, width = cache_keys.shape[:2]
    depth, qcols = w_query.shape
    kvcols = w_keyval.shape[1]
    part = decode_inputs.shape[-1]
    heads = qcols // HD
    group = heads * chunks // KVH
    split = group // heads
    pages = slots // PAIR
    per_page = PAIR * STEPS
    page_rows = per_page * group
    rows = slots * STEPS
    body = rows * heads
    index = lax.axis_index("tensor")
    swap = [(0, 1), (1, 0)]
    direct = chunks == KVH

    meta, take, give = pl.pallas_call(
        functools.partial(plan_kernel, slots, STEPS),
        in_specs=[SMEM, SMEM],
        out_specs=[SMEM, VMEM, VMEM],
        out_shape=(
            jax.ShapeDtypeStruct((2 * pages,), jnp.int32),
            jax.ShapeDtypeStruct((rows, 2 * rows), jnp.bfloat16),
            jax.ShapeDtypeStruct((rows, 2 * rows), jnp.bfloat16),
        ),
        scratch_shapes=[
            pltpu.SMEM(slot_map.shape, jnp.int32),
            pltpu.SMEM(slot_map.shape, jnp.int32),
        ],
        compiler_params=pltpu.CompilerParams(vmem_limit_bytes=MIB),
        name="plan",
    )(slot_map, lengths)

    early = pl.pallas_call(
        early_kernel,
        in_specs=[ANY] * 3,
        out_specs=VMEM,
        out_shape=jax.ShapeDtypeStruct((EXT, LANES), jnp.float32),
        compiler_params=pltpu.CompilerParams(vmem_limit_bytes=38 * MIB),
        name="early",
    )(w_out, w_out, w_out)
    own = decode_inputs.reshape(rows, part)
    far = lax.ppermute(own, "dp", swap)
    if direct:
        near = partner(own, chunks, 1)
        cross = [
            (d * chunks + t, (1 - d) * chunks + (t ^ 1)) for d in range(2) for t in range(chunks)
        ]
        both = lax.ppermute(own, ("dp", "tensor"), cross)
        pair = pl.pallas_call(
            choose_kernel,
            in_specs=[ANY] + [VMEM] * 5,
            out_specs=VMEM,
            out_shape=jax.ShapeDtypeStruct((2, rows, part), jnp.bfloat16),
            compiler_params=pltpu.CompilerParams(vmem_limit_bytes=MIB),
            name="choose",
        )(early, take, own, far, near, both)
        tokens = spread_line(pair, chunks)
    else:
        chosen = dot(take, jnp.concatenate([own, far], axis=0)).astype(jnp.bfloat16)
        tokens, _ = spread_all(chosen, chunks, index)

    pieces = max(kvcols // LANES, 1)
    packed_rows = body + pieces * rows
    packed = pl.pallas_call(
        functools.partial(project_kernel, pages, per_page, depth),
        in_specs=[VMEM] * 4,
        out_specs=VMEM,
        out_shape=jax.ShapeDtypeStruct((packed_rows, LANES), jnp.bfloat16),
        compiler_params=pltpu.CompilerParams(vmem_limit_bytes=4 * MIB),
        cost_estimate=pl.CostEstimate(
            flops=2 * rows * depth * (qcols + kvcols),
            bytes_accessed=2 * depth * (qcols + kvcols),
            transcendentals=0,
        ),
        name="project",
    )(tokens, attn_gain.reshape(chunks, 1, part), w_query, w_keyval)
    gathered, after = spread_all(packed, chunks, index)

    span = reward_hidden.shape[1]
    tiled = direct and slots == chunks and span <= EXT // 4 * LANES
    reward_parts = pl.pallas_call(
        reward_kernel,
        in_specs=[ANY, ANY, VMEM, VMEM] + [ANY] * 0,
        out_specs=VMEM,
        out_shape=jax.ShapeDtypeStruct(
            (slots, EXT // 2, LANES) if tiled else (2 * slots, span), jnp.float32
        ),
        scratch_shapes=[
            pltpu.VMEM(reward_hidden.shape, reward_hidden.dtype),
            pltpu.SemaphoreType.DMA((slots,)),
        ],
        compiler_params=pltpu.CompilerParams(vmem_limit_bytes=8 * MIB),
        cost_estimate=pl.CostEstimate(
            flops=4 * reward_hidden.size,
            bytes_accessed=2 * reward_hidden.size,
            transcendentals=0,
        ),
        name="reward",
    )(after, reward_hidden, reward_gain[None], reward_head[None])

    def tile(values):
        values = values.reshape(chunks, -1)
        size = EXT // 4 * LANES
        return jnp.pad(values, ((0, 0), (0, size - values.shape[1]))).reshape(
            chunks, EXT // 4, LANES
        )

    if not tiled:
        reward_parts = jnp.concatenate(
            [tile(reward_parts[:slots]), tile(reward_parts[slots:])], axis=1
        )
    fresh = gathered
    if not direct:
        fresh = jnp.take(gathered[:, body:, :kvcols], index ^ jnp.arange(chunks), axis=0)
        fresh = fresh.transpose(1, 0, 2).reshape(rows, 2 * KVH, HD).transpose(1, 0, 2)
    queries = gathered
    if not direct:
        queries = (
            jnp.take(gathered[:, :body], index ^ jnp.arange(chunks), axis=0)
            .reshape(KVH, split, pages, heads * per_page, HD)
            .transpose(0, 2, 1, 3, 4)
            .reshape(KVH, pages * page_rows, HD)
        )

    big = pages * page_rows
    block = (big + EXT, HD)
    attended = pl.pallas_call(
        functools.partial(attend_kernel, pages, page_rows),
        in_specs=[SMEM] + [VMEM] * 4,
        out_specs=[VMEM] * (KVH if direct else 1),
        out_shape=(
            [jax.ShapeDtypeStruct(block, jnp.float32)] * KVH
            if direct
            else [jax.ShapeDtypeStruct((KVH,) + block, jnp.float32)]
        ),
        scratch_shapes=[
            pltpu.VMEM((KVH * page_rows, KVH * HD), jnp.bfloat16),
            pltpu.VMEM((KVH * page_rows, LANES // page_rows * HD), jnp.float32),
        ],
        compiler_params=pltpu.CompilerParams(vmem_limit_bytes=6 * MIB),
        cost_estimate=pl.CostEstimate(
            flops=4 * pages * width * KVH * HD * KVH * page_rows,
            bytes_accessed=4 * pages * width * KVH * HD,
            transcendentals=pages * width * KVH * page_rows,
        ),
        name="attend",
    )(meta, queries, cache_keys, cache_values, reward_parts)
    if not direct:
        acc = (
            attended[0][:, :big]
            .reshape(KVH, pages, split, heads * per_page, HD)
            .transpose(0, 2, 1, 3, 4)
            .reshape(chunks, body, HD)
        )
        extra = attended[0][:, big : big + 2].reshape(KVH, 2, pages, split, heads * per_page)
        extra = extra.transpose(0, 3, 1, 2, 4).reshape(chunks, 2, body)
        extra = jnp.pad(extra, ((0, 0), (0, 2), (0, LANES - body)))
        attended = [jnp.concatenate([acc, extra, reward_parts], axis=1)]
    parts = trade(attended, chunks)

    chunk_rows = part // LANES * rows + EXT
    partial = pl.pallas_call(
        functools.partial(merge_kernel, pages, per_page, depth, span, slots, chunks),
        in_specs=[VMEM] * (3 + len(parts)),
        out_specs=[VMEM] * len(parts),
        out_shape=(
            [jax.ShapeDtypeStruct((chunk_rows, LANES), jnp.float32)] * chunks
            if direct
            else [jax.ShapeDtypeStruct((chunks, chunk_rows, LANES), jnp.float32)]
        ),
        scratch_shapes=[pltpu.VMEM((rows, qcols), jnp.bfloat16)],
        compiler_params=pltpu.CompilerParams(vmem_limit_bytes=8 * MIB),
        cost_estimate=pl.CostEstimate(
            flops=2 * rows * qcols * depth, bytes_accessed=2 * qcols * depth, transcendentals=0
        ),
        name="merge",
    )(packed, fresh, w_out, *parts)
    partial = trade(partial, chunks)

    decoded, reward = pl.pallas_call(
        functools.partial(sum_kernel, rows),
        out_shape=(
            jax.ShapeDtypeStruct((rows, part), jnp.bfloat16),
            jax.ShapeDtypeStruct((EXT, LANES), jnp.float32),
        ),
        compiler_params=pltpu.CompilerParams(vmem_limit_bytes=8 * MIB),
        name="total",
    )(*partial)
    far = lax.ppermute(decoded, "dp", swap)
    decoded = dot(give, jnp.concatenate([decoded, far], axis=0)).astype(jnp.bfloat16)
    return (reward[:slots, 0], decoded.reshape(STEPS, slots, part))


def solution(mesh):
    chunks = mesh.shape["tensor"]

    def body(*arrays):
        return local(chunks, *arrays)

    return jax.shard_map(
        body,
        mesh=mesh,
        in_specs=(
            P(("groups", "dp"), None, "tensor"),
            P("tensor"),
            P("tensor"),
            P(None, ("groups", "dp"), "tensor"),
            P(),
            P(None, "tensor"),
            P(None, "tensor"),
            P("tensor", None),
            P(("groups", "dp"), "tensor", None),
            P(("groups", "dp"), "tensor", None),
            P("groups"),
            P("groups"),
        ),
        out_specs=(P(("groups", "dp")), P(None, ("groups", "dp"), "tensor")),
        check_vma=False,
    )
```

```python
import functools

import jax
import jax.numpy as jnp
from jax import lax
from jax.experimental import pallas as pl
from jax.experimental.pallas import tpu as pltpu
from jax.sharding import PartitionSpec as P


HD = 128
KVH = 8
STEPS = 2
PAIR = 2
LANES = 128
EXT = 8
EPS = 1e-05
NEG = -1e30
SCALE = HD ** (-0.5)
NT = (((1,), (1,)), ((), ()))
TN = (((0,), (0,)), ((), ()))
MIB = 1 << 20
ANY = pl.BlockSpec(memory_space=pl.ANY)
VMEM = pl.BlockSpec(memory_space=pltpu.VMEM)
SMEM = pl.BlockSpec(memory_space=pltpu.SMEM)


def iota(shape, dim):
    return lax.broadcasted_iota(jnp.int32, shape, dim)


def dot(a, b, dims=(((1,), (0,)), ((), ()))):
    return lax.dot_general(a, b, dims, preferred_element_type=jnp.float32)


def head_major(shape, pages, per_page, heads):
    o, s = iota(shape, 0), iota(shape, 1)
    row = o % per_page
    head = (o // per_page) % heads
    page = o // (per_page * heads)
    return (s == (head * pages + page) * per_page + row).astype(jnp.bfloat16)


def aligned(index, size):
    return pl.ds(pl.multiple_of(index * size, size), size)


def early_kernel(*refs):
    refs[-1][...] = jnp.zeros_like(refs[-1])


def plan_kernel(slots, steps, map_ref, length_ref, meta_ref, take_ref, give_ref, before_ref, place_ref):
    count = map_ref.shape[0]
    mine = lax.axis_index("dp")
    base = mine * slots
    for block in range(count // slots):
        found = jnp.int32(0)
        for s in range(block * slots, (block + 1) * slots):
            before_ref[s] = found
            found = found + (map_ref[s] == s).astype(jnp.int32)
    for s in range(slots):
        own = map_ref[base + s] == base + s

        @pl.when(own)
        def _():
            slot = before_ref[base + s]
            meta_ref[slot] = jnp.int32(s)
            meta_ref[slots // PAIR + slot] = length_ref[base + s]

    for r in range(count):
        source = map_ref[r]
        place_ref[r] = (
            lax.div(source, slots) * slots
            + PAIR * before_ref[source]
            + (source != r).astype(jnp.int32)
        )
    rows = slots * steps
    line, col = iota((rows, 2 * rows), 0), iota((rows, 2 * rows), 1)
    same = line % steps == (col // slots) % steps
    take = jnp.zeros((rows, 2 * rows), jnp.bool_)
    give = jnp.zeros((rows, 2 * rows), jnp.bool_)
    for side in range(2):
        start = base if side == 0 else (1 - mine) * slots
        for s in range(slots):
            target = place_ref[start + s] - base
            column = (col // rows == side) & (col % slots == s)
            take = take | (same & column & (line // steps == target))
    for s in range(slots):
        place = place_ref[base + s]
        far = (lax.div(place, slots) != mine).astype(jnp.int32)
        target = far * rows + lax.rem(place, slots) * steps
        give = give | ((line % slots == s) & (col == line // slots + target))
    take_ref[...] = take.astype(jnp.float32).astype(jnp.bfloat16)
    give_ref[...] = give.astype(jnp.float32).astype(jnp.bfloat16)


def reward_kernel(after_ref, hidden_ref, gain_ref, head_ref, *rest):
    out_ref, buffer, sems = rest[-3:]
    slots = hidden_ref.shape[0]
    loads = [
        pltpu.make_async_copy(hidden_ref.at[s], buffer.at[s], sems.at[s]) for s in range(slots)
    ]
    for load in loads:
        load.start()
    weight = gain_ref[...] * head_ref[...]
    for s in range(slots):
        loads[s].wait()
        hidden = buffer[s].astype(jnp.float32)
        for half, value in enumerate((hidden * hidden, hidden * weight)):
            sums = jnp.sum(value, axis=-1)
            if len(out_ref.shape) == 2:
                out_ref[half * slots + s] = sums
                continue
            for c in range(EXT // 4):
                piece = jnp.zeros((LANES,), jnp.float32)
                if c < sums.shape[0] // LANES:
                    piece = sums[c * LANES : (c + 1) * LANES]
                out_ref[s, half * (EXT // 4) + c] = piece


def choose_kernel(after_ref, take_ref, own_ref, far_ref, near_ref, both_ref, out_ref):
    for w, (a, b) in enumerate(((own_ref, far_ref), (near_ref, both_ref))):
        rows = jnp.concatenate([a[...], b[...]], axis=0)
        out_ref[w] = dot(take_ref[...], rows).astype(jnp.bfloat16)


def project_kernel(pages, per_page, width, x_ref, gain_ref, wq_ref, wkv_ref, out_ref):
    me = lax.axis_index("tensor")
    chunks, rows, depth = x_ref.shape
    total = jnp.zeros((rows, depth), jnp.float32)
    for r in range(chunks):
        part = x_ref[r].astype(jnp.float32)
        total = total + part * part
    inv = lax.rsqrt(jnp.sum(total, axis=-1, keepdims=True) / width + EPS)

    query = jnp.zeros((rows, wq_ref.shape[1]), jnp.float32)
    keyval = jnp.zeros((rows, wkv_ref.shape[1]), jnp.float32)
    for r in range(chunks):
        normed = (x_ref[r].astype(jnp.float32) * inv * gain_ref[me ^ r]).astype(jnp.bfloat16)
        query = query + dot(normed, wq_ref[aligned(me ^ r, depth), :])
        keyval = keyval + dot(normed, wkv_ref[aligned(me ^ r, depth), :])

    heads = query.shape[1] // HD
    query = query.astype(jnp.bfloat16)
    stacked = jnp.concatenate([query[:, h * HD : (h + 1) * HD] for h in range(heads)], axis=0)
    order = head_major((rows * heads, rows * heads), pages, per_page, heads)
    body = rows * heads
    out_ref[:body] = dot(order, stacked).astype(jnp.bfloat16)
    keyval = keyval.astype(jnp.bfloat16)
    columns = keyval.shape[1]
    if columns < LANES:
        pad = jnp.zeros((rows, LANES - columns), jnp.bfloat16)
        keyval = jnp.concatenate([keyval, pad], axis=1)
    for v in range(keyval.shape[1] // LANES):
        out_ref[body + v * rows : body + (v + 1) * rows] = keyval[:, v * LANES : (v + 1) * LANES]


def attend_kernel(pages, page_rows, meta_ref, q_ref, k_ref, v_ref, reward_ref, *rest):
    outs, (spread, product) = rest[:-2], rest[-2:]
    width = k_ref.shape[1]
    span = KVH * page_rows
    body = pages * page_rows
    first = lax.axis_index("tensor") * width
    me = lax.axis_index("tensor") if len(outs) > 1 else 0
    spread[...] = jnp.zeros_like(spread)
    share = LANES // page_rows
    stats = [[jnp.zeros((1, LANES), jnp.float32)] * 2 for _ in range(KVH)]
    for i in range(pages):
        for r in range(KVH):
            spread[r * page_rows : (r + 1) * page_rows, aligned(me ^ r, HD)] = q_ref[
                r, i * page_rows : (i + 1) * page_rows, :
            ]
        scores = dot(k_ref[meta_ref[i]], spread[...], NT) * SCALE
        valid = first + iota((width, span), 0) < meta_ref[pages + i]
        scores = jnp.where(valid, scores, NEG)
        top = jnp.max(scores, axis=0, keepdims=True)
        expo = jnp.where(valid, jnp.exp(scores - top), 0.0)
        total = jnp.sum(expo, axis=0, keepdims=True)
        weights = expo.astype(jnp.bfloat16)
        for part in range(KVH // share):
            values = v_ref[meta_ref[i], :, aligned(part ^ lax.div(me, share), share * HD)]
            lines = slice(part * share * page_rows, (part + 1) * share * page_rows)
            product[lines] = dot(weights[:, lines], values, TN)
        for r in range(KVH):
            out = outs[r] if len(outs) > 1 else outs[0].at[r]
            out[i * page_rows : (i + 1) * page_rows, :] = product[
                r * page_rows : (r + 1) * page_rows, aligned((me ^ r) & (share - 1), HD)
            ]
            start = r * page_rows
            lane = start // LANES * LANES
            shift = (i * page_rows - start) % LANES
            mask = iota((1, LANES), 1) // page_rows == i
            for k, packed in enumerate((top, total)):
                packed = packed[:, lane : lane + LANES]
                if shift:
                    packed = pltpu.roll(packed, shift, 1)
                stats[r][k] = jnp.where(mask, packed, stats[r][k])
    for r in range(KVH):
        out = outs[r] if len(outs) > 1 else outs[0].at[r]
        out[body : body + 2, :] = jnp.concatenate(stats[r], axis=0)
        if len(outs) > 1:
            out[body + 2 : body + 4, :] = jnp.zeros((2, LANES), jnp.float32)
            out[body + 4 :, :] = reward_ref[me ^ r]
        else:
            out[body + 2 :, :] = jnp.zeros((EXT - 2, LANES), jnp.float32)


def merge_kernel(pages, per_page, width, span, slots, chunks, q_ref, gathered_ref, w_ref, *rest):
    att = rest[-1]
    split = len(rest) > 3
    parts = rest[:chunks] if split else [rest[0].at[b] for b in range(chunks)]
    outs = rest[chunks:-1] if split else rest[1:-1]
    me = lax.axis_index("tensor")
    body = parts[0].shape[0] - EXT
    page_rows = body // pages
    heads = page_rows // per_page
    rows = pages * per_page

    kv_head = lax.div(me * heads, heads * chunks // KVH)
    if split:
        pieces = (gathered_ref.shape[1] - body) // rows

        def fresh_of(column):
            source = lax.div(column, pieces) ^ me
            start = pl.multiple_of(body + lax.rem(column, pieces) * rows, rows)
            return gathered_ref[source, pl.ds(start, rows), :]

        fresh_k, fresh_v = fresh_of(kv_head), fresh_of(KVH + kv_head)
    else:
        fresh_k, fresh_v = gathered_ref[kv_head], gathered_ref[KVH + kv_head]

    query = q_ref[:body, :]
    recent = dot(query, fresh_k, NT) * SCALE
    line, col = iota(recent.shape, 0), iota(recent.shape, 1)
    mine = (line // page_rows) * per_page + line % per_page
    seen = (mine // STEPS == col // STEPS) & (col <= mine)
    recent = jnp.where(seen, recent, NEG)
    recent_max = jnp.max(recent, axis=-1, keepdims=True)
    recent_exp = jnp.where(seen, jnp.exp(recent - recent_max), 0.0)
    recent_total = jnp.sum(recent_exp, axis=-1, keepdims=True)
    recent_acc = dot(recent_exp.astype(jnp.bfloat16), fresh_v)

    maxima = [parts[b][body : body + 1, :] for b in range(chunks)]
    totals = [parts[b][body + 1 : body + 2, :] for b in range(chunks)]
    top = functools.reduce(jnp.maximum, maxima)
    factors = [jnp.exp(m - top) for m in maxima]
    total = functools.reduce(jnp.add, [f * t for f, t in zip(factors, totals)])

    pick = iota((body, LANES), 0) == iota((body, LANES), 1)

    def column(packed):
        wide = jnp.where(pick, jnp.broadcast_to(packed, pick.shape), 0.0)
        return jnp.sum(wide, axis=-1, keepdims=True)

    acc = jnp.zeros((body, HD), jnp.float32)
    for b in range(chunks):
        acc = acc + column(factors[b]) * parts[b][:body, :]
    cache_top, cache_total = column(top), column(total)
    top = jnp.maximum(cache_top, recent_max)
    cache_factor = jnp.exp(cache_top - top)
    recent_factor = jnp.exp(recent_max - top)
    total = cache_factor * cache_total + recent_factor * recent_total
    acc = cache_factor * acc + recent_factor * recent_acc
    attended = (acc / total).astype(jnp.bfloat16)
    order = head_major((body, body), pages, per_page, heads)
    attended = dot(order, attended, TN).astype(jnp.bfloat16)
    for h in range(heads):
        att[:, h * HD : (h + 1) * HD] = attended[h * rows : (h + 1) * rows]

    tile = functools.reduce(jnp.add, [parts[b][body + EXT // 2 :, :] for b in range(chunks)])
    used = EXT // 4
    value = tile[used:] * lax.rsqrt(tile[:used] / width + EPS)
    mean = jnp.sum(value, keepdims=True) / span
    own = lax.div(me * (slots * span // chunks), span)
    mean = jnp.where(iota((EXT, LANES), 0) == own, mean, 0.0)

    part = w_ref.shape[1] // chunks
    for r in range(chunks):
        out = outs[r] if split else outs[0].at[me ^ r]
        product = dot(att[...], w_ref[:, aligned(me ^ r, part)])
        for c in range(part // LANES):
            out[c * rows : (c + 1) * rows, :] = product[:, c * LANES : (c + 1) * LANES]
        out[out.shape[0] - EXT :, :] = mean


def sum_kernel(rows, *refs):
    parts, (out_ref, reward_ref) = refs[:-2], refs[-2:]
    if len(parts) == 1:
        parts = [parts[0].at[b] for b in range(parts[0].shape[0])]
    total = parts[0][...]
    for part in parts[1:]:
        total = total + part[...]
    for c in range(out_ref.shape[1] // LANES):
        out_ref[:, c * LANES : (c + 1) * LANES] = total[c * rows : (c + 1) * rows].astype(
            jnp.bfloat16
        )
    reward_ref[...] = total[total.shape[0] - EXT :]


LINE = (6, 2, 4)
ALL = (6, 1, 7, 2, 5, 3, 4)


def partner(x, chunks, bits):
    return lax.ppermute(x, "tensor", [(i, i ^ bits) for i in range(chunks)])


def spread_line(pair, chunks):
    others = {bits: partner(pair, chunks, bits) for bits in LINE}
    stacked = jnp.stack([pair] + [others[bits] for bits in sorted(LINE)])
    return stacked.reshape((chunks,) + pair.shape[1:])


def spread_all(x, chunks, index):
    if chunks != KVH:
        every = jnp.broadcast_to(x[None], (chunks,) + x.shape)
        every = lax.all_to_all(every, "tensor", 0, 0, tiled=True)
        return jnp.take(every, index ^ jnp.arange(chunks), axis=0), x
    pair = jnp.stack([x, partner(x, chunks, 1)])
    return spread_line(pair, chunks), pair


def trade(blocks, chunks):
    if len(blocks) == 1:
        return [lax.all_to_all(blocks[0], "tensor", 0, 0, tiled=True)]
    traded = {bits: partner(blocks[bits], chunks, bits) for bits in ALL}
    return [blocks[0]] + [traded[bits] for bits in range(1, chunks)]


def local(
    chunks,
    reward_hidden,
    reward_gain,
    reward_head,
    decode_inputs,
    attn_gain,
    w_query,
    w_keyval,
    w_out,
    cache_keys,
    cache_values,
    lengths,
    slot_map,
):
    slots, width = cache_keys.shape[:2]
    depth, qcols = w_query.shape
    kvcols = w_keyval.shape[1]
    part = decode_inputs.shape[-1]
    heads = qcols // HD
    group = heads * chunks // KVH
    split = group // heads
    pages = slots // PAIR
    per_page = PAIR * STEPS
    page_rows = per_page * group
    rows = slots * STEPS
    body = rows * heads
    index = lax.axis_index("tensor")
    swap = [(0, 1), (1, 0)]
    direct = chunks == KVH

    meta, take, give = pl.pallas_call(
        functools.partial(plan_kernel, slots, STEPS),
        in_specs=[SMEM, SMEM],
        out_specs=[SMEM, VMEM, VMEM],
        out_shape=(
            jax.ShapeDtypeStruct((2 * pages,), jnp.int32),
            jax.ShapeDtypeStruct((rows, 2 * rows), jnp.bfloat16),
            jax.ShapeDtypeStruct((rows, 2 * rows), jnp.bfloat16),
        ),
        scratch_shapes=[
            pltpu.SMEM(slot_map.shape, jnp.int32),
            pltpu.SMEM(slot_map.shape, jnp.int32),
        ],
        compiler_params=pltpu.CompilerParams(vmem_limit_bytes=MIB),
        name="plan",
    )(slot_map, lengths)

    early = pl.pallas_call(
        early_kernel,
        in_specs=[ANY] * 3,
        out_specs=VMEM,
        out_shape=jax.ShapeDtypeStruct((EXT, LANES), jnp.float32),
        compiler_params=pltpu.CompilerParams(vmem_limit_bytes=38 * MIB),
        name="early",
    )(w_out, w_out, w_out)
    own = decode_inputs.reshape(rows, part)
    far = lax.ppermute(own, "dp", swap)
    if direct:
        near = partner(own, chunks, 1)
        cross = [
            (d * chunks + t, (1 - d) * chunks + (t ^ 1)) for d in range(2) for t in range(chunks)
        ]
        both = lax.ppermute(own, ("dp", "tensor"), cross)
        pair = pl.pallas_call(
            choose_kernel,
            in_specs=[ANY] + [VMEM] * 5,
            out_specs=VMEM,
            out_shape=jax.ShapeDtypeStruct((2, rows, part), jnp.bfloat16),
            compiler_params=pltpu.CompilerParams(vmem_limit_bytes=MIB),
            name="choose",
        )(early, take, own, far, near, both)
        tokens = spread_line(pair, chunks)
    else:
        chosen = dot(take, jnp.concatenate([own, far], axis=0)).astype(jnp.bfloat16)
        tokens, _ = spread_all(chosen, chunks, index)

    pieces = max(kvcols // LANES, 1)
    packed_rows = body + pieces * rows
    packed = pl.pallas_call(
        functools.partial(project_kernel, pages, per_page, depth),
        in_specs=[VMEM] * 4,
        out_specs=VMEM,
        out_shape=jax.ShapeDtypeStruct((packed_rows, LANES), jnp.bfloat16),
        compiler_params=pltpu.CompilerParams(vmem_limit_bytes=4 * MIB),
        cost_estimate=pl.CostEstimate(
            flops=2 * rows * depth * (qcols + kvcols),
            bytes_accessed=2 * depth * (qcols + kvcols),
            transcendentals=0,
        ),
        name="project",
    )(tokens, attn_gain.reshape(chunks, 1, part), w_query, w_keyval)
    gathered, after = spread_all(packed, chunks, index)

    span = reward_hidden.shape[1]
    tiled = direct and slots == chunks and span <= EXT // 4 * LANES
    reward_parts = pl.pallas_call(
        reward_kernel,
        in_specs=[ANY, ANY, VMEM, VMEM] + [ANY] * 0,
        out_specs=VMEM,
        out_shape=jax.ShapeDtypeStruct(
            (slots, EXT // 2, LANES) if tiled else (2 * slots, span), jnp.float32
        ),
        scratch_shapes=[
            pltpu.VMEM(reward_hidden.shape, reward_hidden.dtype),
            pltpu.SemaphoreType.DMA((slots,)),
        ],
        compiler_params=pltpu.CompilerParams(vmem_limit_bytes=8 * MIB),
        cost_estimate=pl.CostEstimate(
            flops=4 * reward_hidden.size,
            bytes_accessed=2 * reward_hidden.size,
            transcendentals=0,
        ),
        name="reward",
    )(after, reward_hidden, reward_gain[None], reward_head[None])

    def tile(values):
        values = values.reshape(chunks, -1)
        size = EXT // 4 * LANES
        return jnp.pad(values, ((0, 0), (0, size - values.shape[1]))).reshape(
            chunks, EXT // 4, LANES
        )

    if not tiled:
        reward_parts = jnp.concatenate(
            [tile(reward_parts[:slots]), tile(reward_parts[slots:])], axis=1
        )
    fresh = gathered
    if not direct:
        fresh = jnp.take(gathered[:, body:, :kvcols], index ^ jnp.arange(chunks), axis=0)
        fresh = fresh.transpose(1, 0, 2).reshape(rows, 2 * KVH, HD).transpose(1, 0, 2)
    queries = gathered
    if not direct:
        queries = (
            jnp.take(gathered[:, :body], index ^ jnp.arange(chunks), axis=0)
            .reshape(KVH, split, pages, heads * per_page, HD)
            .transpose(0, 2, 1, 3, 4)
            .reshape(KVH, pages * page_rows, HD)
        )

    big = pages * page_rows
    block = (big + EXT, HD)
    attended = pl.pallas_call(
        functools.partial(attend_kernel, pages, page_rows),
        in_specs=[SMEM] + [VMEM] * 4,
        out_specs=[VMEM] * (KVH if direct else 1),
        out_shape=(
            [jax.ShapeDtypeStruct(block, jnp.float32)] * KVH
            if direct
            else [jax.ShapeDtypeStruct((KVH,) + block, jnp.float32)]
        ),
        scratch_shapes=[
            pltpu.VMEM((KVH * page_rows, KVH * HD), jnp.bfloat16),
            pltpu.VMEM((KVH * page_rows, LANES // page_rows * HD), jnp.float32),
        ],
        compiler_params=pltpu.CompilerParams(vmem_limit_bytes=6 * MIB),
        cost_estimate=pl.CostEstimate(
            flops=4 * pages * width * KVH * HD * KVH * page_rows,
            bytes_accessed=4 * pages * width * KVH * HD,
            transcendentals=pages * width * KVH * page_rows,
        ),
        name="attend",
    )(meta, queries, cache_keys, cache_values, reward_parts)
    if not direct:
        acc = (
            attended[0][:, :big]
            .reshape(KVH, pages, split, heads * per_page, HD)
            .transpose(0, 2, 1, 3, 4)
            .reshape(chunks, body, HD)
        )
        extra = attended[0][:, big : big + 2].reshape(KVH, 2, pages, split, heads * per_page)
        extra = extra.transpose(0, 3, 1, 2, 4).reshape(chunks, 2, body)
        extra = jnp.pad(extra, ((0, 0), (0, 2), (0, LANES - body)))
        attended = [jnp.concatenate([acc, extra, reward_parts], axis=1)]
    parts = trade(attended, chunks)

    chunk_rows = part // LANES * rows + EXT
    partial = pl.pallas_call(
        functools.partial(merge_kernel, pages, per_page, depth, span, slots, chunks),
        in_specs=[VMEM] * (3 + len(parts)),
        out_specs=[VMEM] * len(parts),
        out_shape=(
            [jax.ShapeDtypeStruct((chunk_rows, LANES), jnp.float32)] * chunks
            if direct
            else [jax.ShapeDtypeStruct((chunks, chunk_rows, LANES), jnp.float32)]
        ),
        scratch_shapes=[pltpu.VMEM((rows, qcols), jnp.bfloat16)],
        compiler_params=pltpu.CompilerParams(vmem_limit_bytes=8 * MIB),
        cost_estimate=pl.CostEstimate(
            flops=2 * rows * qcols * depth, bytes_accessed=2 * qcols * depth, transcendentals=0
        ),
        name="merge",
    )(packed, fresh, w_out, *parts)
    partial = trade(partial, chunks)

    decoded, reward = pl.pallas_call(
        functools.partial(sum_kernel, rows),
        out_shape=(
            jax.ShapeDtypeStruct((rows, part), jnp.bfloat16),
            jax.ShapeDtypeStruct((EXT, LANES), jnp.float32),
        ),
        compiler_params=pltpu.CompilerParams(vmem_limit_bytes=8 * MIB),
        name="total",
    )(*partial)
    far = lax.ppermute(decoded, "dp", swap)
    decoded = dot(give, jnp.concatenate([decoded, far], axis=0)).astype(jnp.bfloat16)
    return (reward[:slots, 0], decoded.reshape(STEPS, slots, part))


def solution(mesh):
    chunks = mesh.shape["tensor"]

    def body(*arrays):
        return local(chunks, *arrays)

    return jax.shard_map(
        body,
        mesh=mesh,
        in_specs=(
            P(("groups", "dp"), None, "tensor"),
            P("tensor"),
            P("tensor"),
            P(None, ("groups", "dp"), "tensor"),
            P(),
            P(None, "tensor"),
            P(None, "tensor"),
            P("tensor", None),
            P(("groups", "dp"), "tensor", None),
            P(("groups", "dp"), "tensor", None),
            P("groups"),
            P("groups"),
        ),
        out_specs=(P(("groups", "dp")), P(None, ("groups", "dp"), "tensor")),
        check_vma=False,
    )
```
